32 devices in a mesh: rep: 4 (over x, core), shard: 8 (over z, y).
Axes of the slice: x: 2, y: 2, z: 4, core: 2. Of those that a mesh axis runs over, the one named last changes fastest.
Arguments:
- tokens: bfloat16 [8192, 768], P(('rep', 'shard')), may hold values from -6 to 6
- cotangent: bfloat16 [8192, 768], P(('rep', 'shard')), may hold values from -6 to 6
- offsets: int32 [8192], replicated, may hold values from 0 to 255, as said below
- w_query: bfloat16 [768, 768], P('shard'), may hold values from -0.0546875 to 0.0546875
- w_key: bfloat16 [768, 768], P('shard'), may hold values from -0.21875 to 0.21875
- w_value: bfloat16 [768, 768], P('shard'), may hold values from -0.21875 to 0.21875
- w_attn_out: bfloat16 [768, 768], P('shard'), may hold values from -0.875 to 0.875
- w_gate: bfloat16 [768, 2048], P('shard'), may hold values from -0.21875 to 0.21875
- w_up: bfloat16 [768, 2048], P('shard'), may hold values from -0.21875 to 0.21875
- w_ff_out: bfloat16 [2048, 768], P('shard'), may hold values from -0.125 to 0.125
- gain_attn: bfloat16 [768], P('shard'), may hold values from 0.5 to 1.5
- gain_ff: bfloat16 [768], P('shard'), may hold values from 0.5 to 1.5
- rel_table: bfloat16 [32, 12], P('shard'), may hold values from -4 to 4
Outputs:
- output: bfloat16 [8192, 768], P(('rep', 'shard'))
- d_tokens: float32 [8192, 768], P(('rep', 'shard'))
- d_w_query: float32 [768, 768], P('shard')
- d_w_key: float32 [768, 768], P('shard')
- d_w_value: float32 [768, 768], P('shard')
- d_w_attn_out: float32 [768, 768], P('shard')
- d_w_gate: float32 [768, 2048], P('shard')
- d_w_up: float32 [768, 2048], P('shard')
- d_w_ff_out: float32 [2048, 768], P('shard')
- d_gain_attn: float32 [768], P('shard')
- d_gain_ff: float32 [768], P('shard')
- d_rel_table: float32 [32, 12], P('shard')
The draws below stay inside these ranges and needn't reach their ends.
Inputs may be any that keep to these rules, and one draw needn't show every extreme that they name: offsets[p] is 0 where a document starts and offsets[p - 1] + 1 otherwise; each sequence of 2048 tokens begins a document; a document lies in one sequence and has 1 to 256 tokens, and some document has exactly 256; every aligned block of 256 tokens holds two or more document starts.
All inputs are finite; a program needn't handle non-finite values.
Results may differ from the reference program's by a relative error of at most 0.014.
The reference program's roundings to bfloat16 on the way count: a program that leaves them out, or rounds other values in their place, can miss the bound.
Values may be sent and summed in bfloat16 or wider, within the bound.
No kernel may reach another device: no remote copies, remote signals or barrier semaphores. Data moves between devices by JAX's collectives and lax.ppermute only.
A program may use at most 128 MiB of HBM per device.

```python
import jax
import jax.numpy as jnp
from jax import lax

D = 768
H = 12
DK = 64
FF = 2048
NB = 32
TOK_DEV = 256
HD = 768
SEQ_LEN = 2048
TOKENS = 8192


def draw_offsets(key, part):
    stretches = TOKENS // TOK_DEV
    half = TOK_DEV // 2
    quarter = TOK_DEV // 4
    streams_keys = jax.random.split(jax.random.fold_in(key, 11), 5)
    stretch_index = jnp.arange(stretches, dtype=jnp.int32)
    leading = jax.random.randint(streams_keys[0], (stretches,), 0, half + 1)
    trailing = jax.random.randint(streams_keys[1], (stretches,), half + 1, TOK_DEV)
    late_trail = jax.random.randint(streams_keys[4], (stretches,), TOK_DEV - quarter + 1, TOK_DEV)
    in_sequence = stretch_index % (SEQ_LEN // TOK_DEV)
    lead_table = jnp.array([0, half, TOK_DEV - 2, 0, 1, quarter, TOK_DEV - quarter], jnp.int32)
    trail_table = jnp.array([half, TOK_DEV - 2, TOK_DEV - 1, 1, quarter, TOK_DEV - quarter, 0], jnp.int32)
    placed = jnp.minimum(in_sequence, 6)
    forced = in_sequence < 7
    leading = jnp.where(forced, lead_table[placed], leading)
    trailing = jnp.where(forced, trail_table[placed], trailing)
    trailing = jnp.where(in_sequence == 6, late_trail, trailing)
    position = jnp.arange(TOKENS, dtype=jnp.int32)
    marks = jnp.zeros((TOKENS,), jnp.int32)
    marks = marks.at[stretch_index * TOK_DEV + leading].set(1)
    marks = marks.at[stretch_index * TOK_DEV + trailing].set(1)
    level = jax.random.randint(streams_keys[2], (stretches,), 0, 4)
    rates = jnp.array([0, 1, 4, 16], jnp.int32)[level]
    rolls = jax.random.randint(streams_keys[3], (TOKENS,), 0, 64)
    within = position % SEQ_LEN
    allowed = jnp.logical_or(within < half, within >= 7 * TOK_DEV)
    extra = jnp.logical_and(rolls < jnp.repeat(rates, TOK_DEV), allowed)
    marks = jnp.maximum(marks, extra.astype(jnp.int32))
    begun = lax.cummax(jnp.where(marks > 0, position, 0), axis=0)
    return (position - begun).astype(jnp.int32)


def block_levels(own_key, dims, shards, low, high):
    factor_of, own = 1.0, jax.random.fold_in(own_key, 6)
    for axis_at, parts in shards:
        heights = jnp.exp(jax.random.uniform(jax.random.fold_in(own, axis_at), (parts,), jnp.float32, low / len(shards), high / len(shards)))
        factor_of = factor_of * jnp.repeat(heights, dims[axis_at] // parts).reshape([-1 if axis == axis_at else 1 for axis in range(len(dims))])
    return factor_of


def gaussian(key, extent, scale, limit, shards=(), held_as=jnp.bfloat16):
    values = scale * jax.random.normal(key, extent, jnp.float32)
    if shards:
        values = values * block_levels(key, extent, shards, -0.22, 0.18)
    return jnp.clip(values, -limit, limit).astype(held_as)


def setup_inputs(seed: int = 0) -> dict:
    seeds = jax.random.split(jax.random.key(seed), 14)
    tokens = gaussian(seeds[0], (TOKENS, D), 1.0, 6.0, ((0, 32),))
    cotangent = gaussian(seeds[1], (TOKENS, D), 1.0, 6.0, ((0, 32),))
    offsets = draw_offsets(jax.random.fold_in(seeds[13], 71), 0)
    w_query = gaussian(seeds[3], (D, HD), (16 * D) ** -0.5, 0.0546875, ((0, 8),))
    w_key = gaussian(seeds[4], (D, HD), D ** -0.5, 0.21875, ((0, 8),))
    w_value = gaussian(seeds[5], (D, HD), D ** -0.5, 0.21875, ((0, 8),))
    w_attn_out = gaussian(seeds[6], (HD, D), (HD // 16) ** -0.5, 0.875, ((0, 8),))
    w_gate = gaussian(seeds[7], (D, FF), D ** -0.5, 0.21875, ((0, 8),))
    w_up = gaussian(seeds[8], (D, FF), D ** -0.5, 0.21875, ((0, 8),))
    w_ff_out = gaussian(seeds[9], (FF, D), FF ** -0.5, 0.125, ((0, 8),))
    gain_attn = jnp.clip(1.0 + 0.1 * jax.random.normal(seeds[10], (D,), jnp.float32), 0.5, 1.5).astype(jnp.bfloat16)
    gain_ff = jnp.clip(1.0 + 0.1 * jax.random.normal(seeds[11], (D,), jnp.float32), 0.5, 1.5).astype(jnp.bfloat16)
    rel_table = gaussian(seeds[12], (NB, H), 1.0, 4.0, ((0, 8),))
    return dict(tokens=tokens, cotangent=cotangent, offsets=offsets, w_query=w_query, w_key=w_key, w_value=w_value, w_attn_out=w_attn_out, w_gate=w_gate, w_up=w_up, w_ff_out=w_ff_out, gain_attn=gain_attn, gain_ff=gain_ff, rel_table=rel_table)


NEG_FILL = -1e+30
EPSILON = 1e-06
BORDERS = (1, 2, 3, 4, 5, 6, 7, 8, 12, 16, 23, 32, 46, 64, 91)

@jax.custom_vjp
def low(v):
    return lax.optimization_barrier(v.astype(jnp.bfloat16)).astype(jnp.float32)

@jax.custom_vjp
def low_back(v):
    return v

def low_keep(v):
    return (low(v), None)

def low_pass(kept, grad):
    return (grad,)

def back_keep(v):
    return (v, None)

def back_low(kept, grad):
    return (low(grad),)
low.defvjp(low_keep, low_pass)
low_back.defvjp(back_keep, back_low)

def bucket_of(relative):
    distance = jnp.abs(relative)
    bucket = NB // 2 * (relative > 0).astype(jnp.int32)
    for border in BORDERS:
        bucket = bucket + (distance >= border).astype(jnp.int32)
    return bucket

def rms_norm(values, gain):
    return values * lax.rsqrt(lax.optimization_barrier(jnp.mean(values * values, axis=-1, keepdims=True)) + EPSILON) * gain

def forward(layer_in, w_query, w_key, w_value, w_attn_out, w_gate, w_up, w_ff_out, gain_attn, gain_ff, rel_table, offsets):
    highest = lax.Precision.HIGHEST
    normed = low(rms_norm(layer_in, gain_attn))
    queries = low_back(low(jnp.dot(normed, w_query, precision=highest)))
    key_rows = low_back(low(jnp.dot(normed, w_key, precision=highest)))
    value_rows = low_back(low(jnp.dot(normed, w_value, precision=highest)))
    position = jnp.arange(TOKENS, dtype=jnp.int32)
    starts = position - offsets
    key_pad = jnp.pad(key_rows, ((TOK_DEV, TOK_DEV), (0, 0)))
    value_pad = jnp.pad(value_rows, ((TOK_DEV, TOK_DEV), (0, 0)))
    start_pad = jnp.pad(starts, (TOK_DEV, TOK_DEV), constant_values=-1)
    offset_pad = jnp.pad(offsets, (TOK_DEV, TOK_DEV))

    def attend(index):
        first = (index * TOK_DEV).astype(jnp.int32)
        query_blk = lax.dynamic_slice_in_dim(queries, first, TOK_DEV).reshape(TOK_DEV, H, DK)
        key_win = lax.dynamic_slice_in_dim(key_pad, first, 3 * TOK_DEV).reshape(3 * TOK_DEV, H, DK)
        value_win = lax.dynamic_slice_in_dim(value_pad, first, 3 * TOK_DEV).reshape(3 * TOK_DEV, H, DK)
        start_own = lax.dynamic_slice_in_dim(starts, first, TOK_DEV)
        start_win = lax.dynamic_slice_in_dim(start_pad, first, 3 * TOK_DEV)
        offset_own = lax.dynamic_slice_in_dim(offsets, first, TOK_DEV)
        offset_win = lax.dynamic_slice_in_dim(offset_pad, first, 3 * TOK_DEV)
        bias = rel_table[bucket_of(offset_win[None, :] - offset_own[:, None])]
        scores = jnp.einsum('qhd,khd->hqk', query_blk, key_win, precision=highest) + jnp.transpose(bias, (2, 0, 1))
        scores = low_back(scores)
        same_doc = (start_own[:, None] == start_win[None, :])[None]
        scores = jnp.where(same_doc, scores, NEG_FILL)
        probs = low(jax.nn.softmax(scores, axis=-1))
        return jnp.einsum('hqk,khd->qhd', probs, value_win, precision=highest).reshape(TOK_DEV, HD)
    blocks = jnp.arange(TOKENS // TOK_DEV, dtype=jnp.int32)
    mixed = lax.map(jax.checkpoint(attend), blocks).reshape(TOKENS, HD)
    heads = low_back(low(mixed))
    attn = low_back(jnp.dot(heads, w_attn_out, precision=highest))
    resid = layer_in + attn
    normed_ff = low(rms_norm(resid, gain_ff))
    gate = low_back(jnp.dot(normed_ff, w_gate, precision=highest))
    linear = low_back(jnp.dot(normed_ff, w_up, precision=highest))
    hidden = low(jax.nn.gelu(gate, approximate=True) * linear)
    return resid + jnp.dot(hidden, w_ff_out, precision=highest)

def reference(tokens, cotangent, offsets, w_query, w_key, w_value, w_attn_out, w_gate, w_up, w_ff_out, gain_attn, gain_ff, rel_table):

    def layer(layer_in, wq_in, wk_in, wv_in, wo_in, wg_in, wu_in, wf_in, ga_in, gf_in, table_in):
        return forward(layer_in, wq_in, wk_in, wv_in, wo_in, wg_in, wu_in, wf_in, ga_in, gf_in, table_in, offsets)
    result, pull = jax.vjp(layer, tokens.astype(jnp.float32), w_query.astype(jnp.float32), w_key.astype(jnp.float32), w_value.astype(jnp.float32), w_attn_out.astype(jnp.float32), w_gate.astype(jnp.float32), w_up.astype(jnp.float32), w_ff_out.astype(jnp.float32), gain_attn.astype(jnp.float32), gain_ff.astype(jnp.float32), rel_table.astype(jnp.float32))
    grads = pull(cotangent.astype(jnp.float32))
    return (result.astype(jnp.bfloat16), grads[0], grads[1], grads[2], grads[3], grads[4], grads[5], grads[6], grads[7], grads[8], grads[9], grads[10])
```

```python
import functools

import jax
import jax.numpy as jnp
import numpy as np
from jax import lax
from jax.experimental import pallas as pl
from jax.experimental.pallas import tpu as pltpu
from jax.sharding import PartitionSpec as P

NEG_FILL = -1e30
EPSILON = 1e-06
BORDERS = (1, 2, 3, 4, 5, 6, 7, 8, 12, 16, 23, 32, 46, 64, 91)
LANES = 128
PARTS = 4
GROUPS = (8, 4)
LOW = jnp.bfloat16
FULL = jnp.float32
GELU_A = float(np.sqrt(2.0 / np.pi))
GELU_B = 0.044715


def bits_of(count):
    return count.bit_length() - 1


def swap(block, axis, bit):
    count = lax.axis_size(axis)
    return lax.ppermute(block, axis, [(i, i ^ (1 << bit)) for i in range(count)])


def add_low(left, right):
    return (left.astype(FULL) + right.astype(FULL)).astype(LOW)


def gather_shards(block):
    for bit in reversed(range(bits_of(lax.axis_size("shard")))):
        block = jnp.concatenate([block, swap(block, "shard", bit)], axis=0)
    return block


def scatter_shards(blocks):
    for bit in range(bits_of(lax.axis_size("shard"))):
        half = blocks.shape[0] // 2
        blocks = add_low(blocks[:half], swap(blocks[half:], "shard", bit))
    return blocks[0]


def sum_replicas(block, first_bit):
    for bit in range(first_bit, bits_of(lax.axis_size("rep"))):
        block = add_low(block, swap(block, "rep", bit))
    return block


def bucket_onehot(period, buckets):
    index = np.arange(period)
    relative = np.where(index < period // 2, index, index - period)
    distance = np.abs(relative)
    bucket = buckets // 2 * (relative > 0).astype(np.int64)
    for border in BORDERS:
        bucket = bucket + (distance >= border).astype(np.int64)
    return (bucket[:, None] == np.arange(buckets)[None, :]).astype(np.float32)


def mm(left, right):
    return lax.dot_general(left, right, (((1,), (0,)), ((), ())), preferred_element_type=FULL)


def mm_nt(left, right):
    return lax.dot_general(left, right, (((1,), (1,)), ((), ())), preferred_element_type=FULL)


def mm_tn(left, right):
    return lax.dot_general(left, right, (((0,), (0,)), ((), ())), preferred_element_type=FULL)


def inverse_rms(values):
    return lax.rsqrt(jnp.mean(values * values, axis=-1, keepdims=True) + EPSILON)


def norm_back(values, scale, gain, grad):
    inner = jnp.mean(gain * grad * values, axis=-1, keepdims=True)
    return scale * gain * grad - values * (scale * scale * scale * inner)


def pick(mask, left, right):
    return jnp.where(mask, left.astype(FULL), right.astype(FULL)).astype(left.dtype)


def aligned(index, size):
    return pl.ds(pl.multiple_of(index, 8), size)


def lanes_at(index, size):
    return pl.ds(pl.multiple_of(index, LANES), size)


def bias_tiles(bias_row, rows):
    rolled = pltpu.roll(
        jnp.broadcast_to(bias_row, (rows, 2 * rows)), 0, 1, stride=1, stride_axis=0
    )
    return rolled[:, :rows], rolled[:, rows:]


def place_halves(pos, core, mine, other, full, shard_rows, shards):
    width = mine.shape[1]

    def place(j, carry):
        source = aligned(pos[j] * shard_rows, shard_rows)
        target = aligned(j * shard_rows, shard_rows)
        full[target, lanes_at(core * width, width)] = mine[source, :]
        full[target, lanes_at((1 - core) * width, width)] = other[source, :]
        return carry

    lax.fori_loop(0, shards, place, 0)


def attend_kernel(
    shards,
    heads_count,
    pos,
    meta,
    before,
    own,
    after,
    gain,
    mine,
    other,
    own_col,
    own_row,
    before_row,
    after_row,
    bias,
    heads,
    normed,
    qkv,
    weights,
    kv_before,
):
    rows, width = own.shape
    place_halves(pos, meta[0], mine, other, weights, width // shards, shards)

    def normed_of(ref):
        values = ref[...].astype(FULL)
        return (values * inverse_rms(values) * gain[...]).astype(LOW)

    normed[:rows, :] = normed_of(own)
    normed[rows:, :] = normed_of(after)
    normed_before = normed_of(before)
    hidden = weights.shape[1] // 3
    for part in range(3):
        columns = slice(part * hidden, (part + 1) * hidden)
        qkv[:, columns] = mm(normed[...], weights[:, columns]).astype(LOW)
        if part:
            kv_before[:, (part - 1) * hidden : part * hidden] = mm(
                normed_before, weights[:, columns]
            ).astype(LOW)
    in_own = own_col[...] == own_row[...]
    in_before = own_col[...] == before_row[...]
    in_after = own_col[...] == after_row[...]
    allowed = in_own | in_before | in_after
    size = hidden // heads_count
    for pair in range(heads_count // 2):
        mixed = []
        for head in (2 * pair, 2 * pair + 1):
            at = head * size
            query = qkv[:rows, at : at + size]
            keys = slice(hidden + at, hidden + at + size)
            values = slice(2 * hidden + at, 2 * hidden + at + size)
            near, far = bias_tiles(bias[head : head + 1, :], rows)
            scores = jnp.where(
                in_own,
                mm_nt(query, qkv[:rows, keys]) + near,
                jnp.where(
                    in_before,
                    mm_nt(query, kv_before[:, at : at + size]),
                    mm_nt(query, qkv[rows:, keys]),
                )
                + far,
            )
            scores = jnp.where(allowed, scores, NEG_FILL)
            expd = jnp.exp(scores - jnp.max(scores, axis=-1, keepdims=True))
            probs = expd * (1.0 / jnp.sum(expd, axis=-1, keepdims=True))
            total = mm(jnp.where(in_own, probs, 0.0).astype(LOW), qkv[:rows, values])
            total = total + mm(
                jnp.where(in_before, probs, 0.0).astype(LOW),
                kv_before[:, hidden + at : hidden + at + size],
            )
            total = total + mm(
                jnp.where(in_after, probs, 0.0).astype(LOW), qkv[rows:, values]
            )
            mixed.append(total)
        heads[:, 2 * pair * size : (2 * pair + 2) * size] = jnp.concatenate(mixed, axis=1).astype(LOW)


def feed_kernel(
    shards,
    pos,
    meta,
    heads,
    own,
    cotangent,
    gain,
    out_mine,
    out_other,
    part_0,
    part_1,
    part_2,
    part_3,
    output,
    d_resid,
    d_heads,
    normed_ff,
    hidden,
    d_gate,
    d_linear,
    d_gain,
    w_out,
    w_gate,
    w_up,
    w_down,
):
    rows, width = own.shape
    inner = w_gate.shape[1]
    shard_rows, down_rows = width // shards, inner // shards // PARTS
    slab = inner // PARTS
    tiles, down_tiles = slab // LANES, width // LANES
    block = part_0.shape[0] // shards
    place_halves(pos, meta[0], out_mine, out_other, w_out, shard_rows, shards)

    def place(j, carry):
        for relative, part in enumerate((part_0, part_1, part_2, part_3)):
            quarter = meta[1] ^ relative
            start = pos[j] * block
            target = aligned(j * shard_rows, shard_rows)
            for t in range(tiles):
                lane = lanes_at(quarter * slab + t * LANES, LANES)
                w_gate[target, lane] = part[aligned(start + t * shard_rows, shard_rows), :]
                w_up[target, lane] = part[aligned(start + (tiles + t) * shard_rows, shard_rows), :]
            down = start + 2 * tiles * shard_rows
            target = aligned(j * (PARTS * down_rows) + quarter * down_rows, down_rows)
            for t in range(down_tiles):
                w_down[target, t * LANES : (t + 1) * LANES] = part[
                    aligned(down + t * down_rows, down_rows), :
                ]
        return carry

    lax.fori_loop(0, shards, place, 0)
    resid = own[...].astype(FULL) + mm(heads[...], w_out[...])
    scale = inverse_rms(resid)
    normed_ff[...] = (resid * scale * gain[...]).astype(LOW)
    d_resid[...] = resid
    total = resid
    d_normed = jnp.zeros((rows, width), FULL)
    for q in range(PARTS):
        columns = slice(q * slab, (q + 1) * slab)
        gate = mm(normed_ff[...], w_gate[:, columns])
        linear = mm(normed_ff[...], w_up[:, columns])
        d_hidden = mm_nt(cotangent[...], w_down[columns, :])
        square = gate * gate
        tanh = jnp.tanh(GELU_A * (gate + GELU_B * square * gate))
        half = 0.5 * (1.0 + tanh)
        gelu = gate * half
        slope = half + 0.5 * gate * (1.0 - tanh * tanh) * (GELU_A * (1.0 + 3.0 * GELU_B * square))
        hidden[:, columns] = (gelu * linear).astype(LOW)
        d_gate[:, columns] = (d_hidden * linear * slope).astype(LOW)
        d_linear[:, columns] = (d_hidden * gelu).astype(LOW)
        total = total + mm(hidden[:, columns], w_down[columns, :])
        d_normed = d_normed + mm_nt(d_gate[:, columns], w_gate[:, columns])
        d_normed = d_normed + mm_nt(d_linear[:, columns], w_up[:, columns])
    output[...] = total.astype(LOW)
    resid = d_resid[...]
    d_gain[...] = jnp.sum(d_normed * resid * scale, axis=0, keepdims=True)
    grad = cotangent[...].astype(FULL) + norm_back(resid, scale, gain[...], d_normed)
    d_resid[...] = grad
    d_heads[...] = mm_nt(grad.astype(LOW), w_out[...]).astype(LOW)


def feed_grads_kernel(
    shards,
    pos,
    meta,
    heads,
    d_resid,
    normed_ff,
    hidden,
    d_gate,
    d_linear,
    cotangent,
    d_ff,
    d_out,
):
    width, inner = heads.shape[1], hidden.shape[1]
    shard_rows, down_rows = width // shards, inner // shards // PARTS
    slab = inner // PARTS
    tiles, down_tiles = slab // LANES, width // LANES
    for q in range(PARTS):
        columns = slice(q * slab, (q + 1) * slab)
        at = meta[2 + q]
        for side, grad in enumerate((d_gate, d_linear)):
            value = mm_tn(normed_ff[...], grad[:, columns]).astype(LOW)
            for j in range(shards):
                for t in range(tiles):
                    first = (side * tiles + t) * shard_rows
                    d_ff[at, pos[j], first : first + shard_rows, :] = value[
                        j * shard_rows : (j + 1) * shard_rows, t * LANES : (t + 1) * LANES
                    ]
        value = mm_tn(hidden[:, columns], cotangent[...]).astype(LOW)
        for piece in range(slab // down_rows):
            j, quarter = divmod(q * (slab // down_rows) + piece, PARTS)
            for t in range(down_tiles):
                first = 2 * tiles * shard_rows + t * down_rows
                d_ff[meta[2 + quarter], pos[j], first : first + down_rows, :] = value[
                    piece * down_rows : (piece + 1) * down_rows, t * LANES : (t + 1) * LANES
                ]
    half = width // 2
    grad = d_resid[...].astype(LOW)
    for side in range(2):
        value = mm_tn(heads[...], grad[:, side * half : (side + 1) * half]).astype(LOW)
        at = meta[0] ^ side
        for j in range(shards):
            d_out[at, pos[j], :, :] = value[j * shard_rows : (j + 1) * shard_rows, :]


def attend_grads_kernel(
    shards,
    first,
    last,
    size,
    pos,
    meta,
    qkv,
    normed,
    dh_own,
    dh_after,
    own_col,
    own_row,
    after_col,
    after_row,
    bias,
    d_cols,
    d_weights,
    d_bias,
    qkv_mix,
    dh_keep,
    dh_mix,
):
    rows, width = dh_own.shape
    hidden = width
    group = (last - first) * size
    tail = meta[6]
    is_last_col, is_last_row = own_col[...] == tail, own_row[...] == tail
    mix_col = jnp.where(is_last_col, own_col[...], after_col[...])
    mix_row = jnp.where(is_last_row, own_row[...], after_row[...])
    inside = (own_col[...] == own_row[...]) & jnp.logical_not(is_last_col)
    crossing = (mix_col == tail) & (mix_row == tail)
    turned = is_last_col != is_last_row
    began = (own_col[...] >= meta[7]) & jnp.logical_not(is_last_col)
    span = slice(first * size, last * size)
    for part in range(3):
        columns = slice(part * hidden + first * size, part * hidden + last * size)
        qkv_mix[:, part * group : (part + 1) * group] = pick(
            is_last_col, qkv[:rows, columns], qkv[rows:, columns]
        )
    keep = jnp.where(began, dh_own[:, span].astype(FULL), 0.0)
    dh_keep[...] = keep.astype(LOW)
    mixed = jnp.where(is_last_col, dh_own[:, span].astype(FULL), dh_after[:, span].astype(FULL))
    dh_mix[...] = jnp.where(mix_col == tail, mixed, 0.0).astype(LOW)

    def tile(query, key, value, grad, offset, mask):
        scores = jnp.where(mask, mm_nt(query, key) + offset, NEG_FILL)
        expd = jnp.exp(scores - jnp.max(scores, axis=-1, keepdims=True))
        probs = expd * (1.0 / jnp.sum(expd, axis=-1, keepdims=True))
        d_probs = mm_nt(grad, value)
        weighted = jnp.sum(d_probs * probs, axis=-1, keepdims=True)
        d_scores = (probs * (d_probs - weighted)).astype(LOW)
        return (
            mm(d_scores, key),
            mm_tn(d_scores, query),
            mm_tn(probs.astype(LOW), grad),
            d_scores.astype(FULL),
        )

    for pair in range((last - first) // 2):
        outs = []
        for index in (2 * pair, 2 * pair + 1):
            head = first + index
            near, far = bias_tiles(bias[head : head + 1, :], rows)
            at, here = head * size, index * size
            one = tile(
                qkv[:rows, at : at + size],
                qkv[:rows, hidden + at : hidden + at + size],
                qkv[:rows, 2 * hidden + at : 2 * hidden + at + size],
                dh_keep[:, here : here + size],
                near,
                inside,
            )
            two = tile(
                qkv_mix[:, here : here + size],
                qkv_mix[:, group + here : group + here + size],
                qkv_mix[:, 2 * group + here : 2 * group + here + size],
                dh_mix[:, here : here + size],
                jnp.where(turned, far, near),
                crossing,
            )
            flat = jnp.concatenate(
                [one[3] + jnp.where(turned, 0.0, two[3]), jnp.where(turned, two[3], 0.0)], axis=1
            )
            folded = flat[:8, :]
            for base in range(8, rows, 8):
                folded = folded + pltpu.roll(flat[base : base + 8, :], 2 * rows - base, 1)
            d_bias[8 * index : 8 * index + 8, :] = folded
            outs.append((one, two))
        for part in range(3):
            columns = slice(part * group + 2 * pair * size, part * group + (2 * pair + 2) * size)
            for side in range(2):
                d_cols[side * rows : (side + 1) * rows, columns] = jnp.concatenate(
                    [outs[0][side][part], outs[1][side][part]], axis=1
                ).astype(LOW)
    normed_mix = pick(is_last_col, normed[:rows, :], normed[rows:, :])
    half = 3 * group // 2
    shard_rows = width // shards
    for side in range(2):
        columns = slice(side * half, (side + 1) * half)
        value = mm_tn(normed[:rows, :], d_cols[:rows, columns])
        value = (value + mm_tn(normed_mix, d_cols[rows:, columns])).astype(LOW)
        at = meta[0] ^ side
        for j in range(shards):
            d_weights[at, pos[j], :, :] = value[j * shard_rows : (j + 1) * shard_rows, :]


def token_grads_kernel(
    sizes, meta, weights, own, after, gain, own_col, *refs
):
    *columns, d_own, d_after, d_gain = refs
    rows, width = own.shape
    is_last = own_col[...] == meta[6]
    total = jnp.zeros((2 * rows, width), FULL)
    begin = 0
    for ref, group in zip(columns, sizes, strict=True):
        for part in range(3):
            total = total + mm_nt(
                ref[:, part * group : (part + 1) * group],
                weights[:, part * width + begin : part * width + begin + group],
            )
        begin += group
    mine = jnp.where(is_last, total[rows:], total[:rows])
    sent = jnp.where(is_last, 0.0, total[rows:])
    d_own[...] = mine
    d_after[...] = sent.astype(LOW)
    values, ahead = own[...].astype(FULL), after[...].astype(FULL)
    share = mine * values * inverse_rms(values) + sent * ahead * inverse_rms(ahead)
    d_gain[...] = jnp.sum(share, axis=0, keepdims=True)


def tokens_kernel(own, gain, d_resid, d_own, d_before, d_tokens):
    values = own[...].astype(FULL)
    grad = d_own[...] + d_before[...].astype(FULL)
    d_tokens[...] = d_resid[...] + norm_back(values, inverse_rms(values), gain[...], grad)


def unpack_ff_kernel(meta, part_0, part_1, part_2, part_3, d_gate, d_up, d_down):
    shard_rows = d_gate.shape[0]
    slab = d_gate.shape[1] // PARTS
    down_rows, down_tiles = d_down.shape[0] // PARTS, d_down.shape[1] // LANES
    tiles = slab // LANES
    for relative, part in enumerate((part_0, part_1, part_2, part_3)):
        quarter = meta[1] ^ relative
        for t in range(tiles):
            lane = lanes_at(quarter * slab + t * LANES, LANES)
            d_gate[:, lane] = part[t * shard_rows : (t + 1) * shard_rows, :].astype(FULL)
            first = (tiles + t) * shard_rows
            d_up[:, lane] = part[first : first + shard_rows, :].astype(FULL)
        for t in range(down_tiles):
            first = 2 * tiles * shard_rows + t * down_rows
            d_down[aligned(quarter * down_rows, down_rows), t * LANES : (t + 1) * LANES] = part[
                first : first + down_rows, :
            ].astype(FULL)


def unpack_attend_kernel(sizes, meta, *refs):
    halves, (d_query, d_key, d_value) = refs[:-3], refs[-3:]
    begin = 0
    for g, group in enumerate(sizes):
        mine, other = halves[2 * g], halves[2 * g + 1]
        for core in range(2):

            @pl.when(meta[0] == core)
            def _():
                pair = (mine, other) if core == 0 else (other, mine)
                whole = jnp.concatenate([pair[0][...], pair[1][...]], axis=1).astype(FULL)
                for part, ref in enumerate((d_query, d_key, d_value)):
                    ref[:, begin : begin + group] = whole[:, part * group : (part + 1) * group]

        begin += group


def unpack_out_kernel(meta, mine, other, d_out):
    width = mine.shape[1]
    d_out[:, lanes_at(meta[0] * width, width)] = mine[...].astype(FULL)
    d_out[:, lanes_at((1 - meta[0]) * width, width)] = other[...].astype(FULL)


def call(kernel, scalars, arrays, outs, scratch=(), flops=0):
    def in_vmem(_):
        return pl.BlockSpec(memory_space=pltpu.VMEM)

    def in_smem(_):
        return pl.BlockSpec(memory_space=pltpu.SMEM)

    moved = sum(a.size * a.dtype.itemsize for a in (*arrays, *outs))
    return pl.pallas_call(
        kernel,
        out_shape=outs,
        in_specs=[in_smem(a) for a in scalars] + [in_vmem(a) for a in arrays],
        out_specs=tuple(in_vmem(a) for a in outs),
        scratch_shapes=scratch,
        compiler_params=pltpu.CompilerParams(vmem_limit_bytes=58 * 2**20),
        cost_estimate=pl.CostEstimate(flops=flops, bytes_accessed=moved, transcendentals=0),
    )(*scalars, *arrays)


def shaped(shape, dtype):
    return jax.ShapeDtypeStruct(shape, dtype)


def per_device(
    tokens,
    cotangent,
    offsets,
    w_query,
    w_key,
    w_value,
    w_attn_out,
    w_gate,
    w_up,
    w_ff_out,
    gain_attn,
    gain_ff,
    rel_table,
):
    rows, width = tokens.shape
    shards, reps = lax.axis_size("shard"), lax.axis_size("rep")
    shard, rep = lax.axis_index("shard"), lax.axis_index("rep")
    block_index = rep * shards + shard
    core, quarter = rep % 2, rep % PARTS
    heads_count, table_rows = rel_table.shape[1], rel_table.shape[0]
    buckets = table_rows * shards
    shard_rows, inner = w_gate.shape
    down_rows = w_ff_out.shape[0] // PARTS
    slab = inner // PARTS
    size = width // heads_count

    relative = jnp.arange(shards, dtype=jnp.int32) ^ shard
    pos = jnp.zeros_like(relative)
    for bit in range(bits_of(shards)):
        pos = pos | (((relative >> bit) & 1) << (bits_of(shards) - 1 - bit))
    quarters = jnp.arange(PARTS, dtype=jnp.int32) ^ quarter
    quarter_pos = ((quarters & 1) << 1) | (quarters >> 1)

    starts_all = jnp.arange(offsets.shape[0], dtype=jnp.int32) - offsets
    start_pad = jnp.pad(starts_all, (rows, rows), constant_values=-1)
    window = lax.dynamic_slice_in_dim(start_pad, block_index * rows, 3 * rows)
    before_row = window[:rows].reshape(1, rows)
    own_row = window[rows : 2 * rows].reshape(1, rows)
    after_row = window[2 * rows :].reshape(1, rows)
    own_col, after_col = own_row.reshape(rows, 1), after_row.reshape(rows, 1)
    meta = jnp.concatenate(
        [
            jnp.stack([core, quarter]),
            quarter_pos,
            jnp.stack([window[2 * rows - 1], block_index * rows]),
        ]
    ).astype(jnp.int32)

    qkv_own = jnp.concatenate([w_query, w_key, w_value], axis=1)
    qkv_half = lax.dynamic_slice_in_dim(qkv_own, core * (3 * width // 2), 3 * width // 2, axis=1)
    small = jnp.stack(
        [
            jnp.pad(gain_attn, (0, LANES - shard_rows)),
            jnp.pad(gain_ff, (0, LANES - shard_rows)),
            jnp.pad(rel_table.reshape(-1), (0, LANES - table_rows * heads_count)),
        ]
    )
    small = jnp.pad(small, ((0, 5), (0, 0)))
    up = [(i, i + 1) for i in range(shards - 1)]
    down = [(i + 1, i) for i in range(shards - 1)]
    small_all = gather_shards(small)
    qkv_mine = gather_shards(qkv_half)
    qkv_other = swap(qkv_mine, "rep", 0)
    before = lax.ppermute(tokens, "shard", up)
    after = lax.ppermute(tokens, "shard", down)
    out_half = lax.dynamic_slice_in_dim(w_attn_out, core * (width // 2), width // 2, axis=1)
    out_mine = gather_shards(out_half)
    out_other = swap(out_mine, "rep", 0)

    def tiles_of(matrix):
        count = matrix.shape[1] // LANES
        return [matrix[:, t * LANES : (t + 1) * LANES] for t in range(count)]

    ff_own = jnp.concatenate(
        tiles_of(lax.dynamic_slice_in_dim(w_gate, quarter * slab, slab, axis=1))
        + tiles_of(lax.dynamic_slice_in_dim(w_up, quarter * slab, slab, axis=1))
        + tiles_of(lax.dynamic_slice_in_dim(w_ff_out, quarter * down_rows, down_rows, axis=0)),
        axis=0,
    )
    ff_0 = gather_shards(ff_own)
    ff_2 = swap(ff_0, "rep", 1)
    ff_1 = swap(ff_0, "rep", 0)
    ff_3 = swap(ff_2, "rep", 0)

    order = (pos[:, None] == jnp.arange(shards, dtype=jnp.int32)[None, :]).astype(LOW)
    small_all = jnp.dot(
        order, small_all.reshape(shards, 8 * LANES), preferred_element_type=FULL
    ).reshape(shards, 8, LANES)
    gain_one = small_all[:, 0, :shard_rows].reshape(1, width)
    gain_two = small_all[:, 1, :shard_rows].reshape(1, width)
    table = small_all[:, 2, : table_rows * heads_count].reshape(buckets, heads_count)
    selector = jnp.asarray(bucket_onehot(2 * rows, buckets))
    bias = lax.dot_general(
        table.astype(LOW),
        selector.astype(LOW),
        (((0,), (1,)), ((), ())),
        preferred_element_type=FULL,
    )

    heads, normed, qkv, w_qkv = call(
        functools.partial(attend_kernel, shards, heads_count),
        (pos, meta),
        (
            before,
            tokens,
            after,
            gain_one,
            qkv_mine,
            qkv_other,
            own_col,
            own_row,
            before_row,
            after_row,
            bias,
        ),
        (
            shaped((rows, width), LOW),
            shaped((2 * rows, width), LOW),
            shaped((2 * rows, 3 * width), LOW),
            shaped((width, 3 * width), LOW),
        ),
        [pltpu.VMEM((rows, 2 * width), LOW)],
        flops=10 * rows * width * width * 2,
    )
    wide = shaped((rows, inner), LOW)
    output, d_resid, d_heads, normed_ff, hidden, d_gate, d_linear, d_gain_two = call(
        functools.partial(feed_kernel, shards),
        (pos, meta),
        (heads, tokens, cotangent, gain_two, out_mine, out_other, ff_0, ff_1, ff_2, ff_3),
        (
            shaped((rows, width), LOW),
            shaped((rows, width), FULL),
            shaped((rows, width), LOW),
            shaped((rows, width), LOW),
            wide,
            wide,
            wide,
            shaped((1, width), FULL),
        ),
        [
            pltpu.VMEM((width, width), LOW),
            pltpu.VMEM((width, inner), LOW),
            pltpu.VMEM((width, inner), LOW),
            pltpu.VMEM((inner, width), LOW),
        ],
        flops=14 * rows * width * inner,
    )
    d_heads_after = lax.ppermute(d_heads, "shard", down)
    block = ff_own.shape[0]
    d_ff, d_out = call(
        functools.partial(feed_grads_kernel, shards),
        (pos, meta),
        (heads, d_resid, normed_ff, hidden, d_gate, d_linear, cotangent),
        (
            shaped((PARTS, shards, block, LANES), LOW),
            shaped((2, shards, shard_rows, width // 2), LOW),
        ),
        flops=7 * rows * width * inner,
    )

    d_ff = add_low(d_ff[:2], swap(d_ff[2:], "rep", 0))
    d_ff = add_low(d_ff[0], swap(d_ff[1], "rep", 1))
    d_ff = sum_replicas(scatter_shards(d_ff), 2)
    d_ff_2 = swap(d_ff, "rep", 1)
    d_ff_1 = swap(d_ff, "rep", 0)
    d_ff_3 = swap(d_ff_2, "rep", 0)
    d_out = sum_replicas(scatter_shards(add_low(d_out[0], swap(d_out[1], "rep", 0))), 1)
    d_out_other = swap(d_out, "rep", 0)

    halves, column_grads, d_biases, sizes = [], [], [], []
    first = 0
    for count in GROUPS:
        group = count * size
        sizes.append(group)
        d_cols, d_weights, d_bias = call(
            functools.partial(attend_grads_kernel, shards, first, first + count, size),
            (pos, meta),
            (
                qkv,
                normed,
                d_heads,
                d_heads_after,
                own_col,
                own_row,
                after_col,
                after_row,
                bias,
            ),
            (
                shaped((2 * rows, 3 * group), LOW),
                shaped((2, shards, shard_rows, 3 * group // 2), LOW),
                shaped((8 * count, 2 * rows), FULL),
            ),
            [
                pltpu.VMEM((rows, 3 * group), LOW),
                pltpu.VMEM((rows, group), LOW),
                pltpu.VMEM((rows, group), LOW),
            ],
            flops=24 * rows * width * group,
        )
        first += count
        column_grads.append(d_cols)
        d_biases.append(d_bias)
        mine = add_low(d_weights[0], swap(d_weights[1], "rep", 0))
        mine = sum_replicas(scatter_shards(mine), 1)
        halves += [mine, swap(mine, "rep", 0)]

    d_own, d_after, d_gain_one = call(
        functools.partial(token_grads_kernel, tuple(sizes)),
        (meta,),
        (w_qkv, tokens, after, gain_one, own_col, *column_grads),
        (
            shaped((rows, width), FULL),
            shaped((rows, width), LOW),
            shaped((1, width), FULL),
        ),
        flops=12 * rows * width * width,
    )
    d_before = lax.ppermute(d_after, "shard", up)
    (d_tokens,) = call(
        tokens_kernel,
        (),
        (tokens, gain_one, d_resid, d_own, d_before),
        (shaped((rows, width), FULL),),
    )

    folds = np.stack([np.roll(bucket_onehot(2 * rows, buckets), row, axis=0) for row in range(8)])
    d_table = lax.dot_general(
        jnp.concatenate(d_biases, axis=0).reshape(heads_count, 16 * rows),
        jnp.asarray(folds.reshape(16 * rows, buckets)),
        (((1,), (0,)), ((), ())),
        precision=lax.Precision.HIGHEST,
    ).T
    smalls = jnp.concatenate([d_gain_one.reshape(-1), d_gain_two.reshape(-1), d_table.reshape(-1)])
    extra = -smalls.shape[0] % (8 * LANES)
    smalls = jnp.pad(smalls, (0, extra)).reshape(-1, LANES)
    for axis in ("rep", "shard"):
        for bit in range(bits_of(lax.axis_size(axis))):
            smalls = smalls + swap(smalls, axis, bit)
    smalls = smalls.reshape(-1)

    def own_part(begin, length):
        return lax.dynamic_slice_in_dim(smalls, begin + shard * length, length)

    d_w_gate, d_w_up, d_w_ff_out = call(
        unpack_ff_kernel,
        (meta,),
        (d_ff, d_ff_1, d_ff_2, d_ff_3),
        (
            shaped(w_gate.shape, FULL),
            shaped(w_up.shape, FULL),
            shaped(w_ff_out.shape, FULL),
        ),
    )
    (d_w_attn_out,) = call(
        unpack_out_kernel, (meta,), (d_out, d_out_other), (shaped(w_attn_out.shape, FULL),)
    )
    d_w_query, d_w_key, d_w_value = call(
        functools.partial(unpack_attend_kernel, tuple(sizes)),
        (meta,),
        tuple(halves),
        (shaped(w_query.shape, FULL),) * 3,
    )
    return (
        output,
        d_tokens,
        d_w_query,
        d_w_key,
        d_w_value,
        d_w_attn_out,
        d_w_gate,
        d_w_up,
        d_w_ff_out,
        own_part(0, shard_rows),
        own_part(width, shard_rows),
        own_part(2 * width, table_rows * heads_count).reshape(table_rows, heads_count),
    )


def solution(mesh):
    tokens_spec, rows_spec, line_spec = P(("rep", "shard"), None), P("shard", None), P("shard")
    return jax.shard_map(
        per_device,
        mesh=mesh,
        in_specs=(tokens_spec, tokens_spec, P()) + (rows_spec,) * 7 + (line_spec,) * 2 + (rows_spec,),
        out_specs=(tokens_spec,) * 2 + (rows_spec,) * 7 + (line_spec,) * 2 + (rows_spec,),
        check_vma=False,
    )
```

```python
import functools

import jax
import jax.numpy as jnp
import numpy as np
from jax import lax
from jax.experimental import pallas as pl
from jax.experimental.pallas import tpu as pltpu
from jax.sharding import PartitionSpec as P

NEG_FILL = -1e30
EPSILON = 1e-06
BORDERS = (1, 2, 3, 4, 5, 6, 7, 8, 12, 16, 23, 32, 46, 64, 91)
LANES = 128
GROUPS = (4, 2)
LOW = jnp.bfloat16
FULL = jnp.float32
GELU_A = float(np.sqrt(2.0 / np.pi))
GELU_B = 0.044715


def bits_of(count):
    return count.bit_length() - 1


def swap(block, axis, bit):
    count = lax.axis_size(axis)
    return lax.ppermute(block, axis, [(i, i ^ (1 << bit)) for i in range(count)])


def add_low(left, right):
    return (left.astype(FULL) + right.astype(FULL)).astype(LOW)


def gather_shards(block):
    for bit in reversed(range(bits_of(lax.axis_size("shard")))):
        block = jnp.concatenate([block, swap(block, "shard", bit)], axis=0)
    return block


def gather_halves(block):
    for bit in reversed(range(1, bits_of(lax.axis_size("shard")))):
        block = jnp.concatenate([block, swap(block, "shard", bit)], axis=0)
    return block, swap(block, "shard", 0)


def scatter_shards(blocks, first_bit=0):
    for bit in range(first_bit, bits_of(lax.axis_size("shard"))):
        half = blocks.shape[0] // 2
        blocks = add_low(blocks[:half], swap(blocks[half:], "shard", bit))
    return blocks[0]


def sum_replicas(block, first_bit):
    for bit in range(first_bit, bits_of(lax.axis_size("rep"))):
        block = add_low(block, swap(block, "rep", bit))
    return block


def bucket_onehot(period, buckets):
    index = np.arange(period)
    relative = np.where(index < period // 2, index, index - period)
    distance = np.abs(relative)
    bucket = buckets // 2 * (relative > 0).astype(np.int64)
    for border in BORDERS:
        bucket = bucket + (distance >= border).astype(np.int64)
    return (bucket[:, None] == np.arange(buckets)[None, :]).astype(np.float32)


def mm(left, right):
    return lax.dot_general(left, right, (((1,), (0,)), ((), ())), preferred_element_type=FULL)


def mm_nt(left, right):
    return lax.dot_general(left, right, (((1,), (1,)), ((), ())), preferred_element_type=FULL)


def mm_tn(left, right):
    return lax.dot_general(left, right, (((0,), (0,)), ((), ())), preferred_element_type=FULL)


def inverse_rms(values):
    return lax.rsqrt(jnp.mean(values * values, axis=-1, keepdims=True) + EPSILON)


def norm_back(values, scale, gain, grad):
    inner = jnp.mean(gain * grad * values, axis=-1, keepdims=True)
    return scale * gain * grad - values * (scale * scale * scale * inner)


def pick(mask, left, right):
    return jnp.where(mask, left.astype(FULL), right.astype(FULL)).astype(left.dtype)


def aligned(index, size):
    return pl.ds(pl.multiple_of(index, 8), size)


def lanes_at(index, size):
    return pl.ds(pl.multiple_of(index, LANES), size)


def bias_tiles(bias_row, rows):
    rolled = pltpu.roll(
        jnp.broadcast_to(bias_row, (rows, 2 * rows)), 0, 1, stride=1, stride_axis=0
    )
    return rolled[:, :rows], rolled[:, rows:]


def pack_kernel(
    tile_step,
    meta,
    w_query,
    w_key,
    w_value,
    w_out,
    w_gate,
    w_up,
    w_down,
    gain_one,
    gain_two,
    table,
    qkv,
    out,
    feed,
    small,
):
    core, side = meta[0], meta[1]
    rows, half = w_query.shape[0], w_query.shape[1] // 2
    tiles = w_gate.shape[1] // (4 * LANES)
    for part, ref in enumerate((w_query, w_key, w_value)):
        qkv[:, part * half : (part + 1) * half] = ref[:, lanes_at(core * half, half)]
    out[...] = w_out[:, lanes_at(core * half, half)]
    for which, ref in enumerate((w_gate, w_up)):
        for t in range(tiles):
            lane = tile_step(core, side * tiles + t)
            first = (which * tiles + t) * rows
            feed[first : first + rows, :] = ref[:, lanes_at(lane, LANES)]
    down_rows = w_down.shape[0] // 4
    for t in range(w_down.shape[1] // LANES):
        first = 2 * tiles * rows + t * down_rows
        feed[first : first + down_rows, :] = w_down[
            aligned((2 * core + side) * down_rows, down_rows), t * LANES : (t + 1) * LANES
        ]
    small[...] = jnp.zeros(small.shape, LOW)
    small[0:1, :rows] = gain_one[...]
    small[1:2, :rows] = gain_two[...]
    small[2 : 2 + table.shape[0], : table.shape[1]] = table[...]


def norm_kernel(before, own, after, gain, normed):
    rows = own.shape[0]
    for index, ref in enumerate((before, own, after)):
        values = ref[...].astype(FULL)
        normed[index * rows : (index + 1) * rows, :] = (
            values * inverse_rms(values) * gain[...]
        ).astype(LOW)


def attend_kernel(
    shards,
    size,
    inv,
    meta,
    normed_a,
    normed_b,
    near_half,
    far_half,
    row_starts,
    col_starts,
    bias,
    heads,
    qkv,
    weights,
    kv_before,
):
    rows = row_starts.shape[1]
    width = normed_a.shape[1]
    shard_rows, half = width // shards, weights.shape[1] // 3
    for index in range(shards):
        source = (near_half, far_half)[index // (shards // 2)]
        first = index % (shards // 2) * shard_rows
        weights[aligned(inv[index] * shard_rows, shard_rows), :] = source[
            first : first + shard_rows, :
        ]
    for stream, normed in enumerate((normed_a, normed_b)):
        base = 2 * stream * rows
        for part in range(3):
            columns = slice(part * half, (part + 1) * half)
            qkv[base : base + 2 * rows, columns] = mm(
                normed[rows:, :], weights[:, columns]
            ).astype(LOW)
            if part:
                kv_before[:, (part - 1) * half : part * half] = mm(
                    normed[:rows, :], weights[:, columns]
                ).astype(LOW)
        own_col = col_starts[:, 2 * stream : 2 * stream + 1]
        in_before = own_col == row_starts[3 * stream : 3 * stream + 1, :]
        in_own = own_col == row_starts[3 * stream + 1 : 3 * stream + 2, :]
        in_after = own_col == row_starts[3 * stream + 2 : 3 * stream + 3, :]
        allowed = in_own | in_before | in_after
        own, ahead = slice(base, base + rows), slice(base + rows, base + 2 * rows)
        for pair in range(half // size // 2):
            mixed = []
            for head in (2 * pair, 2 * pair + 1):
                at = head * size
                query = qkv[own, at : at + size]
                keys = slice(half + at, half + at + size)
                values = slice(2 * half + at, 2 * half + at + size)
                near, far = bias_tiles(bias[head : head + 1, :], rows)
                scores = jnp.where(
                    in_own,
                    mm_nt(query, qkv[own, keys]) + near,
                    jnp.where(
                        in_before,
                        mm_nt(query, kv_before[:, at : at + size]),
                        mm_nt(query, qkv[ahead, keys]),
                    )
                    + far,
                )
                scores = jnp.where(allowed, scores, NEG_FILL)
                expd = jnp.exp(scores - jnp.max(scores, axis=-1, keepdims=True))
                probs = expd * (1.0 / jnp.sum(expd, axis=-1, keepdims=True))
                total = mm(jnp.where(in_own, probs, 0.0).astype(LOW), qkv[own, values])
                total = total + mm(
                    jnp.where(in_before, probs, 0.0).astype(LOW),
                    kv_before[:, half + at : half + at + size],
                )
                total = total + mm(
                    jnp.where(in_after, probs, 0.0).astype(LOW), qkv[ahead, values]
                )
                mixed.append(total)
            heads[stream * rows : (stream + 1) * rows, 2 * pair * size : (2 * pair + 2) * size] = (
                jnp.concatenate(mixed, axis=1).astype(LOW)
            )


def feed_kernel(
    shards,
    inv,
    meta,
    heads_mine,
    heads_other,
    tokens_a,
    tokens_b,
    cotangent_a,
    cotangent_b,
    gain,
    out_0,
    out_1,
    out_2,
    out_3,
    part_0,
    part_1,
    part_2,
    part_3,
    out_keep,
    out_send,
    d_keep,
    d_send,
    resid,
    normed_ff,
    hidden,
    d_gate,
    d_linear,
    w_out,
    w_gate,
    w_up,
    w_down,
):
    rows, width = tokens_a.shape
    inner = w_gate.shape[1]
    shard_rows, down_rows = width // shards, inner // shards // 2
    slab, half = inner // 2, width // 2
    tiles, down_tiles = slab // LANES, width // LANES
    block = part_0.shape[0] // (shards // 2)
    core, side = meta[0], meta[1]
    for index in range(shards):
        shard, first = inv[index], index % (shards // 2)
        upper = index // (shards // 2)
        target = aligned(shard * shard_rows, shard_rows)
        for other, sources in enumerate(((out_0, out_1), (out_2, out_3))):
            w_out[target, lanes_at((core ^ other) * half, half)] = sources[upper][
                first * shard_rows : (first + 1) * shard_rows, :
            ]
        for other, sources in enumerate(((part_0, part_1), (part_2, part_3))):
            part, start = sources[upper], first * block
            for t in range(tiles):
                lane = lanes_at((side ^ other) * slab + t * LANES, LANES)
                at = start + t * shard_rows
                w_gate[target, lane] = part[at : at + shard_rows, :]
                at = start + (tiles + t) * shard_rows
                w_up[target, lane] = part[at : at + shard_rows, :]
            down = aligned(shard * (2 * down_rows) + (side ^ other) * down_rows, down_rows)
            for t in range(down_tiles):
                at = start + 2 * tiles * shard_rows + t * down_rows
                w_down[down, t * LANES : (t + 1) * LANES] = part[at : at + down_rows, :]
    mine = mm(heads_mine[...], w_out[aligned(core * half, half), :])
    other = mm(heads_other[...], w_out[aligned((1 - core) * half, half), :])
    for stream, tokens in enumerate((tokens_a, tokens_b)):
        span, back = slice(stream * rows, (stream + 1) * rows), slice((1 - stream) * rows, (2 - stream) * rows)
        value = tokens[...].astype(FULL) + (mine[span] + other[back])
        resid[span, :] = value
        normed_ff[span, :] = (value * inverse_rms(value) * gain[...]).astype(LOW)
    for q in range(2):
        columns = slice(q * slab, (q + 1) * slab)
        for stream, cotangent in enumerate((cotangent_a, cotangent_b)):
            span = slice(stream * rows, (stream + 1) * rows)
            gate = mm(normed_ff[span, :], w_gate[:, columns])
            linear = mm(normed_ff[span, :], w_up[:, columns])
            d_hidden = mm_nt(cotangent[...], w_down[columns, :])
            square = gate * gate
            tanh = jnp.tanh(GELU_A * (gate + GELU_B * square * gate))
            rise = 0.5 * (1.0 + tanh)
            gelu = gate * rise
            slope = rise + 0.5 * gate * (1.0 - tanh * tanh) * (
                GELU_A * (1.0 + 3.0 * GELU_B * square)
            )
            hidden[span, columns] = (gelu * linear).astype(LOW)
            d_gate[span, columns] = (d_hidden * linear * slope).astype(LOW)
            d_linear[span, columns] = (d_hidden * gelu).astype(LOW)
    d_normed = mm_nt(d_gate[...], w_gate[...]) + mm_nt(d_linear[...], w_up[...])
    d_keep[...] = d_normed
    d_send[...] = d_normed.astype(LOW)
    out_keep[...] = resid[:rows, :] + mm(hidden[:rows, :], w_down[...])
    out_send[...] = mm(hidden[rows:, :], w_down[...]).astype(LOW)


def resid_grads_kernel(
    meta,
    d_keep,
    d_other,
    resid,
    cotangent_a,
    cotangent_b,
    gain,
    w_out,
    d_resid,
    d_attn,
    d_heads,
    d_gain,
):
    rows, width = cotangent_a.shape
    half = width // 2
    for stream, cotangent in enumerate((cotangent_a, cotangent_b)):
        span, back = slice(stream * rows, (stream + 1) * rows), slice((1 - stream) * rows, (2 - stream) * rows)
        d_normed = d_keep[span, :] + d_other[back, :].astype(FULL)
        values = resid[span, :]
        scale = inverse_rms(values)
        grad = cotangent[...].astype(FULL) + norm_back(values, scale, gain[...], d_normed)
        d_attn[span, :] = grad.astype(LOW)
        if stream == 0:
            d_resid[...] = grad
            d_gain[...] = jnp.sum(d_normed * values * scale, axis=0, keepdims=True)
    d_heads[...] = mm_nt(d_attn[...], w_out[aligned(meta[0] * half, half), :]).astype(LOW)


def feed_grads_kernel(
    shards,
    pos,
    meta,
    normed_ff,
    hidden,
    d_gate,
    d_linear,
    cotangent_a,
    cotangent_b,
    keep,
    send,
    down,
):
    width, inner = normed_ff.shape[1], hidden.shape[1]
    rows = cotangent_a.shape[0]
    shard_rows, down_rows = width // shards, inner // shards // 2
    slab = inner // 2
    tiles, down_tiles = slab // LANES, width // LANES
    for q in range(2):
        columns = slice(q * slab, (q + 1) * slab)
        down[columns, :] = (
            mm_tn(hidden[:rows, columns], cotangent_a[...])
            + mm_tn(hidden[rows:, columns], cotangent_b[...])
        ).astype(LOW)
    for other, target in ((1, send), (0, keep)):
        part = meta[1] ^ other
        for which, grad in enumerate((d_gate, d_linear)):
            value = mm_tn(normed_ff[...], grad[:, lanes_at(part * slab, slab)]).astype(LOW)
            for j in range(shards):
                for t in range(tiles):
                    first = (which * tiles + t) * shard_rows
                    target[pos[j], first : first + shard_rows, :] = value[
                        j * shard_rows : (j + 1) * shard_rows, t * LANES : (t + 1) * LANES
                    ]
        for j in range(shards):
            source = aligned(j * 2 * down_rows + part * down_rows, down_rows)
            for t in range(down_tiles):
                first = 2 * tiles * shard_rows + t * down_rows
                target[pos[j], first : first + down_rows, :] = down[
                    source, t * LANES : (t + 1) * LANES
                ]


def score_grads(query, key, value, grad, offset, mask):
    scores = jnp.where(mask, mm_nt(query, key) + offset, NEG_FILL)
    expd = jnp.exp(scores - jnp.max(scores, axis=-1, keepdims=True))
    probs = expd * (1.0 / jnp.sum(expd, axis=-1, keepdims=True))
    d_probs = mm_nt(grad, value)
    weighted = jnp.sum(d_probs * probs, axis=-1, keepdims=True)
    d_scores = (probs * (d_probs - weighted)).astype(LOW)
    return (
        mm(d_scores, key),
        mm_tn(d_scores, query),
        mm_tn(probs.astype(LOW), grad),
        d_scores.astype(FULL),
    )


def fold_diagonals(flat):
    rows = flat.shape[0]
    folded = flat[:8, :]
    for base in range(8, rows, 8):
        folded = folded + pltpu.roll(flat[base : base + 8, :], 2 * rows - base, 1)
    return folded


def inside_grads_kernel(
    size, meta, qkv, d_heads, row_starts, col_starts, bias, d_cols, d_bias
):
    rows, half = row_starts.shape[1], d_heads.shape[1]
    masks, grads = [], []
    for stream in range(2):
        own_col = col_starts[:, 2 * stream : 2 * stream + 1]
        own_row = row_starts[3 * stream + 1 : 3 * stream + 2, :]
        settled = own_col != meta[2 + stream]
        masks.append((own_col == own_row) & settled)
        began = settled & (own_col >= meta[4 + stream])
        grad = d_heads[stream * rows : (stream + 1) * rows, :].astype(FULL)
        grads.append(jnp.where(began, grad, 0.0).astype(LOW))
    for pair in range(half // size // 2):
        outs = []
        for head in (2 * pair, 2 * pair + 1):
            near, _ = bias_tiles(bias[head : head + 1, :], rows)
            at = head * size
            flat = jnp.zeros((rows, rows), FULL)
            for stream in range(2):
                own = slice(2 * stream * rows, (2 * stream + 1) * rows)
                one = score_grads(
                    qkv[own, at : at + size],
                    qkv[own, half + at : half + at + size],
                    qkv[own, 2 * half + at : 2 * half + at + size],
                    grads[stream][:, at : at + size],
                    near,
                    masks[stream],
                )
                flat = flat + one[3]
                outs.append(one)
            flat = jnp.concatenate([flat, jnp.zeros((rows, rows), FULL)], axis=1)
            d_bias[8 * head : 8 * head + 8, :] = fold_diagonals(flat)
        for part in range(3):
            columns = slice(part * half + 2 * pair * size, part * half + (2 * pair + 2) * size)
            for stream in range(2):
                d_cols[stream * rows : (stream + 1) * rows, columns] = jnp.concatenate(
                    [outs[stream][part], outs[2 + stream][part]], axis=1
                ).astype(LOW)


def crossing_grads_kernel(
    shards,
    first_head,
    last_head,
    size,
    with_out,
    inv,
    meta,
    qkv,
    normed_a,
    normed_b,
    d_heads,
    d_after,
    d_inside,
    row_starts,
    col_starts,
    bias,
    *refs,
):
    if with_out:
        heads_mine, heads_other, d_attn, d_cols, keep, send, d_bias, d_weights = refs
    else:
        d_cols, keep, send, d_bias, d_weights = refs
    rows, half = row_starts.shape[1], d_heads.shape[1]
    width = normed_a.shape[1]
    group = (last_head - first_head) * size
    span = slice(first_head * size, last_head * size)
    last_cols, masks, turns, mixes, grads = [], [], [], [], []
    for stream in range(2):
        tail = meta[2 + stream]
        own_col = col_starts[:, 2 * stream : 2 * stream + 1]
        after_col = col_starts[:, 2 * stream + 1 : 2 * stream + 2]
        own_row = row_starts[3 * stream + 1 : 3 * stream + 2, :]
        after_row = row_starts[3 * stream + 2 : 3 * stream + 3, :]
        is_last_col, is_last_row = own_col == tail, own_row == tail
        mix_col = jnp.where(is_last_col, own_col, after_col)
        mix_row = jnp.where(is_last_row, own_row, after_row)
        last_cols.append(is_last_col)
        masks.append((mix_col == tail) & (mix_row == tail))
        turns.append(is_last_col != is_last_row)
        base = 2 * stream * rows
        mix = []
        for part in range(3):
            columns = slice(part * half + first_head * size, part * half + last_head * size)
            mix.append(
                pick(
                    is_last_col,
                    qkv[base : base + rows, columns],
                    qkv[base + rows : base + 2 * rows, columns],
                )
            )
        mixes.append(mix)
        here = slice(stream * rows, (stream + 1) * rows)
        mixed = jnp.where(
            is_last_col, d_heads[here, span].astype(FULL), d_after[here, span].astype(FULL)
        )
        grads.append(jnp.where(mix_col == tail, mixed, 0.0).astype(LOW))
    for pair in range((last_head - first_head) // 2):
        outs = []
        for index in (2 * pair, 2 * pair + 1):
            head = first_head + index
            near, far = bias_tiles(bias[head : head + 1, :], rows)
            at = index * size
            kept, turned = jnp.zeros((rows, rows), FULL), jnp.zeros((rows, rows), FULL)
            for stream in range(2):
                mix = mixes[stream]
                two = score_grads(
                    mix[0][:, at : at + size],
                    mix[1][:, at : at + size],
                    mix[2][:, at : at + size],
                    grads[stream][:, at : at + size],
                    jnp.where(turns[stream], far, near),
                    masks[stream],
                )
                kept = kept + jnp.where(turns[stream], 0.0, two[3])
                turned = turned + jnp.where(turns[stream], two[3], 0.0)
                outs.append(two)
            d_bias[8 * index : 8 * index + 8, :] = fold_diagonals(
                jnp.concatenate([kept, turned], axis=1)
            )
        for part in range(3):
            columns = slice(part * group + 2 * pair * size, part * group + (2 * pair + 2) * size)
            for stream in range(2):
                d_cols[stream * rows : (stream + 1) * rows, columns] = jnp.concatenate(
                    [outs[stream][part], outs[2 + stream][part]], axis=1
                ).astype(LOW)
    total = [jnp.zeros((width, group), FULL) for _ in range(3)]
    for stream, normed in enumerate((normed_a, normed_b)):
        own, ahead = normed[rows : 2 * rows, :], normed[2 * rows :, :]
        normed_mix = pick(last_cols[stream], own, ahead)
        here = slice(stream * rows, (stream + 1) * rows)
        for part in range(3):
            inner = slice(part * half + first_head * size, part * half + last_head * size)
            total[part] = total[part] + mm_tn(own, d_inside[here, inner])
            total[part] = total[part] + mm_tn(
                normed_mix, d_cols[here, part * group : (part + 1) * group]
            )
    for part in range(3):
        d_weights[:, part * group : (part + 1) * group] = total[part].astype(LOW)
    if with_out:
        columns = slice(3 * group, 3 * group + half)
        lane = lanes_at(meta[0] * half, half)
        value = mm_tn(heads_mine[...], d_attn[:, lane])
        d_weights[aligned(meta[0] * half, half), columns] = value.astype(LOW)
        value = mm_tn(heads_other[:rows, :], d_attn[rows:, lane])
        value = value + mm_tn(heads_other[rows:, :], d_attn[:rows, lane])
        d_weights[aligned((1 - meta[0]) * half, half), columns] = value.astype(LOW)
    shard_rows = width // shards
    for index in range(shards):
        target = (keep, send)[index // (shards // 2)]
        target[index % (shards // 2), :, :] = d_weights[
            aligned(inv[index] * shard_rows, shard_rows), :
        ]


def normed_grads_kernel(sizes, meta, weights, d_inside, col_starts, *refs):
    *crossing, keep, send = refs
    rows, half = col_starts.shape[0], weights.shape[1] // 3
    inside = mm_nt(d_inside[...], weights[...])
    across = jnp.zeros(inside.shape, FULL)
    begin = 0
    for ref, group in zip(crossing, sizes, strict=True):
        for part in range(3):
            across = across + mm_nt(
                ref[:, part * group : (part + 1) * group],
                weights[:, part * half + begin : part * half + begin + group],
            )
        begin += group
    for stream, target in enumerate((keep, send)):
        is_last = col_starts[:, 2 * stream : 2 * stream + 1] == meta[2 + stream]
        here = slice(stream * rows, (stream + 1) * rows)
        target[:rows, :] = jnp.where(is_last, across[here], inside[here]).astype(target.dtype)
        target[rows:, :] = jnp.where(is_last, 0.0, across[here]).astype(target.dtype)


def join_kernel(own, after, keep, other, d_own, d_after, d_gain):
    rows = own.shape[0]
    mine = keep[:rows, :] + other[:rows, :].astype(FULL)
    sent = keep[rows:, :] + other[rows:, :].astype(FULL)
    d_own[...] = mine
    d_after[...] = sent.astype(LOW)
    values, ahead = own[...].astype(FULL), after[...].astype(FULL)
    share = mine * values * inverse_rms(values) + sent * ahead * inverse_rms(ahead)
    d_gain[...] = jnp.sum(share, axis=0, keepdims=True)


def tokens_kernel(own, gain, d_resid, d_own, d_before, out_keep, out_other, d_tokens, output):
    values = own[...].astype(FULL)
    grad = d_own[...] + d_before[...].astype(FULL)
    d_tokens[...] = d_resid[...] + norm_back(values, inverse_rms(values), gain[...], grad)
    output[...] = (out_keep[...] + out_other[...].astype(FULL)).astype(LOW)


def unpack_feed_kernel(
    tile_step, meta, part_0, part_1, part_2, part_3, d_gate, d_up, d_down
):
    rows = d_gate.shape[0]
    tiles = d_gate.shape[1] // (4 * LANES)
    down_rows = d_down.shape[0] // 4
    for index, part in enumerate((part_0, part_1, part_2, part_3)):
        core, side = meta[0] ^ (index & 1), meta[1] ^ (index >> 1)
        for t in range(tiles):
            lane = lanes_at(tile_step(core, side * tiles + t), LANES)
            d_gate[:, lane] = part[t * rows : (t + 1) * rows, :].astype(FULL)
            first = (tiles + t) * rows
            d_up[:, lane] = part[first : first + rows, :].astype(FULL)
        target = aligned((2 * core + side) * down_rows, down_rows)
        for t in range(d_down.shape[1] // LANES):
            first = 2 * tiles * rows + t * down_rows
            d_down[target, t * LANES : (t + 1) * LANES] = part[
                first : first + down_rows, :
            ].astype(FULL)


def unpack_attend_kernel(sizes, meta, *refs):
    halves, (d_query, d_key, d_value, d_out) = refs[:-4], refs[-4:]
    half = d_query.shape[1] // 2
    begin = 0
    for g, group in enumerate(sizes):
        for other in range(2):
            ref = halves[2 * g + other]
            core = meta[0] ^ other
            for part, target in enumerate((d_query, d_key, d_value)):
                target[:, lanes_at(core * half + begin, group)] = ref[
                    :, part * group : (part + 1) * group
                ].astype(FULL)
            if g == 0:
                d_out[:, lanes_at(core * half, half)] = ref[:, 3 * group :].astype(FULL)
        begin += group


def call(kernel, scalars, arrays, outs, scratch=(), flops=0, after=()):
    def in_vmem(_):
        return pl.BlockSpec(memory_space=pltpu.VMEM)

    def in_smem(_):
        return pl.BlockSpec(memory_space=pltpu.SMEM)

    skip = len(after)

    def body(*refs):
        kernel(*refs[skip:])

    moved = sum(a.size * a.dtype.itemsize for a in (*arrays, *outs))
    return pl.pallas_call(
        body,
        out_shape=outs,
        in_specs=[pl.BlockSpec(memory_space=pl.ANY) for _ in after]
        + [in_smem(a) for a in scalars]
        + [in_vmem(a) for a in arrays],
        out_specs=tuple(in_vmem(a) for a in outs),
        scratch_shapes=scratch,
        compiler_params=pltpu.CompilerParams(vmem_limit_bytes=58 * 2**20),
        cost_estimate=pl.CostEstimate(flops=flops, bytes_accessed=moved, transcendentals=0),
        name=getattr(kernel, "func", kernel).__name__,
    )(*after, *scalars, *arrays)


def shaped(shape, dtype):
    return jax.ShapeDtypeStruct(shape, dtype)


def per_device(
    tokens,
    cotangent,
    offsets,
    w_query,
    w_key,
    w_value,
    w_attn_out,
    w_gate,
    w_up,
    w_ff_out,
    gain_attn,
    gain_ff,
    rel_table,
):
    rows, width = tokens.shape
    shards = lax.axis_size("shard")
    shard, rep = lax.axis_index("shard"), lax.axis_index("rep")
    heads_count, table_rows = rel_table.shape[1], rel_table.shape[0]
    buckets = table_rows * shards
    shard_rows, inner = w_gate.shape
    half, size = width // 2, width // heads_count
    own_heads = heads_count // 2
    piece = w_ff_out.shape[0] // 2
    core, side = rep % 2, rep // 2 % 2
    index = jnp.arange(shards, dtype=jnp.int32)

    def turned(values):
        result = jnp.zeros_like(values)
        for bit in range(bits_of(shards)):
            result = result | (((values >> bit) & 1) << (bits_of(shards) - 1 - bit))
        return result

    pos, inv = turned(index ^ shard), turned(index) ^ shard
    starts_all = jnp.arange(offsets.shape[0], dtype=jnp.int32) - offsets
    start_pad = jnp.pad(starts_all, (rows, rows), constant_values=-1)
    first_a, first_b = (rep * shards + shard) * rows, ((rep ^ 1) * shards + shard) * rows
    window_a = lax.dynamic_slice_in_dim(start_pad, first_a, 3 * rows).reshape(3, rows)
    window_b = lax.dynamic_slice_in_dim(start_pad, first_b, 3 * rows).reshape(3, rows)
    row_starts = jnp.concatenate([window_a, window_b], axis=0)
    col_starts = jnp.stack([window_a[1], window_a[2], window_b[1], window_b[2]], axis=1)
    meta = jnp.stack(
        [core, side, window_a[1, rows - 1], window_b[1, rows - 1], first_a, first_b]
    ).astype(jnp.int32)

    by_tiles = piece % LANES == 0

    def tile_step(which_core, tile):
        if by_tiles:
            per_shard = piece // LANES
            return ((tile // per_shard * 2 + which_core) * per_shard + tile % per_shard) * LANES
        return which_core * (inner // 2) + tile * LANES

    def by_core(matrix):
        if by_tiles:
            return matrix
        split = matrix.reshape(shard_rows, shards, 2, piece).transpose(0, 2, 1, 3)
        return split.reshape(shard_rows, inner)

    def from_core(matrix):
        if by_tiles:
            return matrix
        split = matrix.reshape(shard_rows, 2, shards, piece).transpose(0, 2, 1, 3)
        return split.reshape(shard_rows, inner)

    tiles = inner // (4 * LANES)
    block = 2 * tiles * shard_rows + width // LANES * (piece // 2)
    qkv_own, out_own, ff_own, small = call(
        functools.partial(pack_kernel, tile_step),
        (meta,),
        (
            w_query,
            w_key,
            w_value,
            w_attn_out,
            by_core(w_gate),
            by_core(w_up),
            w_ff_out,
            gain_attn.reshape(1, shard_rows),
            gain_ff.reshape(1, shard_rows),
            rel_table,
        ),
        (
            shaped((shard_rows, 3 * half), LOW),
            shaped((shard_rows, half), LOW),
            shaped((block, LANES), LOW),
            shaped((8, LANES), LOW),
        ),
    )
    up = [(i, i + 1) for i in range(shards - 1)]
    down = [(i + 1, i) for i in range(shards - 1)]
    small_all = gather_shards(small)
    before = lax.ppermute(tokens, "shard", up)
    after = lax.ppermute(tokens, "shard", down)
    tokens_b, cotangent_b = swap(tokens, "rep", 0), swap(cotangent, "rep", 0)
    qkv_near, qkv_far = gather_halves(qkv_own)
    out_near, out_far = gather_halves(out_own)
    out_parts = (out_near, out_far, swap(out_near, "rep", 0), swap(out_far, "rep", 0))
    ff_near, ff_far = gather_halves(ff_own)
    ff_parts = (ff_near, ff_far, swap(ff_near, "rep", 1), swap(ff_far, "rep", 1))

    order = (pos[:, None] == index[None, :]).astype(LOW)
    small_all = jnp.dot(
        order, small_all.reshape(shards, 8 * LANES), preferred_element_type=FULL
    ).reshape(shards, 8, LANES)
    gain_one = small_all[:, 0, :shard_rows].reshape(1, width)
    gain_two = small_all[:, 1, :shard_rows].reshape(1, width)
    table = small_all[:, 2 : 2 + table_rows, :heads_count].reshape(buckets, heads_count)
    table = lax.dynamic_slice_in_dim(table, core * own_heads, own_heads, axis=1)
    bias = lax.dot_general(
        table.astype(LOW),
        jnp.asarray(bucket_onehot(2 * rows, buckets)).astype(LOW),
        (((0,), (1,)), ((), ())),
        preferred_element_type=FULL,
    )
    (normed_a,) = call(
        norm_kernel, (), (before, tokens, after, gain_one), (shaped((3 * rows, width), LOW),)
    )
    normed_b = swap(normed_a, "rep", 0)

    heads, qkv, w_qkv = call(
        functools.partial(attend_kernel, shards, size),
        (inv, meta),
        (normed_a, normed_b, qkv_near, qkv_far, row_starts, col_starts, bias),
        (
            shaped((2 * rows, half), LOW),
            shaped((4 * rows, 3 * half), LOW),
            shaped((width, 3 * half), LOW),
        ),
        [pltpu.VMEM((rows, 2 * half), LOW)],
        flops=10 * rows * width * width * 2,
    )
    heads_other = swap(heads, "rep", 0)
    wide = shaped((2 * rows, inner // 2), LOW)
    (
        out_keep,
        out_send,
        d_normed_keep,
        d_normed_send,
        resid,
        normed_ff,
        hidden,
        d_gate,
        d_linear,
        w_out,
    ) = call(
        functools.partial(feed_kernel, shards),
        (inv, meta),
        (heads, heads_other, tokens, tokens_b, cotangent, cotangent_b, gain_two)
        + out_parts
        + ff_parts,
        (
            shaped((rows, width), FULL),
            shaped((rows, width), LOW),
            shaped((2 * rows, width), FULL),
            shaped((2 * rows, width), LOW),
            shaped((2 * rows, width), FULL),
            shaped((2 * rows, width), LOW),
            wide,
            wide,
            wide,
            shaped((width, width), LOW),
        ),
        [
            pltpu.VMEM((width, inner // 2), LOW),
            pltpu.VMEM((width, inner // 2), LOW),
            pltpu.VMEM((inner // 2, width), LOW),
        ],
        flops=14 * rows * width * inner,
    )
    d_normed_other = swap(d_normed_send, "rep", 0)
    d_resid, d_attn, d_heads, d_gain_two = call(
        resid_grads_kernel,
        (meta,),
        (d_normed_keep, d_normed_other, resid, cotangent, cotangent_b, gain_two, w_out),
        (
            shaped((rows, width), FULL),
            shaped((2 * rows, width), LOW),
            shaped((2 * rows, half), LOW),
            shaped((1, width), FULL),
        ),
        flops=2 * rows * width * width,
    )
    d_heads_after = lax.ppermute(d_heads, "shard", down)
    out_other = swap(out_send, "rep", 0)
    ff_keep, ff_send = call(
        functools.partial(feed_grads_kernel, shards),
        (pos, meta),
        (normed_ff, hidden, d_gate, d_linear, cotangent, cotangent_b),
        (shaped((shards, block, LANES), LOW),) * 2,
        [pltpu.VMEM((inner // 2, width), LOW)],
        flops=6 * rows * width * inner,
    )
    d_inside, d_bias = call(
        functools.partial(inside_grads_kernel, size),
        (meta,),
        (qkv, d_heads, row_starts, col_starts, bias),
        (shaped((2 * rows, 3 * half), LOW), shaped((8 * own_heads, 2 * rows), FULL)),
        flops=8 * rows * width * width,
    )

    d_ff = add_low(ff_keep, swap(ff_send, "rep", 1))
    d_ff = sum_replicas(scatter_shards(d_ff), 2)
    d_ff_side = swap(d_ff, "rep", 1)
    d_ff_parts = (d_ff, swap(d_ff, "rep", 0), d_ff_side, swap(d_ff_side, "rep", 0))

    halves, crossing, d_biases, sizes = [], [], [], []
    first = 0
    for count in GROUPS:
        group, extra = count * size, 0 if first else half
        more = () if first else (heads, heads_other, d_attn)
        sizes.append(group)
        d_cols, keep, send, d_bias_part = call(
            functools.partial(
                crossing_grads_kernel, shards, first, first + count, size, not first
            ),
            (inv, meta),
            (
                qkv,
                normed_a,
                normed_b,
                d_heads,
                d_heads_after,
                d_inside,
                row_starts,
                col_starts,
                bias,
            )
            + more,
            (
                shaped((2 * rows, 3 * group), LOW),
                shaped((shards // 2, shard_rows, 3 * group + extra), LOW),
                shaped((shards // 2, shard_rows, 3 * group + extra), LOW),
                shaped((8 * count, 2 * rows), FULL),
            ),
            [pltpu.VMEM((width, 3 * group + extra), LOW)],
            flops=24 * rows * width * group,
        )
        first += count
        crossing.append(d_cols)
        d_biases.append(d_bias_part)
        mine = scatter_shards(add_low(keep, swap(send, "shard", 0)), 1)
        mine = sum_replicas(mine, 1)
        halves += [mine, swap(mine, "rep", 0)]

    keep, send = call(
        functools.partial(normed_grads_kernel, tuple(sizes)),
        (meta,),
        (w_qkv, d_inside, col_starts, *crossing),
        (shaped((2 * rows, width), FULL), shaped((2 * rows, width), LOW)),
        flops=12 * rows * width * width,
    )
    d_own, d_after, d_gain_one = call(
        join_kernel,
        (),
        (tokens, after, keep, swap(send, "rep", 0)),
        (
            shaped((rows, width), FULL),
            shaped((rows, width), LOW),
            shaped((1, width), FULL),
        ),
    )
    d_before = lax.ppermute(d_after, "shard", up)
    d_tokens, output = call(
        tokens_kernel,
        (),
        (tokens, gain_one, d_resid, d_own, d_before, out_keep, out_other),
        (shaped((rows, width), FULL), shaped((rows, width), LOW)),
    )

    folds = np.stack([np.roll(bucket_onehot(2 * rows, buckets), row, axis=0) for row in range(8)])
    d_bias = (d_bias + jnp.concatenate(d_biases, axis=0)).reshape(own_heads, 16 * rows)
    d_table = lax.dot_general(
        d_bias,
        jnp.asarray(folds.reshape(16 * rows, buckets)),
        (((1,), (0,)), ((), ())),
        precision=lax.Precision.HIGHEST,
    )
    d_table = lax.dynamic_update_slice(
        jnp.zeros((heads_count, buckets), FULL), d_table, (core * own_heads, 0)
    ).T
    smalls = jnp.concatenate([d_gain_one.reshape(-1), d_gain_two.reshape(-1), d_table.reshape(-1)])
    rest = -smalls.shape[0] % (8 * LANES)
    smalls = jnp.pad(smalls, (0, rest)).reshape(-1, LANES)
    for axis in ("rep", "shard"):
        for bit in range(bits_of(lax.axis_size(axis))):
            smalls = smalls + swap(smalls, axis, bit)
    smalls = smalls.reshape(-1)

    def own_part(begin, length):
        return lax.dynamic_slice_in_dim(smalls, begin + shard * length, length)

    d_w_gate, d_w_up, d_w_ff_out = call(
        functools.partial(unpack_feed_kernel, tile_step),
        (meta,),
        d_ff_parts,
        (
            shaped(w_gate.shape, FULL),
            shaped(w_up.shape, FULL),
            shaped(w_ff_out.shape, FULL),
        ),
    )
    d_w_query, d_w_key, d_w_value, d_w_attn_out = call(
        functools.partial(unpack_attend_kernel, tuple(sizes)),
        (meta,),
        tuple(halves),
        (shaped(w_query.shape, FULL),) * 4,
    )
    return (
        output,
        d_tokens,
        d_w_query,
        d_w_key,
        d_w_value,
        d_w_attn_out,
        from_core(d_w_gate),
        from_core(d_w_up),
        d_w_ff_out,
        own_part(0, shard_rows),
        own_part(width, shard_rows),
        own_part(2 * width, table_rows * heads_count).reshape(table_rows, heads_count),
    )


def solution(mesh):
    tokens_spec, rows_spec, line_spec = P(("rep", "shard"), None), P("shard", None), P("shard")
    return jax.shard_map(
        per_device,
        mesh=mesh,
        in_specs=(tokens_spec, tokens_spec, P()) + (rows_spec,) * 7 + (line_spec,) * 2 + (rows_spec,),
        out_specs=(tokens_spec,) * 2 + (rows_spec,) * 7 + (line_spec,) * 2 + (rows_spec,),
        check_vma=False,
    )
```

```python
import functools

import jax
import jax.numpy as jnp
import numpy as np
from jax import lax
from jax.experimental import pallas as pl
from jax.experimental.pallas import tpu as pltpu
from jax.sharding import PartitionSpec as P

NEG_FILL = -1e30
EPSILON = 1e-06
BORDERS = (1, 2, 3, 4, 5, 6, 7, 8, 12, 16, 23, 32, 46, 64, 91)
LANES = 128
SMALL = 8
SCALE = 2 * 10**8
GROUPS = (4, 2)
LOW = jnp.bfloat16
FULL = jnp.float32
GELU_A = float(np.sqrt(2.0 / np.pi))
GELU_B = 0.044715


def bits_of(count):
    return count.bit_length() - 1


def swap(block, axis, bit):
    count = lax.axis_size(axis)
    return lax.ppermute(block, axis, [(i, i ^ (1 << bit)) for i in range(count)])


def add_low(left, right):
    return (left.astype(FULL) + right.astype(FULL)).astype(LOW)


def gather_shards(block):
    for bit in far_first(lax.axis_size("shard")):
        block = jnp.concatenate([block, swap(block, "shard", bit)], axis=0)
    return block


def reverse_bits(value, count):
    result = 0
    for bit in range(bits_of(count)):
        result = result | (((value >> bit) & 1) << (bits_of(count) - 1 - bit))
    return result


def far_first(shards):
    return tuple(reversed(range(bits_of(shards))))


def near_first(shards):
    return tuple(range(bits_of(shards)))


def shards_at(shard, shards, order):
    places = []
    for place in range(shards):
        moved = sum(((place >> step) & 1) << bit for step, bit in enumerate(order))
        places.append(shard ^ moved)
    return places


def exchange(block, stage):
    return swap(block, *stage)


def places_of(stages, shards):
    places = []
    for place in range(2 ** len(stages)):
        side, shard = 0, 0
        for step, (axis, bit) in enumerate(stages):
            here = (place >> (len(stages) - 1 - step)) & 1
            if axis == "rep":
                side |= here
            else:
                shard |= here << bit
        places.append((side, shard))
    return places


def mark_kernel():
    pass


class Sequence:
    def __init__(self, token):
        self.token = token

    def take(self, received):
        received, self.token = lax.optimization_barrier((received, self.token))
        return received

    def add(self, kept, received):
        return add_low(kept, self.take(received))

    def mark(self, *ready):
        self.call(None, (), (), (), waits=ready, micros=500)

    def call(self, kernel, scalars, arrays, outs, scratch=(), micros=3, waits=()):
        skip, given = 1 + len(waits), 1 + len(waits) + len(scalars) + len(arrays) + len(outs)

        def body(*refs):
            if kernel is not None:
                kernel(*refs[skip:given], *refs[given + 1 :])

        def placed(arrays, space):
            return [pl.BlockSpec(memory_space=space) for _ in arrays]

        *results, self.token = pl.pallas_call(
            body,
            out_shape=(*outs, shaped(self.token.shape, self.token.dtype)),
            in_specs=placed((self.token, *waits), pl.ANY)
            + placed(scalars, pltpu.SMEM)
            + placed(arrays, pltpu.VMEM),
            out_specs=(*placed(outs, pltpu.VMEM), pl.BlockSpec(memory_space=pl.ANY)),
            scratch_shapes=scratch,
            input_output_aliases={0: len(outs)},
            compiler_params=pltpu.CompilerParams(vmem_limit_bytes=58 * 2**20),
            cost_estimate=pl.CostEstimate(
                flops=int(micros * SCALE), bytes_accessed=10**6, transcendentals=0
            ),
            name=getattr(kernel, "func", kernel or mark_kernel).__name__,
        )(self.token, *waits, *scalars, *arrays)
        return results


def halves_of(blocks):
    half = blocks.shape[0] // 2
    return blocks[:half], blocks[half:]


def send_half(blocks, stage):
    kept, sent = halves_of(blocks)
    return kept, exchange(sent, stage)


def sum_replicas(block, first_bit):
    for bit in range(first_bit, bits_of(lax.axis_size("rep"))):
        block = add_low(block, swap(block, "rep", bit))
    return block


def bucket_onehot(period, buckets):
    index = np.arange(period)
    relative = np.where(index < period // 2, index, index - period)
    distance = np.abs(relative)
    bucket = buckets // 2 * (relative > 0).astype(np.int64)
    for border in BORDERS:
        bucket = bucket + (distance >= border).astype(np.int64)
    return (bucket[:, None] == np.arange(buckets)[None, :]).astype(np.float32)


def mm(left, right):
    return lax.dot_general(left, right, (((1,), (0,)), ((), ())), preferred_element_type=FULL)


def mm_nt(left, right):
    return lax.dot_general(left, right, (((1,), (1,)), ((), ())), preferred_element_type=FULL)


def mm_tn(left, right):
    return lax.dot_general(left, right, (((0,), (0,)), ((), ())), preferred_element_type=FULL)


def inverse_rms(values):
    return lax.rsqrt(jnp.mean(values * values, axis=-1, keepdims=True) + EPSILON)


def norm_back(values, scale, gain, grad):
    inner = jnp.mean(gain * grad * values, axis=-1, keepdims=True)
    return scale * gain * grad - values * (scale * scale * scale * inner)


def pick(mask, left, right):
    return jnp.where(mask, left.astype(FULL), right.astype(FULL)).astype(left.dtype)


def aligned(index, size):
    return pl.ds(pl.multiple_of(index, 8), size)


def lanes_at(index, size):
    return pl.ds(pl.multiple_of(index, LANES), size)


def bias_tiles(bias_row, rows):
    rolled = pltpu.roll(
        jnp.broadcast_to(bias_row, (rows, 2 * rows)), 0, 1, stride=1, stride_axis=0
    )
    return rolled[:, :rows], rolled[:, rows:]


def core_of(where):
    return where[0] & 1


def side_of(where):
    return (where[0] >> 1) & 1


def tail_of(row_starts, stream):
    rows = row_starts.shape[1]
    return row_starts[3 * stream + 1 : 3 * stream + 2, rows - 1 : rows]


def pack_kernel(
    tile_step,
    where,
    w_query,
    w_key,
    w_value,
    w_out,
    w_gate,
    w_up,
    w_down,
    gain_one,
    gain_two,
    table,
    qkv,
    feed,
    rest,
):
    core, side = core_of(where), side_of(where)
    rows, half = w_query.shape[0], w_query.shape[1] // 2
    tiles = w_gate.shape[1] // (4 * LANES)
    width = qkv.shape[1]
    qkv[rows:, :] = jnp.zeros((SMALL, width), LOW)
    for which in range(2):

        @pl.when(side == which)
        def _():
            for t in range(width // LANES):
                part, tile = divmod(which * (3 * half - width) // LANES + t, half // LANES)
                qkv[:rows, t * LANES : (t + 1) * LANES] = (w_query, w_key, w_value)[part][
                    :, lanes_at(core * half + tile * LANES, LANES)
                ]

    qkv[rows : rows + 1, :rows] = gain_one[...]
    qkv[rows + 1 : rows + 2, :rows] = gain_two[...]
    qkv[rows + 2 : rows + 2 + table.shape[0], : table.shape[1]] = table[...]
    for which, ref in enumerate((w_gate, w_up)):
        for t in range(tiles):
            lane = tile_step(core, side * tiles + t)
            first = (which * tiles + t) * rows
            feed[first : first + rows, :] = ref[:, lanes_at(lane, LANES)]
    down_rows = w_down.shape[0] // 2
    own = aligned(core * down_rows, down_rows)
    rest[:down_rows, :] = w_down[own, :half]
    rest[down_rows : 2 * down_rows, :] = w_down[own, half:]
    rest[2 * down_rows :, :] = w_out[:, lanes_at(core * half, half)]


def attend_kernel(
    shards,
    size,
    where,
    own_a,
    halo_a,
    pair_b,
    halo_b,
    part_0,
    part_1,
    part_2,
    part_3,
    row_starts,
    col_starts,
    onehot,
    heads,
    normed,
    qkv,
    weights,
    gains,
    bias,
    kv_before,
    smalls,
):
    rows, width = own_a.shape
    shard_rows, half = width // shards, weights.shape[1] // 3
    block = shard_rows + SMALL
    for index, shard in enumerate(shards_at(where[1], shards, far_first(shards))):
        upper, first = index // (shards // 2), index % (shards // 2) * block
        for other, sources in enumerate(((part_0, part_1), (part_2, part_3))):
            source = sources[upper]
            lane = (side_of(where) ^ other) * (weights.shape[1] - source.shape[1])
            weights[
                aligned(shard * shard_rows, shard_rows), lanes_at(lane, source.shape[1])
            ] = source[first : first + shard_rows, :]
        source = (part_0, part_1)[upper]
        smalls[aligned(shard * SMALL, SMALL), :] = source[
            first + shard_rows : first + block, :LANES
        ].astype(FULL)
    total = jnp.zeros((SMALL, width), FULL)
    for shard in range(shards):
        line = jnp.concatenate(
            [
                smalls[shard * SMALL : (shard + 1) * SMALL, :],
                jnp.zeros((SMALL, width - LANES), FULL),
            ],
            axis=1,
        )
        total = total + (pltpu.roll(line, shard * shard_rows, 1) if shard else line)
    gains[...] = total
    gain = total[0:1, :]
    heads_here = half // size
    shift = jnp.where(core_of(where) == 0, 0, LANES - heads_here)
    table = pltpu.roll(smalls[...], shift, 1).astype(LOW)
    bias[...] = mm_tn(table, onehot[...])[: bias.shape[0], :]
    for stream, (own_ref, halo) in enumerate(((own_a, halo_a), (pair_b, halo_b))):
        base = 2 * stream * rows
        lines = []
        for tokens in (halo[:rows, :], own_ref[:rows, :], halo[rows:, :]):
            values = tokens.astype(FULL)
            lines.append((values * inverse_rms(values) * gain).astype(LOW))
        normed[base : base + rows, :] = lines[1]
        normed[base + rows : base + 2 * rows, :] = lines[2]
        for part in range(3):
            columns = slice(part * half, (part + 1) * half)
            qkv[base : base + 2 * rows, columns] = mm(
                normed[base : base + 2 * rows, :], weights[:, columns]
            ).astype(LOW)
            if part:
                kv_before[:, (part - 1) * half : part * half] = mm(
                    lines[0], weights[:, columns]
                ).astype(LOW)
        own_col = col_starts[:, 2 * stream : 2 * stream + 1]
        in_before = own_col == row_starts[3 * stream : 3 * stream + 1, :]
        in_own = own_col == row_starts[3 * stream + 1 : 3 * stream + 2, :]
        in_after = own_col == row_starts[3 * stream + 2 : 3 * stream + 3, :]
        allowed = in_own | in_before | in_after
        own, ahead = slice(base, base + rows), slice(base + rows, base + 2 * rows)
        for pair in range(half // size // 2):
            mixed = []
            for head in (2 * pair, 2 * pair + 1):
                at = head * size
                query = qkv[own, at : at + size]
                keys = slice(half + at, half + at + size)
                values = slice(2 * half + at, 2 * half + at + size)
                near, far = bias_tiles(bias[head : head + 1, :], rows)
                scores = jnp.where(
                    in_own,
                    mm_nt(query, qkv[own, keys]) + near,
                    jnp.where(
                        in_before,
                        mm_nt(query, kv_before[:, at : at + size]),
                        mm_nt(query, qkv[ahead, keys]),
                    )
                    + far,
                )
                scores = jnp.where(allowed, scores, NEG_FILL)
                expd = jnp.exp(scores - jnp.max(scores, axis=-1, keepdims=True))
                probs = expd * (1.0 / jnp.sum(expd, axis=-1, keepdims=True))
                total = mm(jnp.where(in_own, probs, 0.0).astype(LOW), qkv[own, values])
                total = total + mm(
                    jnp.where(in_before, probs, 0.0).astype(LOW),
                    kv_before[:, half + at : half + at + size],
                )
                total = total + mm(
                    jnp.where(in_after, probs, 0.0).astype(LOW), qkv[ahead, values]
                )
                mixed.append(total)
            heads[stream * rows : (stream + 1) * rows, 2 * pair * size : (2 * pair + 2) * size] = (
                jnp.concatenate(mixed, axis=1).astype(LOW)
            )


def feed_kernel(
    shards,
    where,
    heads_mine,
    heads_other,
    tokens_a,
    cotangent_a,
    pair_b,
    gains,
    rest_0,
    rest_1,
    rest_2,
    rest_3,
    part_0,
    part_1,
    part_2,
    part_3,
    out_keep,
    out_send,
    d_keep,
    d_send,
    resid,
    normed_ff,
    hidden,
    d_gate,
    d_linear,
    w_out,
    w_gate,
    w_up,
    w_down,
):
    rows, width = tokens_a.shape
    inner = w_gate.shape[1]
    shard_rows, down_rows = width // shards, inner // shards
    slab, half = inner // 2, width // 2
    tiles = slab // LANES
    block = 2 * tiles * shard_rows
    core, side = core_of(where), side_of(where)
    for index, shard in enumerate(shards_at(where[1], shards, far_first(shards))):
        upper, first = divmod(index, shards // 2)
        target = aligned(shard * shard_rows, shard_rows)
        for other, sources in enumerate(((part_0, part_1), (part_2, part_3))):
            part, start = sources[upper], first * block
            for t in range(tiles):
                lane = lanes_at((side ^ other) * slab + t * LANES, LANES)
                at = start + t * shard_rows
                w_gate[target, lane] = part[at : at + shard_rows, :]
                at = start + (tiles + t) * shard_rows
                w_up[target, lane] = part[at : at + shard_rows, :]
        rest, start = (rest_0, rest_1)[upper], first * (2 * down_rows + shard_rows)
        down = aligned(shard * down_rows, down_rows)
        w_down[down, :half] = rest[start : start + down_rows, :]
        w_down[down, half:] = rest[start + down_rows : start + 2 * down_rows, :]
        for other, sources in enumerate(((rest_0, rest_1), (rest_2, rest_3))):
            at = start + 2 * down_rows
            w_out[target, lanes_at((core ^ other) * half, half)] = sources[upper][
                at : at + shard_rows, :
            ]
    gain = gains[1:2, :]
    mine = mm(heads_mine[...], w_out[aligned(core * half, half), :])
    other = mm(heads_other[...], w_out[aligned((1 - core) * half, half), :])
    cotangents = (cotangent_a[...], pair_b[rows:, :])
    for stream, tokens in enumerate((tokens_a[...], pair_b[:rows, :])):
        span, back = slice(stream * rows, (stream + 1) * rows), slice((1 - stream) * rows, (2 - stream) * rows)
        value = tokens.astype(FULL) + (mine[span] + other[back])
        resid[span, :] = value
        normed_ff[span, :] = (value * inverse_rms(value) * gain).astype(LOW)
    for q in range(2):
        columns = slice(q * slab, (q + 1) * slab)
        for stream, cotangent in enumerate(cotangents):
            span = slice(stream * rows, (stream + 1) * rows)
            gate = mm(normed_ff[span, :], w_gate[:, columns])
            linear = mm(normed_ff[span, :], w_up[:, columns])
            d_hidden = mm_nt(cotangent, w_down[columns, :])
            square = gate * gate
            tanh = jnp.tanh(GELU_A * (gate + GELU_B * square * gate))
            rise = 0.5 * (1.0 + tanh)
            gelu = gate * rise
            slope = rise + 0.5 * gate * (1.0 - tanh * tanh) * (
                GELU_A * (1.0 + 3.0 * GELU_B * square)
            )
            hidden[span, columns] = (gelu * linear).astype(LOW)
            d_gate[span, columns] = (d_hidden * linear * slope).astype(LOW)
            d_linear[span, columns] = (d_hidden * gelu).astype(LOW)
    d_normed = mm_nt(d_gate[...], w_gate[...]) + mm_nt(d_linear[...], w_up[...])
    d_keep[...] = d_normed
    d_send[...] = d_normed.astype(LOW)
    out_keep[...] = resid[:rows, :] + mm(hidden[:rows, :], w_down[...])
    out_send[...] = mm(hidden[rows:, :], w_down[...]).astype(LOW)


def resid_grads_kernel(
    where,
    d_keep,
    d_other,
    resid,
    cotangent_a,
    pair_b,
    gains,
    w_out,
    d_resid,
    d_attn,
    d_heads,
    d_gain,
):
    rows, width = cotangent_a.shape
    half = width // 2
    for stream, cotangent in enumerate((cotangent_a[...], pair_b[rows:, :])):
        span, back = slice(stream * rows, (stream + 1) * rows), slice((1 - stream) * rows, (2 - stream) * rows)
        d_normed = d_keep[span, :] + d_other[back, :].astype(FULL)
        values = resid[span, :]
        scale = inverse_rms(values)
        grad = cotangent.astype(FULL) + norm_back(values, scale, gains[1:2, :], d_normed)
        d_attn[span, :] = grad.astype(LOW)
        if stream == 0:
            d_resid[...] = grad
            d_gain[...] = jnp.sum(d_normed * values * scale, axis=0, keepdims=True)
    d_heads[...] = mm_nt(d_attn[...], w_out[aligned(core_of(where) * half, half), :]).astype(LOW)


def wide_grads_kernel(shards, stages, where, normed_ff, grad, keep, send, whole):
    width, slab = normed_ff.shape[1], grad.shape[1] // 2
    shard_rows = width // shards
    for other in range(2):
        part = side_of(where) ^ other
        whole[other, :, :] = mm_tn(normed_ff[...], grad[:, lanes_at(part * slab, slab)]).astype(LOW)
    for place, (other, relative) in enumerate(places_of(stages, shards)):
        target = (keep, send)[place // shards]
        source = aligned((where[1] ^ relative) * shard_rows, shard_rows)
        for t in range(slab // LANES):
            target[place % shards, t * shard_rows : (t + 1) * shard_rows, :] = whole[
                other, source, t * LANES : (t + 1) * LANES
            ]


def down_grads_kernel(
    shards, stages, where, hidden, cotangent_a, pair_b, keep, send, whole
):
    inner, (rows, width) = hidden.shape[1], cotangent_a.shape
    slab, down_rows = inner // 2, inner // shards // 2
    for q in range(2):
        columns = slice(q * slab, (q + 1) * slab)
        whole[columns, :] = (
            mm_tn(hidden[:rows, columns], cotangent_a[...])
            + mm_tn(hidden[rows:, columns], pair_b[rows:, :])
        ).astype(LOW)
    for place, (other, relative) in enumerate(places_of(stages, shards)):
        target = (keep, send)[place // shards]
        part = side_of(where) ^ other
        source = aligned((where[1] ^ relative) * 2 * down_rows + part * down_rows, down_rows)
        for t in range(width // LANES):
            target[place % shards, t * down_rows : (t + 1) * down_rows, :] = whole[
                source, t * LANES : (t + 1) * LANES
            ]


def split_shards(shards, stages, where, whole, keep, send, by_tiles=False):
    shard_rows = whole.shape[0] // shards
    for place, (_, relative) in enumerate(places_of(stages, shards)):
        target = (keep, send)[place // (shards // 2)]
        source = aligned((where[1] ^ relative) * shard_rows, shard_rows)
        if by_tiles:
            for t in range(whole.shape[1] // LANES):
                target[place % (shards // 2), t * shard_rows : (t + 1) * shard_rows, :] = whole[
                    source, t * LANES : (t + 1) * LANES
                ]
        else:
            target[place % (shards // 2), :, :] = whole[source, :]


def score_grads(query, key, value, grad, offset, mask):
    scores = jnp.where(mask, mm_nt(query, key) + offset, NEG_FILL)
    expd = jnp.exp(scores - jnp.max(scores, axis=-1, keepdims=True))
    probs = expd * (1.0 / jnp.sum(expd, axis=-1, keepdims=True))
    d_probs = mm_nt(grad, value)
    weighted = jnp.sum(d_probs * probs, axis=-1, keepdims=True)
    d_scores = (probs * (d_probs - weighted)).astype(LOW)
    return (
        mm(d_scores, key),
        mm_tn(d_scores, query),
        mm_tn(probs.astype(LOW), grad),
        d_scores.astype(FULL),
    )


def fold_diagonals(flat):
    rows = flat.shape[0]
    folded = flat[:8, :]
    for base in range(8, rows, 8):
        folded = folded + pltpu.roll(flat[base : base + 8, :], 2 * rows - base, 1)
    return folded


def inside_grads_kernel(
    size,
    shards,
    stages,
    where,
    qkv,
    d_heads,
    heads_mine,
    heads_other,
    d_attn,
    row_starts,
    col_starts,
    bias,
    d_cols,
    d_bias,
    keep,
    send,
    d_out,
):
    rows, half = row_starts.shape[1], d_heads.shape[1]
    core = core_of(where)
    lane = lanes_at(core * half, half)
    value = mm_tn(heads_mine[...], d_attn[:, lane])
    d_out[aligned(core * half, half), :] = value.astype(LOW)
    value = mm_tn(heads_other[:rows, :], d_attn[rows:, lane])
    value = value + mm_tn(heads_other[rows:, :], d_attn[:rows, lane])
    d_out[aligned((1 - core) * half, half), :] = value.astype(LOW)
    split_shards(shards, stages, where, d_out, keep, send, by_tiles=True)
    masks, grads = [], []
    for stream in range(2):
        own_col = col_starts[:, 2 * stream : 2 * stream + 1]
        own_row = row_starts[3 * stream + 1 : 3 * stream + 2, :]
        settled = own_col != tail_of(row_starts, stream)
        masks.append((own_col == own_row) & settled)
        began = settled & (own_col >= ((where[0] ^ stream) * shards + where[1]) * rows)
        grad = d_heads[stream * rows : (stream + 1) * rows, :].astype(FULL)
        grads.append(jnp.where(began, grad, 0.0).astype(LOW))
    for pair in range(half // size // 2):
        outs = []
        for head in (2 * pair, 2 * pair + 1):
            near, _ = bias_tiles(bias[head : head + 1, :], rows)
            at = head * size
            flat = jnp.zeros((rows, rows), FULL)
            for stream in range(2):
                own = slice(2 * stream * rows, (2 * stream + 1) * rows)
                one = score_grads(
                    qkv[own, at : at + size],
                    qkv[own, half + at : half + at + size],
                    qkv[own, 2 * half + at : 2 * half + at + size],
                    grads[stream][:, at : at + size],
                    near,
                    masks[stream],
                )
                flat = flat + one[3]
                outs.append(one)
            flat = jnp.concatenate([flat, jnp.zeros((rows, rows), FULL)], axis=1)
            d_bias[8 * head : 8 * head + 8, :] = fold_diagonals(flat)
        for part in range(3):
            columns = slice(part * half + 2 * pair * size, part * half + (2 * pair + 2) * size)
            for stream in range(2):
                d_cols[stream * rows : (stream + 1) * rows, columns] = jnp.concatenate(
                    [outs[stream][part], outs[2 + stream][part]], axis=1
                ).astype(LOW)


def crossing_grads_kernel(
    shards,
    first_head,
    last_head,
    size,
    stages,
    where,
    qkv,
    normed,
    d_heads,
    d_after,
    d_inside,
    row_starts,
    col_starts,
    bias,
    d_cols,
    keep,
    send,
    d_bias,
    d_weights,
):
    rows, half = row_starts.shape[1], d_heads.shape[1]
    width = normed.shape[1]
    group = (last_head - first_head) * size
    span = slice(first_head * size, last_head * size)
    last_cols, masks, turns, mixes, grads = [], [], [], [], []
    for stream in range(2):
        tail = tail_of(row_starts, stream)
        own_col = col_starts[:, 2 * stream : 2 * stream + 1]
        after_col = col_starts[:, 2 * stream + 1 : 2 * stream + 2]
        own_row = row_starts[3 * stream + 1 : 3 * stream + 2, :]
        after_row = row_starts[3 * stream + 2 : 3 * stream + 3, :]
        is_last_col, is_last_row = own_col == tail, own_row == tail
        mix_col = jnp.where(is_last_col, own_col, after_col)
        mix_row = jnp.where(is_last_row, own_row, after_row)
        last_cols.append(is_last_col)
        masks.append((mix_col == tail) & (mix_row == tail))
        turns.append(is_last_col != is_last_row)
        base = 2 * stream * rows
        mix = []
        for part in range(3):
            columns = slice(part * half + first_head * size, part * half + last_head * size)
            mix.append(
                pick(
                    is_last_col,
                    qkv[base : base + rows, columns],
                    qkv[base + rows : base + 2 * rows, columns],
                )
            )
        mixes.append(mix)
        here = slice(stream * rows, (stream + 1) * rows)
        mixed = jnp.where(
            is_last_col, d_heads[here, span].astype(FULL), d_after[here, span].astype(FULL)
        )
        grads.append(jnp.where(mix_col == tail, mixed, 0.0).astype(LOW))
    for pair in range((last_head - first_head) // 2):
        outs = []
        for index in (2 * pair, 2 * pair + 1):
            head = first_head + index
            near, far = bias_tiles(bias[head : head + 1, :], rows)
            at = index * size
            kept, turned = jnp.zeros((rows, rows), FULL), jnp.zeros((rows, rows), FULL)
            for stream in range(2):
                mix = mixes[stream]
                two = score_grads(
                    mix[0][:, at : at + size],
                    mix[1][:, at : at + size],
                    mix[2][:, at : at + size],
                    grads[stream][:, at : at + size],
                    jnp.where(turns[stream], far, near),
                    masks[stream],
                )
                kept = kept + jnp.where(turns[stream], 0.0, two[3])
                turned = turned + jnp.where(turns[stream], two[3], 0.0)
                outs.append(two)
            d_bias[8 * index : 8 * index + 8, :] = fold_diagonals(
                jnp.concatenate([kept, turned], axis=1)
            )
        for part in range(3):
            columns = slice(part * group + 2 * pair * size, part * group + (2 * pair + 2) * size)
            for stream in range(2):
                d_cols[stream * rows : (stream + 1) * rows, columns] = jnp.concatenate(
                    [outs[stream][part], outs[2 + stream][part]], axis=1
                ).astype(LOW)
    total = [jnp.zeros((width, group), FULL) for _ in range(3)]
    for stream in range(2):
        base = 2 * stream * rows
        own, ahead = normed[base : base + rows, :], normed[base + rows : base + 2 * rows, :]
        normed_mix = pick(last_cols[stream], own, ahead)
        here = slice(stream * rows, (stream + 1) * rows)
        for part in range(3):
            inner = slice(part * half + first_head * size, part * half + last_head * size)
            total[part] = total[part] + mm_tn(own, d_inside[here, inner])
            total[part] = total[part] + mm_tn(
                normed_mix, d_cols[here, part * group : (part + 1) * group]
            )
    for part in range(3):
        d_weights[:, part * group : (part + 1) * group] = total[part].astype(LOW)
    split_shards(shards, stages, where, d_weights, keep, send)


def normed_grads_kernel(
    sizes, weights, d_inside, own_a, halo_a, pair_b, halo_b, row_starts, col_starts, *refs
):
    *crossing, keep, send, d_gain = refs
    rows, half = col_starts.shape[0], weights.shape[1] // 3
    inside = mm_nt(d_inside[...], weights[...])
    across = jnp.zeros(inside.shape, FULL)
    begin = 0
    for ref, group in zip(crossing, sizes, strict=True):
        for part in range(3):
            across = across + mm_nt(
                ref[:, part * group : (part + 1) * group],
                weights[:, part * half + begin : part * half + begin + group],
            )
        begin += group
    total = jnp.zeros((1, weights.shape[0]), FULL)
    streams = ((own_a, halo_a, keep), (pair_b, halo_b, send))
    for stream, (own, halo, target) in enumerate(streams):
        is_last = col_starts[:, 2 * stream : 2 * stream + 1] == tail_of(row_starts, stream)
        here = slice(stream * rows, (stream + 1) * rows)
        mine = jnp.where(is_last, across[here], inside[here])
        sent = jnp.where(is_last, 0.0, across[here])
        target[:rows, :] = mine.astype(target.dtype)
        target[rows:, :] = sent.astype(target.dtype)
        values, ahead = own[:rows, :].astype(FULL), halo[rows:, :].astype(FULL)
        share = mine * (values * inverse_rms(values)) + sent * (ahead * inverse_rms(ahead))
        total = total + jnp.sum(share, axis=0, keepdims=True)
    d_gain[...] = total


def tokens_kernel(own, gains, d_resid, d_own, d_before, out_keep, out_other, d_tokens, output):
    values = own[...].astype(FULL)
    grad = d_own[...] + d_before[...].astype(FULL)
    d_tokens[...] = d_resid[...] + norm_back(values, inverse_rms(values), gains[0:1, :], grad)
    output[...] = (out_keep[...] + out_other[...].astype(FULL)).astype(LOW)


def unpack_feed_kernel(tile_step, where, mine, other, d_gate, d_up, d_down, d_out):
    rows, half = d_out.shape[0], d_out.shape[1] // 2
    tiles, down_tiles = d_gate.shape[1] // (4 * LANES), d_down.shape[1] // LANES
    down_rows = d_down.shape[0] // 4
    begin = 0
    for relative in range(2):
        side = side_of(where) ^ relative
        for which, part in enumerate((mine, other)):
            core = core_of(where) ^ which
            at = begin
            target = aligned((2 * core + side) * down_rows, down_rows)
            for t in range(down_tiles):
                d_down[target, t * LANES : (t + 1) * LANES] = part[
                    at + t * down_rows : at + (t + 1) * down_rows, :
                ].astype(FULL)
            at += down_tiles * down_rows
            for matrix in (d_gate, d_up):
                for t in range(tiles):
                    lane = lanes_at(tile_step(core, side * tiles + t), LANES)
                    matrix[:, lane] = part[at + t * rows : at + (t + 1) * rows, :].astype(FULL)
                at += tiles * rows
        begin = at
    for which, part in enumerate((mine, other)):
        core = core_of(where) ^ which
        for t in range(half // LANES):
            first = begin + t * rows
            d_out[:, lanes_at(core * half + t * LANES, LANES)] = part[
                first : first + rows, :
            ].astype(FULL)


def unpack_attend_kernel(sizes, where, mine, other, d_query, d_key, d_value):
    half = d_query.shape[1] // 2
    for which, ref in enumerate((mine, other)):
        core = core_of(where) ^ which
        begin, column = 0, 0
        for group in sizes:
            for target in (d_query, d_key, d_value):
                target[:, lanes_at(core * half + begin, group)] = ref[
                    :, column : column + group
                ].astype(FULL)
                column += group
            begin += group


def shaped(shape, dtype):
    return jax.ShapeDtypeStruct(shape, dtype)


def per_device(
    tokens,
    cotangent,
    offsets,
    w_query,
    w_key,
    w_value,
    w_attn_out,
    w_gate,
    w_up,
    w_ff_out,
    gain_attn,
    gain_ff,
    rel_table,
):
    rows, width = tokens.shape
    shards = lax.axis_size("shard")
    shard, rep = lax.axis_index("shard"), lax.axis_index("rep")
    heads_count, table_rows = rel_table.shape[1], rel_table.shape[0]
    buckets = table_rows * shards
    shard_rows, inner = w_gate.shape
    half, size = width // 2, width // heads_count
    own_heads = heads_count // 2
    piece = w_ff_out.shape[0] // 2
    core = rep % 2
    where = jnp.stack([rep, shard]).astype(jnp.int32)

    starts_all = jnp.arange(offsets.shape[0], dtype=jnp.int32) - offsets
    start_pad = jnp.pad(starts_all, (rows, rows), constant_values=-1)
    first_a, first_b = (rep * shards + shard) * rows, ((rep ^ 1) * shards + shard) * rows
    window_a = lax.dynamic_slice_in_dim(start_pad, first_a, 3 * rows).reshape(3, rows)
    window_b = lax.dynamic_slice_in_dim(start_pad, first_b, 3 * rows).reshape(3, rows)
    row_starts = jnp.concatenate([window_a, window_b], axis=0)
    col_starts = jnp.stack([window_a[1], window_a[2], window_b[1], window_b[2]], axis=1)
    by_tiles = piece % LANES == 0

    def tile_step(which_core, tile):
        if by_tiles:
            per_shard = piece // LANES
            return ((tile // per_shard * 2 + which_core) * per_shard + tile % per_shard) * LANES
        return which_core * (inner // 2) + tile * LANES

    def by_core(matrix):
        if by_tiles:
            return matrix
        split = matrix.reshape(shard_rows, shards, 2, piece).transpose(0, 2, 1, 3)
        return split.reshape(shard_rows, inner)

    def from_core(matrix):
        if by_tiles:
            return matrix
        split = matrix.reshape(shard_rows, 2, shards, piece).transpose(0, 2, 1, 3)
        return split.reshape(shard_rows, inner)

    tiles = inner // (4 * LANES)
    down_block = width // LANES * (piece // 2)
    qkv_side = -(-3 * half // (2 * LANES)) * LANES
    steps = Sequence(jnp.zeros((8, LANES), FULL))
    qkv_own, ff_own, rest_own = steps.call(
        functools.partial(pack_kernel, tile_step),
        (where,),
        (
            w_query,
            w_key,
            w_value,
            w_attn_out,
            by_core(w_gate),
            by_core(w_up),
            w_ff_out,
            gain_attn.reshape(1, shard_rows),
            gain_ff.reshape(1, shard_rows),
            rel_table,
        ),
        (
            shaped((shard_rows + SMALL, qkv_side), LOW),
            shaped((2 * tiles * shard_rows, LANES), LOW),
            shaped((2 * piece + shard_rows, half), LOW),
        ),
    )
    onehot = np.zeros((shards, SMALL, 2 * rows), np.float32)
    onehot[:, 2 : 2 + table_rows] = bucket_onehot(2 * rows, buckets).T.reshape(
        shards, table_rows, 2 * rows
    )
    onehot = jnp.asarray(onehot.reshape(shards * SMALL, 2 * rows), LOW)


    up = [(i, i + 1) for i in range(shards - 1)]
    down = [(i + 1, i) for i in range(shards - 1)]
    by_x, by_core = (("rep", 1),), ("rep", 0)
    far, near = far_first(shards), near_first(shards)

    def joined(*parts, axis=0):
        return jnp.concatenate(parts, axis=axis)

    pair = joined(tokens, cotangent)
    received, pair_b = swap(qkv_own, "shard", far[0]), swap(pair, *by_core)
    steps.mark(qkv_own, pair)
    shifted = steps.take(tokens)
    before, ahead = lax.ppermute(shifted, "shard", up), lax.ppermute(shifted, "shard", down)
    qkv_near = joined(qkv_own, steps.take(received))
    pair_b = steps.take(pair_b)
    ff_received = swap(steps.take(ff_own), "shard", far[0])
    for bit in far[1:-1]:
        received = swap(qkv_near, "shard", bit)
        steps.mark(qkv_near)
        qkv_near = joined(qkv_near, steps.take(received))
    qkv_far, qkv_side = swap(qkv_near, "shard", far[-1]), swap(qkv_near, *by_x[0])
    steps.mark(qkv_near)
    halo = joined(steps.take(before), steps.take(ahead))
    ff_near = joined(ff_own, steps.take(ff_received))
    ff_received, halo_b = swap(ff_near, "shard", far[1]), swap(halo, *by_core)
    rest_received = swap(steps.take(rest_own), "shard", far[0])
    steps.mark(ff_near, halo)
    qkv_far, halo_b = steps.take(qkv_far), steps.take(halo_b)
    qkv_other = swap(qkv_far, *by_x[0])
    steps.mark(qkv_far)
    qkv_side = steps.take(qkv_side)
    ff_near = joined(ff_near, steps.take(ff_received))
    rest_near = rest_own
    for first, bit in zip(far[1:-1], far[2:-1]):
        ff_received = swap(ff_near, "shard", bit)
        rest_near = joined(rest_near, steps.take(rest_received))
        rest_received = swap(rest_near, "shard", first)
        steps.mark(ff_near, rest_near)
        ff_near = joined(ff_near, steps.take(ff_received))
    ff_far, ff_side = swap(ff_near, "shard", far[-1]), swap(ff_near, *by_x[0])
    steps.mark(ff_near)
    rest_near = joined(rest_near, steps.take(rest_received))
    rest_received = swap(rest_near, "shard", far[-2])
    steps.mark(rest_near)
    qkv_other = steps.take(qkv_other)
    heads, normed, qkv, w_qkv, gains, bias = steps.call(
        functools.partial(attend_kernel, shards, size),
        (where,),
        (
            tokens,
            halo,
            pair_b,
            halo_b,
            qkv_near,
            qkv_far,
            qkv_side,
            qkv_other,
            row_starts,
            col_starts,
            onehot,
        ),
        (
            shaped((2 * rows, half), LOW),
            shaped((4 * rows, width), LOW),
            shaped((4 * rows, 3 * half), LOW),
            shaped((width, 3 * half), LOW),
            shaped((SMALL, width), FULL),
            shaped((8, 2 * rows), FULL),
        ),
        [pltpu.VMEM((rows, 2 * half), LOW), pltpu.VMEM((shards * SMALL, LANES), FULL)],
        micros=400,
    )
    heads_other = swap(heads, *by_core)
    rest_near = joined(rest_near, steps.take(rest_received))
    rest_far = swap(rest_near, "shard", far[-1])
    ff_far, ff_side = steps.take(ff_far), steps.take(ff_side)
    ff_other, rest_near_b = swap(steps.take(ff_far), *by_x[0]), swap(rest_near, *by_core)
    steps.mark(rest_near, ff_far, ff_side)
    heads_other, rest_near_b = steps.take(heads_other), steps.take(rest_near_b)
    rest_far = steps.take(rest_far)
    rest_far_b = swap(rest_far, *by_core)
    steps.mark(rest_far)
    ff_other, rest_far_b = steps.take(ff_other), steps.take(rest_far_b)
    wide = shaped((2 * rows, inner // 2), LOW)
    (
        out_keep,
        out_send,
        d_normed_keep,
        d_normed_send,
        resid,
        normed_ff,
        hidden,
        d_gate,
        d_linear,
        w_out,
    ) = steps.call(
        functools.partial(feed_kernel, shards),
        (where,),
        (
            heads,
            heads_other,
            tokens,
            cotangent,
            pair_b,
            gains,
            rest_near,
            rest_far,
            rest_near_b,
            rest_far_b,
            ff_near,
            ff_far,
            ff_side,
            ff_other,
        ),
        (
            shaped((rows, width), FULL),
            shaped((rows, width), LOW),
            shaped((2 * rows, width), FULL),
            shaped((2 * rows, width), LOW),
            shaped((2 * rows, width), FULL),
            shaped((2 * rows, width), LOW),
            wide,
            wide,
            wide,
            shaped((width, width), LOW),
        ),
        [
            pltpu.VMEM((width, inner // 2), LOW),
            pltpu.VMEM((width, inner // 2), LOW),
            pltpu.VMEM((inner // 2, width), LOW),
        ],
        micros=400,
    )
    d_normed_other, out_other = swap(d_normed_send, *by_core), swap(out_send, *by_core)
    slices = shaped((shards, tiles * shard_rows, LANES), LOW)
    down_slices = shaped((shards, down_block, LANES), LOW)
    by_near = tuple(("shard", bit) for bit in near)
    down_stages = by_x + by_near
    gate_stages = by_near[:1] + by_x + by_near[1:]
    up_stages = by_near[1:2] + by_x + by_near[:1] + by_near[2:]
    down_keep, down_send = steps.call(
        functools.partial(down_grads_kernel, shards, down_stages),
        (where,),
        (hidden, cotangent, pair_b),
        (down_slices, down_slices),
        [pltpu.VMEM((inner // 2, width), LOW)],
        micros=4,
    )
    down_received = exchange(down_send, down_stages[0])
    d_normed_other, out_other = steps.take(d_normed_other), steps.take(out_other)
    d_resid, d_attn, d_heads, d_gain_two = steps.call(
        resid_grads_kernel,
        (where,),
        (d_normed_keep, d_normed_other, resid, cotangent, pair_b, gains, w_out),
        (
            shaped((rows, width), FULL),
            shaped((2 * rows, width), LOW),
            shaped((2 * rows, half), LOW),
            shaped((1, width), FULL),
        ),
        micros=5,
    )
    d_heads_after = lax.ppermute(d_heads, "shard", down)
    gate_keep, gate_send = steps.call(
        functools.partial(wide_grads_kernel, shards, gate_stages),
        (where,),
        (normed_ff, d_gate),
        (slices, slices),
        [pltpu.VMEM((2, width, inner // 4), LOW)],
        micros=4,
    )
    gate_received = exchange(gate_send, gate_stages[0])
    up_keep, up_send = steps.call(
        functools.partial(wide_grads_kernel, shards, up_stages),
        (where,),
        (normed_ff, d_linear),
        (slices, slices),
        [pltpu.VMEM((2, width, inner // 4), LOW)],
        micros=4,
    )
    up_received = exchange(up_send, up_stages[0])
    out_slices = shaped((shards // 2, shard_rows * half // LANES, LANES), LOW)
    d_inside, d_bias, o_keep, o_send = steps.call(
        functools.partial(inside_grads_kernel, size, shards, by_near),
        (where,),
        (qkv, d_heads, heads, heads_other, d_attn, row_starts, col_starts, bias),
        (
            shaped((2 * rows, 3 * half), LOW),
            shaped((8 * own_heads, 2 * rows), FULL),
            out_slices,
            out_slices,
        ),
        [pltpu.VMEM((width, half), LOW)],
        micros=11,
    )

    d_down, down_received = send_half(steps.add(down_keep, down_received), down_stages[1])
    o_received = exchange(o_send, by_near[0])
    d_heads_after = steps.take(d_heads_after)
    sizes = [count * size for count in GROUPS]

    def crossing_grads(first, count):
        attn_slices = shaped((shards // 2, shard_rows, 3 * count * size), LOW)
        return steps.call(
            functools.partial(
                crossing_grads_kernel, shards, first, first + count, size, by_near
            ),
            (where,),
            (qkv, normed, d_heads, d_heads_after, d_inside, row_starts, col_starts, bias),
            (
                shaped((2 * rows, 3 * count * size), LOW),
                attn_slices,
                attn_slices,
                shaped((8 * count, 2 * rows), FULL),
            ),
            [pltpu.VMEM((width, 3 * count * size), LOW)],
            micros=12 if not first else 400,
        )

    cols_one, one_keep, one_send, d_bias_one = crossing_grads(0, GROUPS[0])
    one_received = exchange(one_send, by_near[0])
    d_gate, gate_received = send_half(steps.add(gate_keep, gate_received), gate_stages[1])
    d_up, up_received = send_half(steps.add(up_keep, up_received), up_stages[1])
    d_down, down_received = send_half(steps.add(d_down, down_received), down_stages[2])
    cols_two, two_keep, two_send, d_bias_two = crossing_grads(GROUPS[0], GROUPS[1])
    d_out = steps.add(o_keep, o_received)
    two_received = exchange(two_send, by_near[0])
    d_gate = joined(steps.add(d_gate, gate_received), d_out, axis=1)
    d_gate, gate_received = send_half(d_gate, by_near[1])
    d_down, down_received = send_half(steps.add(d_down, down_received), down_stages[3])
    keep, send, d_gain_one = steps.call(
        functools.partial(normed_grads_kernel, tuple(sizes)),
        (),
        (
            w_qkv,
            d_inside,
            tokens,
            halo,
            pair_b,
            halo_b,
            row_starts,
            col_starts,
            cols_one,
            cols_two,
        ),
        (
            shaped((2 * rows, width), FULL),
            shaped((2 * rows, width), LOW),
            shaped((1, width), FULL),
        ),
        micros=400,
    )
    d_own_received = exchange(send, by_core)
    attn = joined(
        steps.add(one_keep, one_received), steps.add(two_keep, two_received), axis=2
    )
    attn, attn_received = send_half(attn, by_near[1])
    d_own = keep + steps.take(d_own_received).astype(FULL)
    d_before = lax.ppermute(d_own[rows:].astype(LOW), "shard", up)
    folds = np.stack([np.roll(bucket_onehot(2 * rows, buckets), row, axis=0) for row in range(8)])
    d_bias = d_bias + jnp.concatenate([d_bias_one, d_bias_two], axis=0)
    d_bias = d_bias.reshape(own_heads, 16 * rows)
    d_table = lax.dot_general(
        d_bias,
        jnp.asarray(folds.reshape(16 * rows, buckets)),
        (((1,), (0,)), ((), ())),
        precision=lax.Precision.HIGHEST,
    )
    d_table = lax.dynamic_update_slice(
        jnp.zeros((heads_count, buckets), FULL), d_table, (core * own_heads, 0)
    ).T
    smalls = jnp.concatenate([d_gain_one.reshape(-1), d_gain_two.reshape(-1), d_table.reshape(-1)])
    rest = -smalls.shape[0] % (8 * LANES)
    smalls = jnp.pad(smalls, (0, rest)).reshape(-1, LANES)
    small_stages = [("rep", bit) for bit in range(bits_of(lax.axis_size("rep")))] + list(by_near)

    def more_smalls(count):
        total = smalls
        for _ in range(count):
            if small_stages:
                total = total + steps.take(exchange(total, small_stages.pop(0)))
        return total

    smalls = more_smalls(1)
    d_up, up_received = send_half(steps.add(d_up, up_received), up_stages[2])
    d_gate, gate_received = send_half(steps.add(d_gate, gate_received), by_near[2])
    d_down = steps.add(d_down, down_received)
    smalls = more_smalls(1)
    attn, attn_received = send_half(steps.add(attn, attn_received), by_near[2])
    d_up, up_received = send_half(steps.add(d_up, up_received), up_stages[3])
    d_gate = steps.add(d_gate, gate_received)
    smalls = more_smalls(1)
    attn = steps.add(attn, attn_received)
    d_up = steps.add(d_up, up_received)
    for stage in by_near[3:]:
        attn, attn_received = send_half(attn, stage)
        attn = steps.add(attn, attn_received)
        d_up, up_received = send_half(d_up, stage)
        d_up = steps.add(d_up, up_received)
        d_gate, gate_received = send_half(d_gate, stage)
        d_gate = steps.add(d_gate, gate_received)
        d_down, down_received = send_half(d_down, stage)
        d_down = steps.add(d_down, down_received)
    wide = tiles * shard_rows
    attn, d_feed = attn[0], jnp.concatenate([d_down[0], d_gate[0, :wide], d_up[0]], axis=0)
    d_out = d_gate[0, wide:]
    for bit in range(2, bits_of(lax.axis_size("rep"))):
        attn = steps.add(attn, exchange(attn, ("rep", bit)))
        d_feed = steps.add(d_feed, exchange(d_feed, ("rep", bit)))
        d_out = steps.add(d_out, exchange(d_out, ("rep", bit)))
    attn_received = exchange(attn, by_x[0])
    feed_received = exchange(jnp.concatenate([d_feed, d_out], axis=0), by_x[0])
    smalls = more_smalls(1)
    attn = steps.add(attn, attn_received)
    attn_other = exchange(attn, by_core)
    feed_received = steps.take(feed_received)
    feed = d_feed.shape[0]
    d_feed = jnp.concatenate(
        [d_feed, feed_received[:feed], add_low(d_out, feed_received[feed:])], axis=0
    )
    feed_other = exchange(d_feed, by_core)
    smalls = more_smalls(len(small_stages)).reshape(-1)
    d_tokens, output = steps.call(
        tokens_kernel,
        (),
        (tokens, gains, d_resid, d_own[:rows], steps.take(d_before), out_keep, out_other),
        (shaped((rows, width), FULL), shaped((rows, width), LOW)),
    )

    def own_part(begin, length):
        return lax.dynamic_slice_in_dim(smalls, begin + shard * length, length)

    d_w_query, d_w_key, d_w_value = steps.call(
        functools.partial(unpack_attend_kernel, tuple(sizes)),
        (where,),
        (attn, attn_other),
        (shaped(w_query.shape, FULL),) * 3,
    )
    d_w_gate, d_w_up, d_w_ff_out, d_w_attn_out = steps.call(
        functools.partial(unpack_feed_kernel, tile_step),
        (where,),
        (d_feed, feed_other),
        (
            shaped(w_gate.shape, FULL),
            shaped(w_up.shape, FULL),
            shaped(w_ff_out.shape, FULL),
            shaped(w_attn_out.shape, FULL),
        ),
    )
    return (
        output,
        d_tokens,
        d_w_query,
        d_w_key,
        d_w_value,
        d_w_attn_out,
        from_core(d_w_gate),
        from_core(d_w_up),
        d_w_ff_out,
        own_part(0, shard_rows),
        own_part(width, shard_rows),
        own_part(2 * width, table_rows * heads_count).reshape(table_rows, heads_count),
    )


def solution(mesh):
    tokens_spec, rows_spec, line_spec = P(("rep", "shard"), None), P("shard", None), P("shard")
    return jax.shard_map(
        per_device,
        mesh=mesh,
        in_specs=(tokens_spec, tokens_spec, P()) + (rows_spec,) * 7 + (line_spec,) * 2 + (rows_spec,),
        out_specs=(tokens_spec,) * 2 + (rows_spec,) * 7 + (line_spec,) * 2 + (rows_spec,),
        check_vma=False,
    )
```

```python
import functools

import jax
import jax.numpy as jnp
import numpy as np
from jax import lax
from jax.experimental import pallas as pl
from jax.experimental.pallas import tpu as pltpu
from jax.sharding import PartitionSpec as P

NEG_FILL = -1e30
EPSILON = 1e-06
BORDERS = (1, 2, 3, 4, 5, 6, 7, 8, 12, 16, 23, 32, 46, 64, 91)
LANES = 128
SMALL = 8
SCALE = 2 * 10**8
GROUPS = (4, 2)
LOW = jnp.bfloat16
FULL = jnp.float32
GELU_A = float(np.sqrt(2.0 / np.pi))
GELU_B = 0.044715


def bits_of(count):
    return count.bit_length() - 1


def swap(block, axis, bit):
    count = lax.axis_size(axis)
    return lax.ppermute(block, axis, [(i, i ^ (1 << bit)) for i in range(count)])


def add_low(left, right):
    return (left.astype(FULL) + right.astype(FULL)).astype(LOW)


def gather_shards(block):
    for bit in far_first(lax.axis_size("shard")):
        block = jnp.concatenate([block, swap(block, "shard", bit)], axis=0)
    return block


def reverse_bits(value, count):
    result = 0
    for bit in range(bits_of(count)):
        result = result | (((value >> bit) & 1) << (bits_of(count) - 1 - bit))
    return result


def far_first(shards):
    return tuple(reversed(range(bits_of(shards))))


def near_first(shards):
    return tuple(range(bits_of(shards)))


def shards_at(shard, shards, order):
    places = []
    for place in range(shards):
        moved = sum(((place >> step) & 1) << bit for step, bit in enumerate(order))
        places.append(shard ^ moved)
    return places


def exchange(block, stage):
    return swap(block, *stage)


def places_of(stages, shards):
    places = []
    for place in range(2 ** len(stages)):
        side, shard = 0, 0
        for step, (axis, bit) in enumerate(stages):
            here = (place >> (len(stages) - 1 - step)) & 1
            if axis == "rep":
                side |= here
            else:
                shard |= here << bit
        places.append((side, shard))
    return places


def mark_kernel():
    pass


class Sequence:
    def __init__(self, token):
        self.token, self.sent = token, []

    def send(self, block, stage):
        self.sent.append(block)
        return exchange(block, stage)

    def send_half(self, blocks, stage):
        kept, sent = halves_of(blocks)
        return kept, self.send(sent, stage)

    def take(self, received):
        received, self.token = lax.optimization_barrier((received, self.token))
        return received

    def add(self, kept, received):
        return add_low(kept, self.take(received))

    def mark(self, *ready, micros=500):
        self.call(None, (), (), (), waits=ready, micros=micros)

    def call(self, kernel, scalars, arrays, outs, scratch=(), micros=3, waits=(), room=4):
        held = [(a.size, a.dtype) for a in (*arrays, *outs)]
        held += [(int(np.prod(a.shape)), a.dtype) for a in scratch]
        needed = sum(size * jnp.dtype(dtype).itemsize for size, dtype in held)
        waits, self.sent = (*waits, *self.sent), []
        skip, given = 1 + len(waits), 1 + len(waits) + len(scalars) + len(arrays) + len(outs)

        def body(*refs):
            if kernel is not None:
                kernel(*refs[skip:given], *refs[given + 1 :])

        def placed(arrays, space):
            return [pl.BlockSpec(memory_space=space) for _ in arrays]

        *results, self.token = pl.pallas_call(
            body,
            out_shape=(*outs, shaped(self.token.shape, self.token.dtype)),
            in_specs=placed((self.token, *waits), pl.ANY)
            + placed(scalars, pltpu.SMEM)
            + placed(arrays, pltpu.VMEM),
            out_specs=(*placed(outs, pltpu.VMEM), pl.BlockSpec(memory_space=pl.ANY)),
            scratch_shapes=scratch,
            input_output_aliases={0: len(outs)},
            compiler_params=pltpu.CompilerParams(vmem_limit_bytes=min(needed + room * 2**20, 58 * 2**20)),
            cost_estimate=pl.CostEstimate(
                flops=int(micros * SCALE), bytes_accessed=10**6, transcendentals=0
            ),
            name=getattr(kernel, "func", kernel or mark_kernel).__name__,
        )(self.token, *waits, *scalars, *arrays)
        return results


def halves_of(blocks):
    half = blocks.shape[0] // 2
    return blocks[:half], blocks[half:]


def sum_replicas(block, first_bit):
    for bit in range(first_bit, bits_of(lax.axis_size("rep"))):
        block = add_low(block, swap(block, "rep", bit))
    return block


def bucket_onehot(period, buckets):
    index = np.arange(period)
    relative = np.where(index < period // 2, index, index - period)
    distance = np.abs(relative)
    bucket = buckets // 2 * (relative > 0).astype(np.int64)
    for border in BORDERS:
        bucket = bucket + (distance >= border).astype(np.int64)
    return (bucket[:, None] == np.arange(buckets)[None, :]).astype(np.float32)


def mm(left, right):
    return lax.dot_general(left, right, (((1,), (0,)), ((), ())), preferred_element_type=FULL)


def mm_nt(left, right):
    return lax.dot_general(left, right, (((1,), (1,)), ((), ())), preferred_element_type=FULL)


def mm_tn(left, right):
    return lax.dot_general(left, right, (((0,), (0,)), ((), ())), preferred_element_type=FULL)


def inverse_rms(values):
    return lax.rsqrt(jnp.mean(values * values, axis=-1, keepdims=True) + EPSILON)


def norm_back(values, scale, gain, grad):
    inner = jnp.mean(gain * grad * values, axis=-1, keepdims=True)
    return scale * gain * grad - values * (scale * scale * scale * inner)


def pick(mask, left, right):
    return jnp.where(mask, left.astype(FULL), right.astype(FULL)).astype(left.dtype)


def aligned(index, size):
    return pl.ds(pl.multiple_of(index, 8), size)


def lanes_at(index, size):
    return pl.ds(pl.multiple_of(index, LANES), size)


def bias_tiles(bias_row, rows):
    rolled = pltpu.roll(
        jnp.broadcast_to(bias_row, (rows, 2 * rows)), 0, 1, stride=1, stride_axis=0
    )
    return rolled[:, :rows], rolled[:, rows:]


def core_of(where):
    return where[0] & 1


def side_of(where):
    return (where[0] >> 1) & 1


def tail_of(row_starts, stream):
    rows = row_starts.shape[1]
    return row_starts[3 * stream + 1 : 3 * stream + 2, rows - 1 : rows]


def pack_kernel(
    tile_step,
    where,
    w_query,
    w_key,
    w_value,
    w_out,
    w_gate,
    w_up,
    w_down,
    gain_one,
    gain_two,
    table,
    qkv,
    feed,
    rest,
):
    core, side = core_of(where), side_of(where)
    rows, half = w_query.shape[0], w_query.shape[1] // 2
    tiles = w_gate.shape[1] // (4 * LANES)
    width = qkv.shape[1]
    qkv[rows:, :] = jnp.zeros((SMALL, width), LOW)
    for which in range(2):

        @pl.when(side == which)
        def _():
            for t in range(width // LANES):
                part, tile = divmod(which * (3 * half - width) // LANES + t, half // LANES)
                qkv[:rows, t * LANES : (t + 1) * LANES] = (w_query, w_key, w_value)[part][
                    :, lanes_at(core * half + tile * LANES, LANES)
                ]

    qkv[rows : rows + 1, :rows] = gain_one[...]
    qkv[rows + 1 : rows + 2, :rows] = gain_two[...]
    qkv[rows + 2 : rows + 2 + table.shape[0], : table.shape[1]] = table[...]
    for which, ref in enumerate((w_gate, w_up)):
        for t in range(tiles):
            lane = tile_step(core, side * tiles + t)
            first = (which * tiles + t) * rows
            feed[first : first + rows, :] = ref[:, lanes_at(lane, LANES)]
    down_rows = w_down.shape[0] // 2
    own = aligned(core * down_rows, down_rows)
    rest[:down_rows, :] = w_down[own, :half]
    rest[down_rows : 2 * down_rows, :] = w_down[own, half:]
    rest[2 * down_rows :, :] = w_out[:, lanes_at(core * half, half)]


def attend_kernel(
    shards,
    size,
    where,
    own_a,
    halo_a,
    pair_b,
    halo_b,
    part_0,
    part_1,
    part_2,
    part_3,
    row_starts,
    col_starts,
    onehot,
    heads,
    normed,
    qkv,
    weights,
    gains,
    bias,
    kv_before,
    smalls,
):
    rows, width = own_a.shape
    shard_rows, half = width // shards, weights.shape[1] // 3
    block = shard_rows + SMALL
    for index, shard in enumerate(shards_at(where[1], shards, far_first(shards))):
        upper, first = index // (shards // 2), index % (shards // 2) * block
        for other, sources in enumerate(((part_0, part_1), (part_2, part_3))):
            source = sources[upper]
            lane = (side_of(where) ^ other) * (weights.shape[1] - source.shape[1])
            weights[
                aligned(shard * shard_rows, shard_rows), lanes_at(lane, source.shape[1])
            ] = source[first : first + shard_rows, :]
        source = (part_0, part_1)[upper]
        smalls[aligned(shard * SMALL, SMALL), :] = source[
            first + shard_rows : first + block, :LANES
        ].astype(FULL)
    total = jnp.zeros((SMALL, width), FULL)
    for shard in range(shards):
        line = jnp.concatenate(
            [
                smalls[shard * SMALL : (shard + 1) * SMALL, :],
                jnp.zeros((SMALL, width - LANES), FULL),
            ],
            axis=1,
        )
        total = total + (pltpu.roll(line, shard * shard_rows, 1) if shard else line)
    gains[...] = total
    gain = total[0:1, :]
    heads_here = half // size
    shift = jnp.where(core_of(where) == 0, 0, LANES - heads_here)
    table = pltpu.roll(smalls[...], shift, 1).astype(LOW)
    bias[...] = mm_tn(table, onehot[...])[: bias.shape[0], :]
    for stream, (own_ref, halo) in enumerate(((own_a, halo_a), (pair_b, halo_b))):
        base = 2 * stream * rows
        lines = []
        for tokens in (halo[:rows, :], own_ref[:rows, :], halo[rows:, :]):
            values = tokens.astype(FULL)
            lines.append((values * inverse_rms(values) * gain).astype(LOW))
        normed[base : base + rows, :] = lines[1]
        normed[base + rows : base + 2 * rows, :] = lines[2]
        for part in range(3):
            columns = slice(part * half, (part + 1) * half)
            qkv[base : base + 2 * rows, columns] = mm(
                normed[base : base + 2 * rows, :], weights[:, columns]
            ).astype(LOW)
            if part:
                kv_before[:, (part - 1) * half : part * half] = mm(
                    lines[0], weights[:, columns]
                ).astype(LOW)
        own_col = col_starts[:, 2 * stream : 2 * stream + 1]
        in_before = own_col == row_starts[3 * stream : 3 * stream + 1, :]
        in_own = own_col == row_starts[3 * stream + 1 : 3 * stream + 2, :]
        in_after = own_col == row_starts[3 * stream + 2 : 3 * stream + 3, :]
        allowed = in_own | in_before | in_after
        own, ahead = slice(base, base + rows), slice(base + rows, base + 2 * rows)
        for pair in range(half // size // 2):
            mixed = []
            for head in (2 * pair, 2 * pair + 1):
                at = head * size
                query = qkv[own, at : at + size]
                keys = slice(half + at, half + at + size)
                values = slice(2 * half + at, 2 * half + at + size)
                near, far = bias_tiles(bias[head : head + 1, :], rows)
                scores = jnp.where(
                    in_own,
                    mm_nt(query, qkv[own, keys]) + near,
                    jnp.where(
                        in_before,
                        mm_nt(query, kv_before[:, at : at + size]),
                        mm_nt(query, qkv[ahead, keys]),
                    )
                    + far,
                )
                scores = jnp.where(allowed, scores, NEG_FILL)
                expd = jnp.exp(scores - jnp.max(scores, axis=-1, keepdims=True))
                probs = expd * (1.0 / jnp.sum(expd, axis=-1, keepdims=True))
                total = mm(jnp.where(in_own, probs, 0.0).astype(LOW), qkv[own, values])
                total = total + mm(
                    jnp.where(in_before, probs, 0.0).astype(LOW),
                    kv_before[:, half + at : half + at + size],
                )
                total = total + mm(
                    jnp.where(in_after, probs, 0.0).astype(LOW), qkv[ahead, values]
                )
                mixed.append(total)
            heads[stream * rows : (stream + 1) * rows, 2 * pair * size : (2 * pair + 2) * size] = (
                jnp.concatenate(mixed, axis=1).astype(LOW)
            )


def feed_kernel(
    shards,
    where,
    heads_mine,
    heads_other,
    tokens_a,
    cotangent_a,
    pair_b,
    gains,
    rest_0,
    rest_1,
    rest_2,
    rest_3,
    part_0,
    part_1,
    part_2,
    part_3,
    out_keep,
    out_send,
    d_keep,
    d_send,
    resid,
    normed_ff,
    hidden,
    d_gate,
    d_linear,
    w_out,
    w_gate,
    w_up,
    w_down,
):
    rows, width = tokens_a.shape
    inner = w_gate.shape[1]
    shard_rows, down_rows = width // shards, inner // shards
    slab, half = inner // 2, width // 2
    tiles = slab // LANES
    block = 2 * tiles * shard_rows
    core, side = core_of(where), side_of(where)
    for index, shard in enumerate(shards_at(where[1], shards, far_first(shards))):
        upper, first = divmod(index, shards // 2)
        target = aligned(shard * shard_rows, shard_rows)
        for other, sources in enumerate(((part_0, part_1), (part_2, part_3))):
            part, start = sources[upper], first * block
            for t in range(tiles):
                lane = lanes_at((side ^ other) * slab + t * LANES, LANES)
                at = start + t * shard_rows
                w_gate[target, lane] = part[at : at + shard_rows, :]
                at = start + (tiles + t) * shard_rows
                w_up[target, lane] = part[at : at + shard_rows, :]
        rest, start = (rest_0, rest_1)[upper], first * (2 * down_rows + shard_rows)
        down = aligned(shard * down_rows, down_rows)
        w_down[down, :half] = rest[start : start + down_rows, :]
        w_down[down, half:] = rest[start + down_rows : start + 2 * down_rows, :]
        for other, sources in enumerate(((rest_0, rest_1), (rest_2, rest_3))):
            at = start + 2 * down_rows
            w_out[target, lanes_at((core ^ other) * half, half)] = sources[upper][
                at : at + shard_rows, :
            ]
    gain = gains[1:2, :]
    mine = mm(heads_mine[...], w_out[aligned(core * half, half), :])
    other = mm(heads_other[...], w_out[aligned((1 - core) * half, half), :])
    cotangents = (cotangent_a[...], pair_b[rows:, :])
    for stream, tokens in enumerate((tokens_a[...], pair_b[:rows, :])):
        span, back = slice(stream * rows, (stream + 1) * rows), slice((1 - stream) * rows, (2 - stream) * rows)
        value = tokens.astype(FULL) + (mine[span] + other[back])
        resid[span, :] = value
        normed_ff[span, :] = (value * inverse_rms(value) * gain).astype(LOW)
    for q in range(2):
        columns = slice(q * slab, (q + 1) * slab)
        for stream, cotangent in enumerate(cotangents):
            span = slice(stream * rows, (stream + 1) * rows)
            gate = mm(normed_ff[span, :], w_gate[:, columns])
            linear = mm(normed_ff[span, :], w_up[:, columns])
            d_hidden = mm_nt(cotangent, w_down[columns, :])
            square = gate * gate
            tanh = jnp.tanh(GELU_A * (gate + GELU_B * square * gate))
            rise = 0.5 * (1.0 + tanh)
            gelu = gate * rise
            slope = rise + 0.5 * gate * (1.0 - tanh * tanh) * (
                GELU_A * (1.0 + 3.0 * GELU_B * square)
            )
            hidden[span, columns] = (gelu * linear).astype(LOW)
            d_gate[span, columns] = (d_hidden * linear * slope).astype(LOW)
            d_linear[span, columns] = (d_hidden * gelu).astype(LOW)
    d_normed = mm_nt(d_gate[...], w_gate[...]) + mm_nt(d_linear[...], w_up[...])
    d_keep[...] = d_normed
    d_send[...] = d_normed.astype(LOW)
    out_keep[...] = resid[:rows, :] + mm(hidden[:rows, :], w_down[...])
    out_send[...] = mm(hidden[rows:, :], w_down[...]).astype(LOW)


def resid_grads_kernel(
    where,
    d_keep,
    d_other,
    resid,
    cotangent_a,
    pair_b,
    gains,
    w_out,
    d_resid,
    d_attn,
    d_heads,
    d_gain,
):
    rows, width = cotangent_a.shape
    half = width // 2
    for stream, cotangent in enumerate((cotangent_a[...], pair_b[rows:, :])):
        span, back = slice(stream * rows, (stream + 1) * rows), slice((1 - stream) * rows, (2 - stream) * rows)
        d_normed = d_keep[span, :] + d_other[back, :].astype(FULL)
        values = resid[span, :]
        scale = inverse_rms(values)
        grad = cotangent.astype(FULL) + norm_back(values, scale, gains[1:2, :], d_normed)
        d_attn[span, :] = grad.astype(LOW)
        if stream == 0:
            d_resid[...] = grad
            d_gain[...] = jnp.sum(d_normed * values * scale, axis=0, keepdims=True)
    d_heads[...] = mm_nt(d_attn[...], w_out[aligned(core_of(where) * half, half), :]).astype(LOW)


def wide_grads_kernel(shards, stages, where, normed_ff, grad, keep, send, whole):
    width, slab = normed_ff.shape[1], grad.shape[1] // 2
    shard_rows = width // shards
    for other in range(2):
        part = side_of(where) ^ other
        whole[other, :, :] = mm_tn(normed_ff[...], grad[:, lanes_at(part * slab, slab)]).astype(LOW)
    for place, (other, relative) in enumerate(places_of(stages, shards)):
        target = (keep, send)[place // shards]
        source = aligned((where[1] ^ relative) * shard_rows, shard_rows)
        for t in range(slab // LANES):
            target[place % shards, t * shard_rows : (t + 1) * shard_rows, :] = whole[
                other, source, t * LANES : (t + 1) * LANES
            ]


def down_grads_kernel(
    shards, stages, where, hidden, cotangent_a, pair_b, keep, send, whole
):
    inner, (rows, width) = hidden.shape[1], cotangent_a.shape
    slab, down_rows = inner // 2, inner // shards // 2
    for q in range(2):
        columns = slice(q * slab, (q + 1) * slab)
        whole[columns, :] = (
            mm_tn(hidden[:rows, columns], cotangent_a[...])
            + mm_tn(hidden[rows:, columns], pair_b[rows:, :])
        ).astype(LOW)
    for place, (other, relative) in enumerate(places_of(stages, shards)):
        target = (keep, send)[place // shards]
        part = side_of(where) ^ other
        source = aligned((where[1] ^ relative) * 2 * down_rows + part * down_rows, down_rows)
        for t in range(width // LANES):
            target[place % shards, t * down_rows : (t + 1) * down_rows, :] = whole[
                source, t * LANES : (t + 1) * LANES
            ]


def split_shards(shards, stages, where, whole, keep, send, by_tiles=False):
    shard_rows = whole.shape[0] // shards
    for place, (_, relative) in enumerate(places_of(stages, shards)):
        target = (keep, send)[place // (shards // 2)]
        source = aligned((where[1] ^ relative) * shard_rows, shard_rows)
        if by_tiles:
            for t in range(whole.shape[1] // LANES):
                target[place % (shards // 2), t * shard_rows : (t + 1) * shard_rows, :] = whole[
                    source, t * LANES : (t + 1) * LANES
                ]
        else:
            target[place % (shards // 2), :, :] = whole[source, :]


def score_grads(query, key, value, grad, offset, mask):
    scores = jnp.where(mask, mm_nt(query, key) + offset, NEG_FILL)
    expd = jnp.exp(scores - jnp.max(scores, axis=-1, keepdims=True))
    probs = expd * (1.0 / jnp.sum(expd, axis=-1, keepdims=True))
    d_probs = mm_nt(grad, value)
    weighted = jnp.sum(d_probs * probs, axis=-1, keepdims=True)
    d_scores = (probs * (d_probs - weighted)).astype(LOW)
    return (
        mm(d_scores, key),
        mm_tn(d_scores, query),
        mm_tn(probs.astype(LOW), grad),
        d_scores.astype(FULL),
    )


def fold_diagonals(flat):
    rows = flat.shape[0]
    folded = flat[:8, :]
    for base in range(8, rows, 8):
        folded = folded + pltpu.roll(flat[base : base + 8, :], 2 * rows - base, 1)
    return folded


def inside_grads_kernel(
    size,
    shards,
    stages,
    where,
    qkv,
    d_heads,
    heads_mine,
    heads_other,
    d_attn,
    row_starts,
    col_starts,
    bias,
    d_cols,
    d_bias,
    keep,
    send,
    d_out,
):
    rows, half = row_starts.shape[1], d_heads.shape[1]
    core = core_of(where)
    lane = lanes_at(core * half, half)
    value = mm_tn(heads_mine[...], d_attn[:, lane])
    d_out[aligned(core * half, half), :] = value.astype(LOW)
    value = mm_tn(heads_other[:rows, :], d_attn[rows:, lane])
    value = value + mm_tn(heads_other[rows:, :], d_attn[:rows, lane])
    d_out[aligned((1 - core) * half, half), :] = value.astype(LOW)
    split_shards(shards, stages, where, d_out, keep, send, by_tiles=True)
    masks, grads = [], []
    for stream in range(2):
        own_col = col_starts[:, 2 * stream : 2 * stream + 1]
        own_row = row_starts[3 * stream + 1 : 3 * stream + 2, :]
        settled = own_col != tail_of(row_starts, stream)
        masks.append((own_col == own_row) & settled)
        began = settled & (own_col >= ((where[0] ^ stream) * shards + where[1]) * rows)
        grad = d_heads[stream * rows : (stream + 1) * rows, :].astype(FULL)
        grads.append(jnp.where(began, grad, 0.0).astype(LOW))
    for pair in range(half // size // 2):
        outs = []
        for head in (2 * pair, 2 * pair + 1):
            near, _ = bias_tiles(bias[head : head + 1, :], rows)
            at = head * size
            flat = jnp.zeros((rows, rows), FULL)
            for stream in range(2):
                own = slice(2 * stream * rows, (2 * stream + 1) * rows)
                one = score_grads(
                    qkv[own, at : at + size],
                    qkv[own, half + at : half + at + size],
                    qkv[own, 2 * half + at : 2 * half + at + size],
                    grads[stream][:, at : at + size],
                    near,
                    masks[stream],
                )
                flat = flat + one[3]
                outs.append(one)
            flat = jnp.concatenate([flat, jnp.zeros((rows, rows), FULL)], axis=1)
            d_bias[8 * head : 8 * head + 8, :] = fold_diagonals(flat)
        for part in range(3):
            columns = slice(part * half + 2 * pair * size, part * half + (2 * pair + 2) * size)
            for stream in range(2):
                d_cols[stream * rows : (stream + 1) * rows, columns] = jnp.concatenate(
                    [outs[stream][part], outs[2 + stream][part]], axis=1
                ).astype(LOW)


def crossing_grads_kernel(
    shards,
    first_head,
    last_head,
    size,
    stages,
    where,
    qkv,
    normed,
    d_heads,
    d_after,
    d_inside,
    row_starts,
    col_starts,
    bias,
    d_cols,
    keep,
    send,
    d_bias,
    d_weights,
):
    rows, half = row_starts.shape[1], d_heads.shape[1]
    width = normed.shape[1]
    group = (last_head - first_head) * size
    span = slice(first_head * size, last_head * size)
    last_cols, masks, turns, mixes, grads = [], [], [], [], []
    for stream in range(2):
        tail = tail_of(row_starts, stream)
        own_col = col_starts[:, 2 * stream : 2 * stream + 1]
        after_col = col_starts[:, 2 * stream + 1 : 2 * stream + 2]
        own_row = row_starts[3 * stream + 1 : 3 * stream + 2, :]
        after_row = row_starts[3 * stream + 2 : 3 * stream + 3, :]
        is_last_col, is_last_row = own_col == tail, own_row == tail
        mix_col = jnp.where(is_last_col, own_col, after_col)
        mix_row = jnp.where(is_last_row, own_row, after_row)
        last_cols.append(is_last_col)
        masks.append((mix_col == tail) & (mix_row == tail))
        turns.append(is_last_col != is_last_row)
        base = 2 * stream * rows
        mix = []
        for part in range(3):
            columns = slice(part * half + first_head * size, part * half + last_head * size)
            mix.append(
                pick(
                    is_last_col,
                    qkv[base : base + rows, columns],
                    qkv[base + rows : base + 2 * rows, columns],
                )
            )
        mixes.append(mix)
        here = slice(stream * rows, (stream + 1) * rows)
        mixed = jnp.where(
            is_last_col, d_heads[here, span].astype(FULL), d_after[here, span].astype(FULL)
        )
        grads.append(jnp.where(mix_col == tail, mixed, 0.0).astype(LOW))
    for pair in range((last_head - first_head) // 2):
        outs = []
        for index in (2 * pair, 2 * pair + 1):
            head = first_head + index
            near, far = bias_tiles(bias[head : head + 1, :], rows)
            at = index * size
            kept, turned = jnp.zeros((rows, rows), FULL), jnp.zeros((rows, rows), FULL)
            for stream in range(2):
                mix = mixes[stream]
                two = score_grads(
                    mix[0][:, at : at + size],
                    mix[1][:, at : at + size],
                    mix[2][:, at : at + size],
                    grads[stream][:, at : at + size],
                    jnp.where(turns[stream], far, near),
                    masks[stream],
                )
                kept = kept + jnp.where(turns[stream], 0.0, two[3])
                turned = turned + jnp.where(turns[stream], two[3], 0.0)
                outs.append(two)
            d_bias[8 * index : 8 * index + 8, :] = fold_diagonals(
                jnp.concatenate([kept, turned], axis=1)
            )
        for part in range(3):
            columns = slice(part * group + 2 * pair * size, part * group + (2 * pair + 2) * size)
            for stream in range(2):
                d_cols[stream * rows : (stream + 1) * rows, columns] = jnp.concatenate(
                    [outs[stream][part], outs[2 + stream][part]], axis=1
                ).astype(LOW)
    total = [jnp.zeros((width, group), FULL) for _ in range(3)]
    for stream in range(2):
        base = 2 * stream * rows
        own, ahead = normed[base : base + rows, :], normed[base + rows : base + 2 * rows, :]
        normed_mix = pick(last_cols[stream], own, ahead)
        here = slice(stream * rows, (stream + 1) * rows)
        for part in range(3):
            inner = slice(part * half + first_head * size, part * half + last_head * size)
            total[part] = total[part] + mm_tn(own, d_inside[here, inner])
            total[part] = total[part] + mm_tn(
                normed_mix, d_cols[here, part * group : (part + 1) * group]
            )
    for part in range(3):
        d_weights[:, part * group : (part + 1) * group] = total[part].astype(LOW)
    split_shards(shards, stages, where, d_weights, keep, send)


def normed_grads_kernel(
    sizes, weights, d_inside, own_a, halo_a, pair_b, halo_b, row_starts, col_starts, *refs
):
    *crossing, keep, send, d_gain = refs
    rows, half = col_starts.shape[0], weights.shape[1] // 3
    inside = mm_nt(d_inside[...], weights[...])
    across = jnp.zeros(inside.shape, FULL)
    begin = 0
    for ref, group in zip(crossing, sizes, strict=True):
        for part in range(3):
            across = across + mm_nt(
                ref[:, part * group : (part + 1) * group],
                weights[:, part * half + begin : part * half + begin + group],
            )
        begin += group
    total = jnp.zeros((1, weights.shape[0]), FULL)
    streams = ((own_a, halo_a, keep), (pair_b, halo_b, send))
    for stream, (own, halo, target) in enumerate(streams):
        is_last = col_starts[:, 2 * stream : 2 * stream + 1] == tail_of(row_starts, stream)
        here = slice(stream * rows, (stream + 1) * rows)
        mine = jnp.where(is_last, across[here], inside[here])
        sent = jnp.where(is_last, 0.0, across[here])
        target[:rows, :] = mine.astype(target.dtype)
        target[rows:, :] = sent.astype(target.dtype)
        values, ahead = own[:rows, :].astype(FULL), halo[rows:, :].astype(FULL)
        share = mine * (values * inverse_rms(values)) + sent * (ahead * inverse_rms(ahead))
        total = total + jnp.sum(share, axis=0, keepdims=True)
    d_gain[...] = total


def tokens_kernel(own, gains, d_resid, d_own, d_before, out_keep, out_other, d_tokens, output):
    values = own[...].astype(FULL)
    grad = d_own[...] + d_before[...].astype(FULL)
    d_tokens[...] = d_resid[...] + norm_back(values, inverse_rms(values), gains[0:1, :], grad)
    output[...] = (out_keep[...] + out_other[...].astype(FULL)).astype(LOW)


def unpack_feed_kernel(tile_step, where, mine, other, d_gate, d_up, d_down, d_out):
    rows, half = d_out.shape[0], d_out.shape[1] // 2
    tiles, down_tiles = d_gate.shape[1] // (4 * LANES), d_down.shape[1] // LANES
    down_rows = d_down.shape[0] // 4
    begin = 0
    for relative in range(2):
        side = side_of(where) ^ relative
        for which, part in enumerate((mine, other)):
            core = core_of(where) ^ which
            at = begin
            target = aligned((2 * core + side) * down_rows, down_rows)
            for t in range(down_tiles):
                d_down[target, t * LANES : (t + 1) * LANES] = part[
                    at + t * down_rows : at + (t + 1) * down_rows, :
                ].astype(FULL)
            at += down_tiles * down_rows
            for matrix in (d_up, d_gate):
                for t in range(tiles):
                    lane = lanes_at(tile_step(core, side * tiles + t), LANES)
                    matrix[:, lane] = part[at + t * rows : at + (t + 1) * rows, :].astype(FULL)
                at += tiles * rows
        begin = at
    for which, part in enumerate((mine, other)):
        core = core_of(where) ^ which
        for t in range(half // LANES):
            first = begin + t * rows
            d_out[:, lanes_at(core * half + t * LANES, LANES)] = part[
                first : first + rows, :
            ].astype(FULL)


def unpack_attend_kernel(sizes, where, mine, other, d_query, d_key, d_value):
    half = d_query.shape[1] // 2
    for which, ref in enumerate((mine, other)):
        core = core_of(where) ^ which
        begin, column = 0, 0
        for group in sizes:
            for target in (d_query, d_key, d_value):
                target[:, lanes_at(core * half + begin, group)] = ref[
                    :, column : column + group
                ].astype(FULL)
                column += group
            begin += group


def shaped(shape, dtype):
    return jax.ShapeDtypeStruct(shape, dtype)


def per_device(
    tokens,
    cotangent,
    offsets,
    w_query,
    w_key,
    w_value,
    w_attn_out,
    w_gate,
    w_up,
    w_ff_out,
    gain_attn,
    gain_ff,
    rel_table,
):
    rows, width = tokens.shape
    shards = lax.axis_size("shard")
    shard, rep = lax.axis_index("shard"), lax.axis_index("rep")
    heads_count, table_rows = rel_table.shape[1], rel_table.shape[0]
    buckets = table_rows * shards
    shard_rows, inner = w_gate.shape
    half, size = width // 2, width // heads_count
    own_heads = heads_count // 2
    piece = w_ff_out.shape[0] // 2
    core = rep % 2
    where = jnp.stack([rep, shard]).astype(jnp.int32)

    starts_all = jnp.arange(offsets.shape[0], dtype=jnp.int32) - offsets
    start_pad = jnp.pad(starts_all, (rows, rows), constant_values=-1)
    first_a, first_b = (rep * shards + shard) * rows, ((rep ^ 1) * shards + shard) * rows
    window_a = lax.dynamic_slice_in_dim(start_pad, first_a, 3 * rows).reshape(3, rows)
    window_b = lax.dynamic_slice_in_dim(start_pad, first_b, 3 * rows).reshape(3, rows)
    row_starts = jnp.concatenate([window_a, window_b], axis=0)
    col_starts = jnp.stack([window_a[1], window_a[2], window_b[1], window_b[2]], axis=1)
    by_tiles = piece % LANES == 0

    def tile_step(which_core, tile):
        if by_tiles:
            per_shard = piece // LANES
            return ((tile // per_shard * 2 + which_core) * per_shard + tile % per_shard) * LANES
        return which_core * (inner // 2) + tile * LANES

    def by_core(matrix):
        if by_tiles:
            return matrix
        split = matrix.reshape(shard_rows, shards, 2, piece).transpose(0, 2, 1, 3)
        return split.reshape(shard_rows, inner)

    def from_core(matrix):
        if by_tiles:
            return matrix
        split = matrix.reshape(shard_rows, 2, shards, piece).transpose(0, 2, 1, 3)
        return split.reshape(shard_rows, inner)

    tiles = inner // (4 * LANES)
    down_block = width // LANES * (piece // 2)
    qkv_side = -(-3 * half // (2 * LANES)) * LANES
    steps = Sequence(jnp.zeros((8, LANES), FULL))
    qkv_own, ff_own, rest_own = steps.call(
        functools.partial(pack_kernel, tile_step),
        (where,),
        (
            w_query,
            w_key,
            w_value,
            w_attn_out,
            by_core(w_gate),
            by_core(w_up),
            w_ff_out,
            gain_attn.reshape(1, shard_rows),
            gain_ff.reshape(1, shard_rows),
            rel_table,
        ),
        (
            shaped((shard_rows + SMALL, qkv_side), LOW),
            shaped((2 * tiles * shard_rows, LANES), LOW),
            shaped((2 * piece + shard_rows, half), LOW),
        ),
        room=58,
    )
    onehot = np.zeros((shards, SMALL, 2 * rows), np.float32)
    onehot[:, 2 : 2 + table_rows] = bucket_onehot(2 * rows, buckets).T.reshape(
        shards, table_rows, 2 * rows
    )
    onehot = jnp.asarray(onehot.reshape(shards * SMALL, 2 * rows), LOW)


    up = [(i, i + 1) for i in range(shards - 1)]
    down = [(i + 1, i) for i in range(shards - 1)]
    by_x, by_core = (("rep", 1),), ("rep", 0)
    far, near = far_first(shards), near_first(shards)

    def joined(*parts, axis=0):
        return jnp.concatenate(parts, axis=axis)

    pair = joined(tokens, cotangent)
    received, pair_b = swap(qkv_own, "shard", far[0]), swap(pair, *by_core)
    steps.mark(qkv_own, pair)
    shifted = steps.take(tokens)
    before, ahead = lax.ppermute(shifted, "shard", up), lax.ppermute(shifted, "shard", down)
    qkv_near = joined(qkv_own, steps.take(received))
    pair_b = steps.take(pair_b)
    ff_received = swap(steps.take(ff_own), "shard", far[0])
    for bit in far[1:-1]:
        received = swap(qkv_near, "shard", bit)
        steps.mark(qkv_near)
        qkv_near = joined(qkv_near, steps.take(received))
    qkv_far, qkv_side = swap(qkv_near, "shard", far[-1]), swap(qkv_near, *by_x[0])
    steps.mark(qkv_near)
    halo = joined(steps.take(before), steps.take(ahead))
    ff_near = joined(ff_own, steps.take(ff_received))
    ff_received, halo_b = swap(ff_near, "shard", far[1]), swap(halo, *by_core)
    rest_received = swap(steps.take(rest_own), "shard", far[0])
    steps.mark(ff_near, halo)
    qkv_far, halo_b = steps.take(qkv_far), steps.take(halo_b)
    qkv_other = swap(qkv_far, *by_x[0])
    steps.mark(qkv_far)
    qkv_side = steps.take(qkv_side)
    ff_near = joined(ff_near, steps.take(ff_received))
    rest_near = rest_own
    for first, bit in zip(far[1:-1], far[2:-1]):
        ff_received = swap(ff_near, "shard", bit)
        rest_near = joined(rest_near, steps.take(rest_received))
        rest_received = swap(rest_near, "shard", first)
        steps.mark(ff_near, rest_near)
        ff_near = joined(ff_near, steps.take(ff_received))
    ff_far, ff_side = swap(ff_near, "shard", far[-1]), swap(ff_near, *by_x[0])
    steps.mark(ff_near)
    rest_near = joined(rest_near, steps.take(rest_received))
    rest_received = swap(rest_near, "shard", far[-2])
    steps.mark(rest_near)
    qkv_other = steps.take(qkv_other)
    heads, normed, qkv, w_qkv, gains, bias = steps.call(
        functools.partial(attend_kernel, shards, size),
        (where,),
        (
            tokens,
            halo,
            pair_b,
            halo_b,
            qkv_near,
            qkv_far,
            qkv_side,
            qkv_other,
            row_starts,
            col_starts,
            onehot,
        ),
        (
            shaped((2 * rows, half), LOW),
            shaped((4 * rows, width), LOW),
            shaped((4 * rows, 3 * half), LOW),
            shaped((width, 3 * half), LOW),
            shaped((SMALL, width), FULL),
            shaped((8, 2 * rows), FULL),
        ),
        [pltpu.VMEM((rows, 2 * half), LOW), pltpu.VMEM((shards * SMALL, LANES), FULL)],
        micros=400,
    )
    heads_other = swap(heads, *by_core)
    rest_near = joined(rest_near, steps.take(rest_received))
    rest_far = swap(rest_near, "shard", far[-1])
    ff_far, ff_side = steps.take(ff_far), steps.take(ff_side)
    ff_other, rest_near_b = swap(steps.take(ff_far), *by_x[0]), swap(rest_near, *by_core)
    steps.mark(rest_near, ff_far, ff_side)
    heads_other, rest_near_b = steps.take(heads_other), steps.take(rest_near_b)
    rest_far = steps.take(rest_far)
    rest_far_b = swap(rest_far, *by_core)
    steps.mark(rest_far)
    ff_other, rest_far_b = steps.take(ff_other), steps.take(rest_far_b)
    wide = shaped((2 * rows, inner // 2), LOW)
    (
        out_keep,
        out_send,
        d_normed_keep,
        d_normed_send,
        resid,
        normed_ff,
        hidden,
        d_gate,
        d_linear,
        w_out,
    ) = steps.call(
        functools.partial(feed_kernel, shards),
        (where,),
        (
            heads,
            heads_other,
            tokens,
            cotangent,
            pair_b,
            gains,
            rest_near,
            rest_far,
            rest_near_b,
            rest_far_b,
            ff_near,
            ff_far,
            ff_side,
            ff_other,
        ),
        (
            shaped((rows, width), FULL),
            shaped((rows, width), LOW),
            shaped((2 * rows, width), FULL),
            shaped((2 * rows, width), LOW),
            shaped((2 * rows, width), FULL),
            shaped((2 * rows, width), LOW),
            wide,
            wide,
            wide,
            shaped((width, width), LOW),
        ),
        [
            pltpu.VMEM((width, inner // 2), LOW),
            pltpu.VMEM((width, inner // 2), LOW),
            pltpu.VMEM((inner // 2, width), LOW),
        ],
        micros=400,
    )
    d_normed_other, out_other = swap(d_normed_send, *by_core), swap(out_send, *by_core)
    slices = shaped((shards, tiles * shard_rows, LANES), LOW)
    down_slices = shaped((shards, down_block, LANES), LOW)
    by_near = tuple(("shard", bit) for bit in near)
    down_stages = by_x + by_near
    gate_stages = by_near[:1] + by_x + by_near[1:]
    up_stages = by_x + by_near[1:2] + by_near[:1] + by_near[2:]
    down_keep, down_send = steps.call(
        functools.partial(down_grads_kernel, shards, down_stages),
        (where,),
        (hidden, cotangent, pair_b),
        (down_slices, down_slices),
        [pltpu.VMEM((inner // 2, width), LOW)],
        micros=4,
    )
    down_received = exchange(down_send, down_stages[0])
    d_normed_other, out_other = steps.take(d_normed_other), steps.take(out_other)
    d_resid, d_attn, d_heads, d_gain_two = steps.call(
        resid_grads_kernel,
        (where,),
        (d_normed_keep, d_normed_other, resid, cotangent, pair_b, gains, w_out),
        (
            shaped((rows, width), FULL),
            shaped((2 * rows, width), LOW),
            shaped((2 * rows, half), LOW),
            shaped((1, width), FULL),
        ),
        micros=5,
    )
    d_heads_after = lax.ppermute(d_heads, "shard", down)
    gate_keep, gate_send = steps.call(
        functools.partial(wide_grads_kernel, shards, gate_stages),
        (where,),
        (normed_ff, d_gate),
        (slices, slices),
        [pltpu.VMEM((2, width, inner // 4), LOW)],
        micros=4,
    )
    gate_received = exchange(gate_send, gate_stages[0])
    up_keep, up_send = steps.call(
        functools.partial(wide_grads_kernel, shards, up_stages),
        (where,),
        (normed_ff, d_linear),
        (slices, slices),
        [pltpu.VMEM((2, width, inner // 4), LOW)],
        micros=4,
    )
    up_received = exchange(up_send, up_stages[0])
    out_slices = shaped((shards // 2, shard_rows * half // LANES, LANES), LOW)
    d_inside, d_bias, o_keep, o_send = steps.call(
        functools.partial(inside_grads_kernel, size, shards, by_near),
        (where,),
        (qkv, d_heads, heads, heads_other, d_attn, row_starts, col_starts, bias),
        (
            shaped((2 * rows, 3 * half), LOW),
            shaped((8 * own_heads, 2 * rows), FULL),
            out_slices,
            out_slices,
        ),
        [pltpu.VMEM((width, half), LOW)],
        micros=11,
    )

    d_down, down_received = steps.send_half(steps.add(down_keep, down_received), down_stages[1])
    o_received = steps.send(o_send, by_near[0])
    d_heads_after = steps.take(d_heads_after)
    sizes = [count * size for count in GROUPS]

    def crossing_grads(first, count):
        attn_slices = shaped((shards // 2, shard_rows, 3 * count * size), LOW)
        return steps.call(
            functools.partial(
                crossing_grads_kernel, shards, first, first + count, size, by_near
            ),
            (where,),
            (qkv, normed, d_heads, d_heads_after, d_inside, row_starts, col_starts, bias),
            (
                shaped((2 * rows, 3 * count * size), LOW),
                attn_slices,
                attn_slices,
                shaped((8 * count, 2 * rows), FULL),
            ),
            [pltpu.VMEM((width, 3 * count * size), LOW)],
            micros=12 if not first else 400,
            room=58,
        )

    cols_one, one_keep, one_send, d_bias_one = crossing_grads(0, GROUPS[0])
    one_received = steps.send(one_send, by_near[0])
    d_gate, gate_received = steps.send_half(steps.add(gate_keep, gate_received), gate_stages[1])
    d_up, up_received = steps.send_half(steps.add(up_keep, up_received), up_stages[1])
    d_down, down_received = steps.send_half(steps.add(d_down, down_received), down_stages[2])
    cols_two, two_keep, two_send, d_bias_two = crossing_grads(GROUPS[0], GROUPS[1])
    d_out = steps.add(o_keep, o_received)
    two_received = steps.send(two_send, by_near[0])
    d_gate = joined(steps.add(d_gate, gate_received), d_out, axis=1)
    d_gate, gate_received = steps.send_half(d_gate, by_near[1])
    d_down, down_received = steps.send_half(steps.add(d_down, down_received), down_stages[3])
    d_up, up_received = steps.send_half(steps.add(d_up, up_received), up_stages[2])
    keep, send, d_gain_one = steps.call(
        functools.partial(normed_grads_kernel, tuple(sizes)),
        (),
        (
            w_qkv,
            d_inside,
            tokens,
            halo,
            pair_b,
            halo_b,
            row_starts,
            col_starts,
            cols_one,
            cols_two,
        ),
        (
            shaped((2 * rows, width), FULL),
            shaped((2 * rows, width), LOW),
            shaped((1, width), FULL),
        ),
        micros=400,
        room=58,
    )
    folds = np.stack([np.roll(bucket_onehot(2 * rows, buckets), row, axis=0) for row in range(8)])
    d_bias = d_bias + jnp.concatenate([d_bias_one, d_bias_two], axis=0)
    d_bias = d_bias.reshape(own_heads, 16 * rows)
    d_table = lax.dot_general(
        d_bias,
        jnp.asarray(folds.reshape(16 * rows, buckets)),
        (((1,), (0,)), ((), ())),
        precision=lax.Precision.HIGHEST,
    )
    d_table = lax.dynamic_update_slice(
        jnp.zeros((heads_count, buckets), FULL), d_table, (core * own_heads, 0)
    ).T
    smalls = jnp.concatenate([d_gain_one.reshape(-1), d_gain_two.reshape(-1), d_table.reshape(-1)])
    rest = -smalls.shape[0] % (8 * LANES)
    smalls = jnp.pad(smalls, (0, rest)).reshape(-1, LANES)
    small_stages = [("rep", bit) for bit in range(bits_of(lax.axis_size("rep")))] + list(by_near)
    attn = joined(
        steps.add(one_keep, one_received), steps.add(two_keep, two_received), axis=2
    )
    attn, attn_received = steps.send_half(attn, by_near[1])
    d_own_received = exchange(send, by_core)
    d_gate = joined(steps.add(d_up, up_received), steps.add(d_gate, gate_received), axis=1)
    d_gate, gate_received = steps.send_half(d_gate, by_near[2])
    small_received = steps.send(smalls, small_stages[0])
    d_down = steps.add(d_down, down_received)
    steps.mark()
    d_own = keep + steps.take(d_own_received).astype(FULL)
    d_before = lax.ppermute(d_own[rows:].astype(LOW), "shard", up)
    smalls = smalls + steps.take(small_received)
    small_received = steps.send(smalls, small_stages[1])
    steps.mark(d_own)
    attn, attn_received = steps.send_half(steps.add(attn, attn_received), by_near[2])
    d_gate = steps.add(d_gate, gate_received)
    for stage in by_near[3:]:
        attn = steps.add(attn, attn_received)
        attn, attn_received = steps.send_half(attn, stage)
        d_gate, gate_received = steps.send_half(d_gate, stage)
        d_gate = steps.add(d_gate, gate_received)
        d_down, down_received = steps.send_half(d_down, stage)
        d_down = steps.add(d_down, down_received)
    wide = tiles * shard_rows
    d_feed, d_out = joined(d_down[0], d_gate[0, : 2 * wide]), d_gate[0, 2 * wide :]
    for bit in range(2, bits_of(lax.axis_size("rep"))):
        d_feed = steps.add(d_feed, exchange(d_feed, ("rep", bit)))
        d_out = steps.add(d_out, exchange(d_out, ("rep", bit)))
    feed_received = steps.send(joined(d_feed, d_out), by_x[0])
    smalls = smalls + steps.take(small_received)
    small_received = steps.send(smalls, small_stages[2])
    steps.mark()
    attn = steps.add(attn, attn_received)[0]
    for bit in range(2, bits_of(lax.axis_size("rep"))):
        attn = steps.add(attn, exchange(attn, ("rep", bit)))
    attn_received = steps.send(attn, by_x[0])
    smalls = smalls + steps.take(small_received)
    small_received = steps.send(smalls, small_stages[3])
    feed_received = steps.take(feed_received)
    feed = d_feed.shape[0]
    d_feed = joined(d_feed, feed_received[:feed], add_low(d_out, feed_received[feed:]))
    feed_other = steps.send(d_feed, by_core)
    d_tokens, output = steps.call(
        tokens_kernel,
        (),
        (tokens, gains, d_resid, d_own[:rows], steps.take(d_before), out_keep, out_other),
        (shaped((rows, width), FULL), shaped((rows, width), LOW)),
        micros=400,
    )
    attn = steps.add(attn, attn_received)
    attn_other = steps.send(attn, by_core)
    feed_other = steps.take(feed_other)
    for stage in small_stages[4:]:
        smalls = smalls + steps.take(small_received)
        small_received = steps.send(smalls, stage)
    d_w_gate, d_w_up, d_w_ff_out, d_w_attn_out = steps.call(
        functools.partial(unpack_feed_kernel, tile_step),
        (where,),
        (d_feed, feed_other),
        (
            shaped(w_gate.shape, FULL),
            shaped(w_up.shape, FULL),
            shaped(w_ff_out.shape, FULL),
            shaped(w_attn_out.shape, FULL),
        ),
        micros=400,
    )
    attn_other = steps.take(attn_other)
    smalls = (smalls + steps.take(small_received)).reshape(-1)
    d_w_query, d_w_key, d_w_value = steps.call(
        functools.partial(unpack_attend_kernel, tuple(sizes)),
        (where,),
        (attn, attn_other),
        (shaped(w_query.shape, FULL),) * 3,
        micros=400,
    )

    def own_part(begin, length):
        return lax.dynamic_slice_in_dim(smalls, begin + shard * length, length)

    return (
        output,
        d_tokens,
        d_w_query,
        d_w_key,
        d_w_value,
        d_w_attn_out,
        from_core(d_w_gate),
        from_core(d_w_up),
        d_w_ff_out,
        own_part(0, shard_rows),
        own_part(width, shard_rows),
        own_part(2 * width, table_rows * heads_count).reshape(table_rows, heads_count),
    )


def solution(mesh):
    tokens_spec, rows_spec, line_spec = P(("rep", "shard"), None), P("shard", None), P("shard")
    return jax.shard_map(
        per_device,
        mesh=mesh,
        in_specs=(tokens_spec, tokens_spec, P()) + (rows_spec,) * 7 + (line_spec,) * 2 + (rows_spec,),
        out_specs=(tokens_spec,) * 2 + (rows_spec,) * 7 + (line_spec,) * 2 + (rows_spec,),
        check_vma=False,
    )
```

```python
import functools

import jax
import jax.numpy as jnp
import numpy as np
from jax import lax
from jax.experimental import pallas as pl
from jax.experimental.pallas import tpu as pltpu
from jax.sharding import PartitionSpec as P

NEG_FILL = -1e30
EPSILON = 1e-06
BORDERS = (1, 2, 3, 4, 5, 6, 7, 8, 12, 16, 23, 32, 46, 64, 91)
LANES = 128
SMALL = 8
SCALE = 2 * 10**8
GROUPS = (4, 2)
LOW = jnp.bfloat16
FULL = jnp.float32
GELU_A = float(np.sqrt(2.0 / np.pi))
GELU_B = 0.044715


def bits_of(count):
    return count.bit_length() - 1


def swap(block, axis, bit):
    count = lax.axis_size(axis)
    return lax.ppermute(block, axis, [(i, i ^ (1 << bit)) for i in range(count)])


def add_low(left, right):
    return (left.astype(FULL) + right.astype(FULL)).astype(LOW)


def gather_shards(block):
    for bit in far_first(lax.axis_size("shard")):
        block = jnp.concatenate([block, swap(block, "shard", bit)], axis=0)
    return block


def reverse_bits(value, count):
    result = 0
    for bit in range(bits_of(count)):
        result = result | (((value >> bit) & 1) << (bits_of(count) - 1 - bit))
    return result


def far_first(shards):
    return tuple(reversed(range(bits_of(shards))))


def near_first(shards):
    return tuple(range(bits_of(shards)))


def shards_at(shard, shards, order):
    places = []
    for place in range(shards):
        moved = sum(((place >> step) & 1) << bit for step, bit in enumerate(order))
        places.append(shard ^ moved)
    return places


def exchange(block, stage):
    return swap(block, *stage)


def places_of(stages, shards):
    places = []
    for place in range(2 ** len(stages)):
        side, shard = 0, 0
        for step, (axis, bit) in enumerate(stages):
            here = (place >> (len(stages) - 1 - step)) & 1
            if axis == "rep":
                side |= here
            else:
                shard |= here << bit
        places.append((side, shard))
    return places


def mark_kernel():
    pass


class Sequence:
    def __init__(self, token):
        self.token, self.sent = token, []

    def send(self, block, stage):
        self.sent.append(block)
        return exchange(block, stage)

    def send_half(self, blocks, stage):
        kept, sent = halves_of(blocks)
        return kept, self.send(sent, stage)

    def take(self, received):
        received, self.token = lax.optimization_barrier((received, self.token))
        return received

    def add(self, kept, received):
        return add_low(kept, self.take(received))

    def mark(self, *ready, micros=500):
        self.call(None, (), (), (), waits=ready, micros=micros)

    def call(self, kernel, scalars, arrays, outs, scratch=(), micros=3, waits=(), room=4):
        held = [(a.size, a.dtype) for a in (*arrays, *outs)]
        held += [(int(np.prod(a.shape)), a.dtype) for a in scratch]
        needed = sum(size * jnp.dtype(dtype).itemsize for size, dtype in held)
        waits, self.sent = (*waits, *self.sent), []
        skip, given = 1 + len(waits), 1 + len(waits) + len(scalars) + len(arrays) + len(outs)

        def body(*refs):
            if kernel is not None:
                kernel(*refs[skip:given], *refs[given + 1 :])

        def placed(arrays, space):
            return [pl.BlockSpec(memory_space=space) for _ in arrays]

        *results, self.token = pl.pallas_call(
            body,
            out_shape=(*outs, shaped(self.token.shape, self.token.dtype)),
            in_specs=placed((self.token, *waits), pl.ANY)
            + placed(scalars, pltpu.SMEM)
            + placed(arrays, pltpu.VMEM),
            out_specs=(*placed(outs, pltpu.VMEM), pl.BlockSpec(memory_space=pl.ANY)),
            scratch_shapes=scratch,
            input_output_aliases={0: len(outs)},
            compiler_params=pltpu.CompilerParams(vmem_limit_bytes=min(needed + room * 2**20, 58 * 2**20)),
            cost_estimate=pl.CostEstimate(
                flops=int(micros * SCALE), bytes_accessed=10**6, transcendentals=0
            ),
            name=getattr(kernel, "func", kernel or mark_kernel).__name__,
        )(self.token, *waits, *scalars, *arrays)
        return results


def halves_of(blocks):
    half = blocks.shape[0] // 2
    return blocks[:half], blocks[half:]


def sum_replicas(block, first_bit):
    for bit in range(first_bit, bits_of(lax.axis_size("rep"))):
        block = add_low(block, swap(block, "rep", bit))
    return block


def bucket_onehot(period, buckets):
    index = np.arange(period)
    relative = np.where(index < period // 2, index, index - period)
    distance = np.abs(relative)
    bucket = buckets // 2 * (relative > 0).astype(np.int64)
    for border in BORDERS:
        bucket = bucket + (distance >= border).astype(np.int64)
    return (bucket[:, None] == np.arange(buckets)[None, :]).astype(np.float32)


def mm(left, right):
    return lax.dot_general(left, right, (((1,), (0,)), ((), ())), preferred_element_type=FULL)


def mm_nt(left, right):
    return lax.dot_general(left, right, (((1,), (1,)), ((), ())), preferred_element_type=FULL)


def mm_tn(left, right):
    return lax.dot_general(left, right, (((0,), (0,)), ((), ())), preferred_element_type=FULL)


def inverse_rms(values):
    return lax.rsqrt(jnp.mean(values * values, axis=-1, keepdims=True) + EPSILON)


def norm_back(values, scale, gain, grad):
    inner = jnp.mean(gain * grad * values, axis=-1, keepdims=True)
    return scale * gain * grad - values * (scale * scale * scale * inner)


def pick(mask, left, right):
    return jnp.where(mask, left.astype(FULL), right.astype(FULL)).astype(left.dtype)


def aligned(index, size):
    return pl.ds(pl.multiple_of(index, 8), size)


def lanes_at(index, size):
    return pl.ds(pl.multiple_of(index, LANES), size)


def bias_tiles(bias_row, rows):
    rolled = pltpu.roll(
        jnp.broadcast_to(bias_row, (rows, 2 * rows)), 0, 1, stride=1, stride_axis=0
    )
    return rolled[:, :rows], rolled[:, rows:]


def core_of(where):
    return where[0] & 1


def side_of(where):
    return (where[0] >> 1) & 1


def tail_of(row_starts, stream):
    rows = row_starts.shape[1]
    return row_starts[3 * stream + 1 : 3 * stream + 2, rows - 1 : rows]


def pack_kernel(
    tile_step,
    where,
    w_query,
    w_key,
    w_value,
    w_out,
    w_gate,
    w_up,
    w_down,
    gain_one,
    gain_two,
    table,
    qkv,
    feed,
    rest,
):
    core, side = core_of(where), side_of(where)
    rows, half = w_query.shape[0], w_query.shape[1] // 2
    tiles = w_gate.shape[1] // (4 * LANES)
    width = qkv.shape[1]
    qkv[rows:, :] = jnp.zeros((SMALL, width), LOW)
    for which in range(2):

        @pl.when(side == which)
        def _():
            for t in range(width // LANES):
                part, tile = divmod(which * (3 * half - width) // LANES + t, half // LANES)
                qkv[:rows, t * LANES : (t + 1) * LANES] = (w_query, w_key, w_value)[part][
                    :, lanes_at(core * half + tile * LANES, LANES)
                ]

    qkv[rows : rows + 1, :rows] = gain_one[...]
    qkv[rows + 1 : rows + 2, :rows] = gain_two[...]
    qkv[rows + 2 : rows + 2 + table.shape[0], : table.shape[1]] = table[...]
    for which, ref in enumerate((w_gate, w_up)):
        for t in range(tiles):
            lane = tile_step(core, side * tiles + t)
            first = (which * tiles + t) * rows
            feed[first : first + rows, :] = ref[:, lanes_at(lane, LANES)]
    down_rows = w_down.shape[0] // 2
    own = aligned(core * down_rows, down_rows)
    rest[:down_rows, :] = w_down[own, :half]
    rest[down_rows : 2 * down_rows, :] = w_down[own, half:]
    rest[2 * down_rows :, :] = w_out[:, lanes_at(core * half, half)]


def attend_kernel(
    shards,
    size,
    where,
    own_a,
    halo_a,
    pair_b,
    halo_b,
    part_0,
    part_1,
    part_2,
    part_3,
    row_starts,
    col_starts,
    onehot,
    heads,
    normed,
    qkv,
    weights,
    gains,
    bias,
    kv_before,
    smalls,
):
    rows, width = own_a.shape
    shard_rows, half = width // shards, weights.shape[1] // 3
    block = shard_rows + SMALL
    for index, shard in enumerate(shards_at(where[1], shards, far_first(shards))):
        upper, first = index // (shards // 2), index % (shards // 2) * block
        for other, sources in enumerate(((part_0, part_1), (part_2, part_3))):
            source = sources[upper]
            lane = (side_of(where) ^ other) * (weights.shape[1] - source.shape[1])
            weights[
                aligned(shard * shard_rows, shard_rows), lanes_at(lane, source.shape[1])
            ] = source[first : first + shard_rows, :]
        source = (part_0, part_1)[upper]
        smalls[aligned(shard * SMALL, SMALL), :] = source[
            first + shard_rows : first + block, :LANES
        ].astype(FULL)
    total = jnp.zeros((SMALL, width), FULL)
    for shard in range(shards):
        line = jnp.concatenate(
            [
                smalls[shard * SMALL : (shard + 1) * SMALL, :],
                jnp.zeros((SMALL, width - LANES), FULL),
            ],
            axis=1,
        )
        total = total + (pltpu.roll(line, shard * shard_rows, 1) if shard else line)
    gains[...] = total
    gain = total[0:1, :]
    heads_here = half // size
    shift = jnp.where(core_of(where) == 0, 0, LANES - heads_here)
    table = pltpu.roll(smalls[...], shift, 1).astype(LOW)
    bias[...] = mm_tn(table, onehot[...])[: bias.shape[0], :]
    for stream, (own_ref, halo) in enumerate(((own_a, halo_a), (pair_b, halo_b))):
        base = 2 * stream * rows
        lines = []
        for tokens in (halo[:rows, :], own_ref[:rows, :], halo[rows:, :]):
            values = tokens.astype(FULL)
            lines.append((values * inverse_rms(values) * gain).astype(LOW))
        normed[base : base + rows, :] = lines[1]
        normed[base + rows : base + 2 * rows, :] = lines[2]
        for part in range(3):
            columns = slice(part * half, (part + 1) * half)
            qkv[base : base + 2 * rows, columns] = mm(
                normed[base : base + 2 * rows, :], weights[:, columns]
            ).astype(LOW)
            if part:
                kv_before[:, (part - 1) * half : part * half] = mm(
                    lines[0], weights[:, columns]
                ).astype(LOW)
        own_col = col_starts[:, 2 * stream : 2 * stream + 1]
        in_before = own_col == row_starts[3 * stream : 3 * stream + 1, :]
        in_own = own_col == row_starts[3 * stream + 1 : 3 * stream + 2, :]
        in_after = own_col == row_starts[3 * stream + 2 : 3 * stream + 3, :]
        allowed = in_own | in_before | in_after
        own, ahead = slice(base, base + rows), slice(base + rows, base + 2 * rows)
        for pair in range(half // size // 2):
            mixed = []
            for head in (2 * pair, 2 * pair + 1):
                at = head * size
                query = qkv[own, at : at + size]
                keys = slice(half + at, half + at + size)
                values = slice(2 * half + at, 2 * half + at + size)
                near, far = bias_tiles(bias[head : head + 1, :], rows)
                scores = jnp.where(
                    in_own,
                    mm_nt(query, qkv[own, keys]) + near,
                    jnp.where(
                        in_before,
                        mm_nt(query, kv_before[:, at : at + size]),
                        mm_nt(query, qkv[ahead, keys]),
                    )
                    + far,
                )
                scores = jnp.where(allowed, scores, NEG_FILL)
                expd = jnp.exp(scores - jnp.max(scores, axis=-1, keepdims=True))
                probs = expd * (1.0 / jnp.sum(expd, axis=-1, keepdims=True))
                total = mm(jnp.where(in_own, probs, 0.0).astype(LOW), qkv[own, values])
                total = total + mm(
                    jnp.where(in_before, probs, 0.0).astype(LOW),
                    kv_before[:, half + at : half + at + size],
                )
                total = total + mm(
                    jnp.where(in_after, probs, 0.0).astype(LOW), qkv[ahead, values]
                )
                mixed.append(total)
            heads[stream * rows : (stream + 1) * rows, 2 * pair * size : (2 * pair + 2) * size] = (
                jnp.concatenate(mixed, axis=1).astype(LOW)
            )


def feed_kernel(
    shards,
    where,
    heads_mine,
    heads_other,
    tokens_a,
    cotangent_a,
    pair_b,
    gains,
    rest_0,
    rest_1,
    rest_2,
    rest_3,
    part_0,
    part_1,
    part_2,
    part_3,
    out_keep,
    out_send,
    d_keep,
    d_send,
    resid,
    normed_ff,
    hidden,
    d_gate,
    d_linear,
    w_out,
    w_gate,
    w_up,
    w_down,
):
    rows, width = tokens_a.shape
    inner = w_gate.shape[1]
    shard_rows, down_rows = width // shards, inner // shards
    slab, half = inner // 2, width // 2
    tiles = slab // LANES
    block = 2 * tiles * shard_rows
    core, side = core_of(where), side_of(where)
    for index, shard in enumerate(shards_at(where[1], shards, far_first(shards))):
        upper, first = divmod(index, shards // 2)
        target = aligned(shard * shard_rows, shard_rows)
        for other, sources in enumerate(((part_0, part_1), (part_2, part_3))):
            part, start = sources[upper], first * block
            for t in range(tiles):
                lane = lanes_at((side ^ other) * slab + t * LANES, LANES)
                at = start + t * shard_rows
                w_gate[target, lane] = part[at : at + shard_rows, :]
                at = start + (tiles + t) * shard_rows
                w_up[target, lane] = part[at : at + shard_rows, :]
        rest, start = (rest_0, rest_1)[upper], first * (2 * down_rows + shard_rows)
        down = aligned(shard * down_rows, down_rows)
        w_down[down, :half] = rest[start : start + down_rows, :]
        w_down[down, half:] = rest[start + down_rows : start + 2 * down_rows, :]
        for other, sources in enumerate(((rest_0, rest_1), (rest_2, rest_3))):
            at = start + 2 * down_rows
            w_out[target, lanes_at((core ^ other) * half, half)] = sources[upper][
                at : at + shard_rows, :
            ]
    gain = gains[1:2, :]
    mine = mm(heads_mine[...], w_out[aligned(core * half, half), :])
    other = mm(heads_other[...], w_out[aligned((1 - core) * half, half), :])
    cotangents = (cotangent_a[...], pair_b[rows:, :])
    for stream, tokens in enumerate((tokens_a[...], pair_b[:rows, :])):
        span, back = slice(stream * rows, (stream + 1) * rows), slice((1 - stream) * rows, (2 - stream) * rows)
        value = tokens.astype(FULL) + (mine[span] + other[back])
        resid[span, :] = value
        normed_ff[span, :] = (value * inverse_rms(value) * gain).astype(LOW)
    for q in range(2):
        columns = slice(q * slab, (q + 1) * slab)
        for stream, cotangent in enumerate(cotangents):
            span = slice(stream * rows, (stream + 1) * rows)
            gate = mm(normed_ff[span, :], w_gate[:, columns])
            linear = mm(normed_ff[span, :], w_up[:, columns])
            d_hidden = mm_nt(cotangent, w_down[columns, :])
            square = gate * gate
            tanh = jnp.tanh(GELU_A * (gate + GELU_B * square * gate))
            rise = 0.5 * (1.0 + tanh)
            gelu = gate * rise
            slope = rise + 0.5 * gate * (1.0 - tanh * tanh) * (
                GELU_A * (1.0 + 3.0 * GELU_B * square)
            )
            hidden[span, columns] = (gelu * linear).astype(LOW)
            d_gate[span, columns] = (d_hidden * linear * slope).astype(LOW)
            d_linear[span, columns] = (d_hidden * gelu).astype(LOW)
    d_normed = mm_nt(d_gate[...], w_gate[...]) + mm_nt(d_linear[...], w_up[...])
    d_keep[...] = d_normed
    d_send[...] = d_normed.astype(LOW)
    out_keep[...] = resid[:rows, :] + mm(hidden[:rows, :], w_down[...])
    out_send[...] = mm(hidden[rows:, :], w_down[...]).astype(LOW)


def resid_grads_kernel(
    where,
    d_keep,
    d_other,
    resid,
    cotangent_a,
    pair_b,
    gains,
    w_out,
    d_resid,
    d_attn,
    d_heads,
    d_gain,
):
    rows, width = cotangent_a.shape
    half = width // 2
    for stream, cotangent in enumerate((cotangent_a[...], pair_b[rows:, :])):
        span, back = slice(stream * rows, (stream + 1) * rows), slice((1 - stream) * rows, (2 - stream) * rows)
        d_normed = d_keep[span, :] + d_other[back, :].astype(FULL)
        values = resid[span, :]
        scale = inverse_rms(values)
        grad = cotangent.astype(FULL) + norm_back(values, scale, gains[1:2, :], d_normed)
        d_attn[span, :] = grad.astype(LOW)
        if stream == 0:
            d_resid[...] = grad
            d_gain[...] = jnp.sum(d_normed * values * scale, axis=0, keepdims=True)
    d_heads[...] = mm_nt(d_attn[...], w_out[aligned(core_of(where) * half, half), :]).astype(LOW)


def wide_grads_kernel(shards, stages, where, normed_ff, grad, keep, send, whole):
    width, slab = normed_ff.shape[1], grad.shape[1] // 2
    shard_rows = width // shards
    for other in range(2):
        part = side_of(where) ^ other
        whole[other, :, :] = mm_tn(normed_ff[...], grad[:, lanes_at(part * slab, slab)]).astype(LOW)
    for place, (other, relative) in enumerate(places_of(stages, shards)):
        target = (keep, send)[place // shards]
        source = aligned((where[1] ^ relative) * shard_rows, shard_rows)
        for t in range(slab // LANES):
            target[place % shards, t * shard_rows : (t + 1) * shard_rows, :] = whole[
                other, source, t * LANES : (t + 1) * LANES
            ]


def down_grads_kernel(
    shards, stages, where, hidden, cotangent_a, pair_b, keep, send, whole
):
    inner, (rows, width) = hidden.shape[1], cotangent_a.shape
    slab, down_rows = inner // 2, inner // shards // 2
    for q in range(2):
        columns = slice(q * slab, (q + 1) * slab)
        whole[columns, :] = (
            mm_tn(hidden[:rows, columns], cotangent_a[...])
            + mm_tn(hidden[rows:, columns], pair_b[rows:, :])
        ).astype(LOW)
    for place, (other, relative) in enumerate(places_of(stages, shards)):
        target = (keep, send)[place // shards]
        part = side_of(where) ^ other
        source = aligned((where[1] ^ relative) * 2 * down_rows + part * down_rows, down_rows)
        for t in range(width // LANES):
            target[place % shards, t * down_rows : (t + 1) * down_rows, :] = whole[
                source, t * LANES : (t + 1) * LANES
            ]


def split_shards(shards, stages, where, whole, keep, send, by_tiles=False):
    shard_rows = whole.shape[0] // shards
    for place, (_, relative) in enumerate(places_of(stages, shards)):
        target = (keep, send)[place // (shards // 2)]
        source = aligned((where[1] ^ relative) * shard_rows, shard_rows)
        if by_tiles:
            for t in range(whole.shape[1] // LANES):
                target[place % (shards // 2), t * shard_rows : (t + 1) * shard_rows, :] = whole[
                    source, t * LANES : (t + 1) * LANES
                ]
        else:
            target[place % (shards // 2), :, :] = whole[source, :]


def score_grads(query, key, value, grad, offset, mask):
    scores = jnp.where(mask, mm_nt(query, key) + offset, NEG_FILL)
    expd = jnp.exp(scores - jnp.max(scores, axis=-1, keepdims=True))
    probs = expd * (1.0 / jnp.sum(expd, axis=-1, keepdims=True))
    d_probs = mm_nt(grad, value)
    weighted = jnp.sum(d_probs * probs, axis=-1, keepdims=True)
    d_scores = (probs * (d_probs - weighted)).astype(LOW)
    return (
        mm(d_scores, key),
        mm_tn(d_scores, query),
        mm_tn(probs.astype(LOW), grad),
        d_scores.astype(FULL),
    )


def fold_diagonals(flat):
    rows = flat.shape[0]
    folded = flat[:8, :]
    for base in range(8, rows, 8):
        folded = folded + pltpu.roll(flat[base : base + 8, :], 2 * rows - base, 1)
    return folded


def inside_grads_kernel(
    size,
    shards,
    stages,
    where,
    qkv,
    d_heads,
    heads_mine,
    heads_other,
    d_attn,
    row_starts,
    col_starts,
    bias,
    d_cols,
    d_bias,
    keep,
    send,
    d_out,
):
    rows, half = row_starts.shape[1], d_heads.shape[1]
    core = core_of(where)
    lane = lanes_at(core * half, half)
    value = mm_tn(heads_mine[...], d_attn[:, lane])
    d_out[aligned(core * half, half), :] = value.astype(LOW)
    value = mm_tn(heads_other[:rows, :], d_attn[rows:, lane])
    value = value + mm_tn(heads_other[rows:, :], d_attn[:rows, lane])
    d_out[aligned((1 - core) * half, half), :] = value.astype(LOW)
    split_shards(shards, stages, where, d_out, keep, send, by_tiles=True)
    masks, grads = [], []
    for stream in range(2):
        own_col = col_starts[:, 2 * stream : 2 * stream + 1]
        own_row = row_starts[3 * stream + 1 : 3 * stream + 2, :]
        settled = own_col != tail_of(row_starts, stream)
        masks.append((own_col == own_row) & settled)
        began = settled & (own_col >= ((where[0] ^ stream) * shards + where[1]) * rows)
        grad = d_heads[stream * rows : (stream + 1) * rows, :].astype(FULL)
        grads.append(jnp.where(began, grad, 0.0).astype(LOW))
    for pair in range(half // size // 2):
        outs = []
        for head in (2 * pair, 2 * pair + 1):
            near, _ = bias_tiles(bias[head : head + 1, :], rows)
            at = head * size
            flat = jnp.zeros((rows, rows), FULL)
            for stream in range(2):
                own = slice(2 * stream * rows, (2 * stream + 1) * rows)
                one = score_grads(
                    qkv[own, at : at + size],
                    qkv[own, half + at : half + at + size],
                    qkv[own, 2 * half + at : 2 * half + at + size],
                    grads[stream][:, at : at + size],
                    near,
                    masks[stream],
                )
                flat = flat + one[3]
                outs.append(one)
            flat = jnp.concatenate([flat, jnp.zeros((rows, rows), FULL)], axis=1)
            d_bias[8 * head : 8 * head + 8, :] = fold_diagonals(flat)
        for part in range(3):
            columns = slice(part * half + 2 * pair * size, part * half + (2 * pair + 2) * size)
            for stream in range(2):
                d_cols[stream * rows : (stream + 1) * rows, columns] = jnp.concatenate(
                    [outs[stream][part], outs[2 + stream][part]], axis=1
                ).astype(LOW)


def crossing_grads_kernel(
    shards,
    first_head,
    last_head,
    size,
    stages,
    where,
    qkv,
    normed,
    d_heads,
    d_after,
    d_inside,
    row_starts,
    col_starts,
    bias,
    d_cols,
    keep,
    send,
    d_bias,
    d_weights,
):
    rows, half = row_starts.shape[1], d_heads.shape[1]
    width = normed.shape[1]
    group = (last_head - first_head) * size
    span = slice(first_head * size, last_head * size)
    last_cols, masks, turns, mixes, grads = [], [], [], [], []
    for stream in range(2):
        tail = tail_of(row_starts, stream)
        own_col = col_starts[:, 2 * stream : 2 * stream + 1]
        after_col = col_starts[:, 2 * stream + 1 : 2 * stream + 2]
        own_row = row_starts[3 * stream + 1 : 3 * stream + 2, :]
        after_row = row_starts[3 * stream + 2 : 3 * stream + 3, :]
        is_last_col, is_last_row = own_col == tail, own_row == tail
        mix_col = jnp.where(is_last_col, own_col, after_col)
        mix_row = jnp.where(is_last_row, own_row, after_row)
        last_cols.append(is_last_col)
        masks.append((mix_col == tail) & (mix_row == tail))
        turns.append(is_last_col != is_last_row)
        base = 2 * stream * rows
        mix = []
        for part in range(3):
            columns = slice(part * half + first_head * size, part * half + last_head * size)
            mix.append(
                pick(
                    is_last_col,
                    qkv[base : base + rows, columns],
                    qkv[base + rows : base + 2 * rows, columns],
                )
            )
        mixes.append(mix)
        here = slice(stream * rows, (stream + 1) * rows)
        mixed = jnp.where(
            is_last_col, d_heads[here, span].astype(FULL), d_after[here, span].astype(FULL)
        )
        grads.append(jnp.where(mix_col == tail, mixed, 0.0).astype(LOW))
    for pair in range((last_head - first_head) // 2):
        outs = []
        for index in (2 * pair, 2 * pair + 1):
            head = first_head + index
            near, far = bias_tiles(bias[head : head + 1, :], rows)
            at = index * size
            kept, turned = jnp.zeros((rows, rows), FULL), jnp.zeros((rows, rows), FULL)
            for stream in range(2):
                mix = mixes[stream]
                two = score_grads(
                    mix[0][:, at : at + size],
                    mix[1][:, at : at + size],
                    mix[2][:, at : at + size],
                    grads[stream][:, at : at + size],
                    jnp.where(turns[stream], far, near),
                    masks[stream],
                )
                kept = kept + jnp.where(turns[stream], 0.0, two[3])
                turned = turned + jnp.where(turns[stream], two[3], 0.0)
                outs.append(two)
            d_bias[8 * index : 8 * index + 8, :] = fold_diagonals(
                jnp.concatenate([kept, turned], axis=1)
            )
        for part in range(3):
            columns = slice(part * group + 2 * pair * size, part * group + (2 * pair + 2) * size)
            for stream in range(2):
                d_cols[stream * rows : (stream + 1) * rows, columns] = jnp.concatenate(
                    [outs[stream][part], outs[2 + stream][part]], axis=1
                ).astype(LOW)
    total = [jnp.zeros((width, group), FULL) for _ in range(3)]
    for stream in range(2):
        base = 2 * stream * rows
        own, ahead = normed[base : base + rows, :], normed[base + rows : base + 2 * rows, :]
        normed_mix = pick(last_cols[stream], own, ahead)
        here = slice(stream * rows, (stream + 1) * rows)
        for part in range(3):
            inner = slice(part * half + first_head * size, part * half + last_head * size)
            total[part] = total[part] + mm_tn(own, d_inside[here, inner])
            total[part] = total[part] + mm_tn(
                normed_mix, d_cols[here, part * group : (part + 1) * group]
            )
    for part in range(3):
        d_weights[:, part * group : (part + 1) * group] = total[part].astype(LOW)
    split_shards(shards, stages, where, d_weights, keep, send)


def normed_grads_kernel(
    sizes, weights, d_inside, own_a, halo_a, pair_b, halo_b, row_starts, col_starts, *refs
):
    *crossing, keep, send, d_gain = refs
    rows, half = col_starts.shape[0], weights.shape[1] // 3
    inside = mm_nt(d_inside[...], weights[...])
    across = jnp.zeros(inside.shape, FULL)
    begin = 0
    for ref, group in zip(crossing, sizes, strict=True):
        for part in range(3):
            across = across + mm_nt(
                ref[:, part * group : (part + 1) * group],
                weights[:, part * half + begin : part * half + begin + group],
            )
        begin += group
    total = jnp.zeros((1, weights.shape[0]), FULL)
    streams = ((own_a, halo_a, keep), (pair_b, halo_b, send))
    for stream, (own, halo, target) in enumerate(streams):
        is_last = col_starts[:, 2 * stream : 2 * stream + 1] == tail_of(row_starts, stream)
        here = slice(stream * rows, (stream + 1) * rows)
        mine = jnp.where(is_last, across[here], inside[here])
        sent = jnp.where(is_last, 0.0, across[here])
        target[:rows, :] = mine.astype(target.dtype)
        target[rows:, :] = sent.astype(target.dtype)
        values, ahead = own[:rows, :].astype(FULL), halo[rows:, :].astype(FULL)
        share = mine * (values * inverse_rms(values)) + sent * (ahead * inverse_rms(ahead))
        total = total + jnp.sum(share, axis=0, keepdims=True)
    d_gain[...] = total


def tokens_kernel(own, gains, d_resid, d_own, d_before, out_keep, out_other, d_tokens, output):
    values = own[...].astype(FULL)
    grad = d_own[...] + d_before[...].astype(FULL)
    d_tokens[...] = d_resid[...] + norm_back(values, inverse_rms(values), gains[0:1, :], grad)
    output[...] = (out_keep[...] + out_other[...].astype(FULL)).astype(LOW)


def unpack_feed_kernel(tile_step, where, mine, other, d_gate, d_up, d_down, d_out):
    rows, half = d_out.shape[0], d_out.shape[1] // 2
    tiles, down_tiles = d_gate.shape[1] // (4 * LANES), d_down.shape[1] // LANES
    down_rows = d_down.shape[0] // 4
    begin = 0
    for relative in range(2):
        side = side_of(where) ^ relative
        for which, part in enumerate((mine, other)):
            core = core_of(where) ^ which
            at = begin
            target = aligned((2 * core + side) * down_rows, down_rows)
            for t in range(down_tiles):
                d_down[target, t * LANES : (t + 1) * LANES] = part[
                    at + t * down_rows : at + (t + 1) * down_rows, :
                ].astype(FULL)
            at += down_tiles * down_rows
            for matrix in (d_up, d_gate):
                for t in range(tiles):
                    lane = lanes_at(tile_step(core, side * tiles + t), LANES)
                    matrix[:, lane] = part[at + t * rows : at + (t + 1) * rows, :].astype(FULL)
                at += tiles * rows
        begin = at
    for which, part in enumerate((mine, other)):
        core = core_of(where) ^ which
        for t in range(half // LANES):
            first = begin + t * rows
            d_out[:, lanes_at(core * half + t * LANES, LANES)] = part[
                first : first + rows, :
            ].astype(FULL)


def unpack_attend_kernel(sizes, where, mine, other, d_query, d_key, d_value):
    half = d_query.shape[1] // 2
    for which, ref in enumerate((mine, other)):
        core = core_of(where) ^ which
        begin, column = 0, 0
        for group in sizes:
            for target in (d_query, d_key, d_value):
                target[:, lanes_at(core * half + begin, group)] = ref[
                    :, column : column + group
                ].astype(FULL)
                column += group
            begin += group


def shaped(shape, dtype):
    return jax.ShapeDtypeStruct(shape, dtype)


def per_device(
    tokens,
    cotangent,
    offsets,
    w_query,
    w_key,
    w_value,
    w_attn_out,
    w_gate,
    w_up,
    w_ff_out,
    gain_attn,
    gain_ff,
    rel_table,
):
    rows, width = tokens.shape
    shards = lax.axis_size("shard")
    shard, rep = lax.axis_index("shard"), lax.axis_index("rep")
    heads_count, table_rows = rel_table.shape[1], rel_table.shape[0]
    buckets = table_rows * shards
    shard_rows, inner = w_gate.shape
    half, size = width // 2, width // heads_count
    own_heads = heads_count // 2
    piece = w_ff_out.shape[0] // 2
    core = rep % 2
    where = jnp.stack([rep, shard]).astype(jnp.int32)

    starts_all = jnp.arange(offsets.shape[0], dtype=jnp.int32) - offsets
    start_pad = jnp.pad(starts_all, (rows, rows), constant_values=-1)
    first_a, first_b = (rep * shards + shard) * rows, ((rep ^ 1) * shards + shard) * rows
    window_a = lax.dynamic_slice_in_dim(start_pad, first_a, 3 * rows).reshape(3, rows)
    window_b = lax.dynamic_slice_in_dim(start_pad, first_b, 3 * rows).reshape(3, rows)
    row_starts = jnp.concatenate([window_a, window_b], axis=0)
    col_starts = jnp.stack([window_a[1], window_a[2], window_b[1], window_b[2]], axis=1)
    by_tiles = piece % LANES == 0

    def tile_step(which_core, tile):
        if by_tiles:
            per_shard = piece // LANES
            return ((tile // per_shard * 2 + which_core) * per_shard + tile % per_shard) * LANES
        return which_core * (inner // 2) + tile * LANES

    def by_core(matrix):
        if by_tiles:
            return matrix
        split = matrix.reshape(shard_rows, shards, 2, piece).transpose(0, 2, 1, 3)
        return split.reshape(shard_rows, inner)

    def from_core(matrix):
        if by_tiles:
            return matrix
        split = matrix.reshape(shard_rows, 2, shards, piece).transpose(0, 2, 1, 3)
        return split.reshape(shard_rows, inner)

    tiles = inner // (4 * LANES)
    down_block = width // LANES * (piece // 2)
    qkv_side = -(-3 * half // (2 * LANES)) * LANES
    steps = Sequence(jnp.zeros((8, LANES), FULL))
    qkv_own, ff_own, rest_own = steps.call(
        functools.partial(pack_kernel, tile_step),
        (where,),
        (
            w_query,
            w_key,
            w_value,
            w_attn_out,
            by_core(w_gate),
            by_core(w_up),
            w_ff_out,
            gain_attn.reshape(1, shard_rows),
            gain_ff.reshape(1, shard_rows),
            rel_table,
        ),
        (
            shaped((shard_rows + SMALL, qkv_side), LOW),
            shaped((2 * tiles * shard_rows, LANES), LOW),
            shaped((2 * piece + shard_rows, half), LOW),
        ),
        room=58,
    )
    onehot = np.zeros((shards, SMALL, 2 * rows), np.float32)
    onehot[:, 2 : 2 + table_rows] = bucket_onehot(2 * rows, buckets).T.reshape(
        shards, table_rows, 2 * rows
    )
    onehot = jnp.asarray(onehot.reshape(shards * SMALL, 2 * rows), LOW)


    up = [(i, i + 1) for i in range(shards - 1)]
    down = [(i + 1, i) for i in range(shards - 1)]
    by_x, by_core = (("rep", 1),), ("rep", 0)
    far, near = far_first(shards), near_first(shards)

    def joined(*parts, axis=0):
        return jnp.concatenate(parts, axis=axis)

    pair = joined(tokens, cotangent)
    received, pair_b = steps.send(qkv_own, ("shard", far[0])), steps.send(pair, by_core)
    steps.mark()
    qkv_near, pair_b = joined(qkv_own, steps.take(received)), steps.take(pair_b)
    shifted = steps.take(tokens)
    ff_received = steps.send(steps.take(ff_own), ("shard", far[0]))
    rest_received = steps.send(steps.take(rest_own), ("shard", far[0]))
    before, ahead = lax.ppermute(shifted, "shard", up), lax.ppermute(shifted, "shard", down)
    for bit in far[1:-1]:
        received = steps.send(qkv_near, ("shard", bit))
        steps.mark()
        qkv_near = joined(qkv_near, steps.take(received))
    qkv_far, qkv_side = steps.send(qkv_near, ("shard", far[-1])), steps.send(qkv_near, by_x[0])
    ff_near = joined(ff_own, steps.take(ff_received))
    ff_received = steps.send(ff_near, ("shard", far[1]))
    steps.mark()
    halo = joined(steps.take(before), steps.take(ahead))
    halo_b = steps.send(halo, by_core)
    rest_near = joined(rest_own, steps.take(rest_received))
    rest_received = steps.send(rest_near, ("shard", far[1]))
    steps.mark()
    qkv_far, qkv_side = steps.take(qkv_far), steps.take(qkv_side)
    qkv_other = steps.send(qkv_far, by_x[0])
    ff_near = joined(ff_near, steps.take(ff_received))
    halo_b = steps.take(halo_b)
    for bit in far[2:-1]:
        ff_received = steps.send(ff_near, ("shard", bit))
        rest_near = joined(rest_near, steps.take(rest_received))
        rest_received = steps.send(rest_near, ("shard", bit))
        steps.mark()
        ff_near = joined(ff_near, steps.take(ff_received))
    ff_far, ff_side = steps.send(ff_near, ("shard", far[-1])), steps.send(ff_near, by_x[0])
    steps.mark()
    rest_near = joined(rest_near, steps.take(rest_received))
    rest_far = steps.send(rest_near, ("shard", far[-1]))
    qkv_other = steps.take(qkv_other)
    heads, normed, qkv, w_qkv, gains, bias = steps.call(
        functools.partial(attend_kernel, shards, size),
        (where,),
        (
            tokens,
            halo,
            pair_b,
            halo_b,
            qkv_near,
            qkv_far,
            qkv_side,
            qkv_other,
            row_starts,
            col_starts,
            onehot,
        ),
        (
            shaped((2 * rows, half), LOW),
            shaped((4 * rows, width), LOW),
            shaped((4 * rows, 3 * half), LOW),
            shaped((width, 3 * half), LOW),
            shaped((SMALL, width), FULL),
            shaped((8, 2 * rows), FULL),
        ),
        [pltpu.VMEM((rows, 2 * half), LOW), pltpu.VMEM((shards * SMALL, LANES), FULL)],
        micros=12,
    )
    heads_other, rest_near_b = steps.send(heads, by_core), steps.send(rest_near, by_core)
    ff_far, ff_side = steps.take(ff_far), steps.take(ff_side)
    ff_other = steps.send(steps.take(ff_far), by_x[0])
    steps.mark()
    heads_other, rest_near_b = steps.take(heads_other), steps.take(rest_near_b)
    rest_far = steps.take(rest_far)
    rest_far_b = steps.send(rest_far, by_core)
    steps.mark()
    ff_other, rest_far_b = steps.take(ff_other), steps.take(rest_far_b)
    wide = shaped((2 * rows, inner // 2), LOW)
    (
        out_keep,
        out_send,
        d_normed_keep,
        d_normed_send,
        resid,
        normed_ff,
        hidden,
        d_gate,
        d_linear,
        w_out,
    ) = steps.call(
        functools.partial(feed_kernel, shards),
        (where,),
        (
            heads,
            heads_other,
            tokens,
            cotangent,
            pair_b,
            gains,
            rest_near,
            rest_far,
            rest_near_b,
            rest_far_b,
            ff_near,
            ff_far,
            ff_side,
            ff_other,
        ),
        (
            shaped((rows, width), FULL),
            shaped((rows, width), LOW),
            shaped((2 * rows, width), FULL),
            shaped((2 * rows, width), LOW),
            shaped((2 * rows, width), FULL),
            shaped((2 * rows, width), LOW),
            wide,
            wide,
            wide,
            shaped((width, width), LOW),
        ),
        [
            pltpu.VMEM((width, inner // 2), LOW),
            pltpu.VMEM((width, inner // 2), LOW),
            pltpu.VMEM((inner // 2, width), LOW),
        ],
        micros=400,
    )
    d_normed_other, out_other = swap(d_normed_send, *by_core), swap(out_send, *by_core)
    slices = shaped((shards, tiles * shard_rows, LANES), LOW)
    down_slices = shaped((shards, down_block, LANES), LOW)
    by_near = tuple(("shard", bit) for bit in near)
    down_stages = by_x + by_near
    gate_stages = by_near[:1] + by_x + by_near[1:]
    up_stages = by_x + by_near[1:2] + by_near[:1] + by_near[2:]
    down_keep, down_send = steps.call(
        functools.partial(down_grads_kernel, shards, down_stages),
        (where,),
        (hidden, cotangent, pair_b),
        (down_slices, down_slices),
        [pltpu.VMEM((inner // 2, width), LOW)],
        micros=4,
    )
    down_received = exchange(down_send, down_stages[0])
    d_normed_other, out_other = steps.take(d_normed_other), steps.take(out_other)
    d_resid, d_attn, d_heads, d_gain_two = steps.call(
        resid_grads_kernel,
        (where,),
        (d_normed_keep, d_normed_other, resid, cotangent, pair_b, gains, w_out),
        (
            shaped((rows, width), FULL),
            shaped((2 * rows, width), LOW),
            shaped((2 * rows, half), LOW),
            shaped((1, width), FULL),
        ),
        micros=5,
    )
    d_heads_after = lax.ppermute(d_heads, "shard", down)
    gate_keep, gate_send = steps.call(
        functools.partial(wide_grads_kernel, shards, gate_stages),
        (where,),
        (normed_ff, d_gate),
        (slices, slices),
        [pltpu.VMEM((2, width, inner // 4), LOW)],
        micros=4,
    )
    gate_received = exchange(gate_send, gate_stages[0])
    up_keep, up_send = steps.call(
        functools.partial(wide_grads_kernel, shards, up_stages),
        (where,),
        (normed_ff, d_linear),
        (slices, slices),
        [pltpu.VMEM((2, width, inner // 4), LOW)],
        micros=4,
    )
    up_received = exchange(up_send, up_stages[0])
    out_slices = shaped((shards // 2, shard_rows * half // LANES, LANES), LOW)
    d_inside, d_bias, o_keep, o_send = steps.call(
        functools.partial(inside_grads_kernel, size, shards, by_near),
        (where,),
        (qkv, d_heads, heads, heads_other, d_attn, row_starts, col_starts, bias),
        (
            shaped((2 * rows, 3 * half), LOW),
            shaped((8 * own_heads, 2 * rows), FULL),
            out_slices,
            out_slices,
        ),
        [pltpu.VMEM((width, half), LOW)],
        micros=11,
    )

    d_down, down_received = steps.send_half(steps.add(down_keep, down_received), down_stages[1])
    o_received = steps.send(o_send, by_near[0])
    d_heads_after = steps.take(d_heads_after)
    sizes = [count * size for count in GROUPS]

    def crossing_grads(first, count):
        attn_slices = shaped((shards // 2, shard_rows, 3 * count * size), LOW)
        return steps.call(
            functools.partial(
                crossing_grads_kernel, shards, first, first + count, size, by_near
            ),
            (where,),
            (qkv, normed, d_heads, d_heads_after, d_inside, row_starts, col_starts, bias),
            (
                shaped((2 * rows, 3 * count * size), LOW),
                attn_slices,
                attn_slices,
                shaped((8 * count, 2 * rows), FULL),
            ),
            [pltpu.VMEM((width, 3 * count * size), LOW)],
            micros=12 if not first else 400,
            room=58,
        )

    cols_one, one_keep, one_send, d_bias_one = crossing_grads(0, GROUPS[0])
    one_received = steps.send(one_send, by_near[0])
    d_gate, gate_received = steps.send_half(steps.add(gate_keep, gate_received), gate_stages[1])
    d_up, up_received = steps.send_half(steps.add(up_keep, up_received), up_stages[1])
    d_down, down_received = steps.send_half(steps.add(d_down, down_received), down_stages[2])
    cols_two, two_keep, two_send, d_bias_two = crossing_grads(GROUPS[0], GROUPS[1])
    d_out = steps.add(o_keep, o_received)
    two_received = steps.send(two_send, by_near[0])
    d_gate = joined(steps.add(d_gate, gate_received), d_out, axis=1)
    d_gate, gate_received = steps.send_half(d_gate, by_near[1])
    d_down, down_received = steps.send_half(steps.add(d_down, down_received), down_stages[3])
    d_up, up_received = steps.send_half(steps.add(d_up, up_received), up_stages[2])
    keep, send, d_gain_one = steps.call(
        functools.partial(normed_grads_kernel, tuple(sizes)),
        (),
        (
            w_qkv,
            d_inside,
            tokens,
            halo,
            pair_b,
            halo_b,
            row_starts,
            col_starts,
            cols_one,
            cols_two,
        ),
        (
            shaped((2 * rows, width), FULL),
            shaped((2 * rows, width), LOW),
            shaped((1, width), FULL),
        ),
        micros=400,
        room=58,
    )
    folds = np.stack([np.roll(bucket_onehot(2 * rows, buckets), row, axis=0) for row in range(8)])
    d_bias = d_bias + jnp.concatenate([d_bias_one, d_bias_two], axis=0)
    d_bias = d_bias.reshape(own_heads, 16 * rows)
    d_table = lax.dot_general(
        d_bias,
        jnp.asarray(folds.reshape(16 * rows, buckets)),
        (((1,), (0,)), ((), ())),
        precision=lax.Precision.HIGHEST,
    )
    d_table = lax.dynamic_update_slice(
        jnp.zeros((heads_count, buckets), FULL), d_table, (core * own_heads, 0)
    ).T
    smalls = jnp.concatenate([d_gain_one.reshape(-1), d_gain_two.reshape(-1), d_table.reshape(-1)])
    rest = -smalls.shape[0] % (8 * LANES)
    smalls = jnp.pad(smalls, (0, rest)).reshape(-1, LANES)
    small_stages = [("rep", bit) for bit in range(bits_of(lax.axis_size("rep")))] + list(by_near)
    attn = joined(
        steps.add(one_keep, one_received), steps.add(two_keep, two_received), axis=2
    )
    attn, attn_received = steps.send_half(attn, by_near[1])
    d_own_received = exchange(send, by_core)
    d_gate = joined(steps.add(d_up, up_received), steps.add(d_gate, gate_received), axis=1)
    d_gate, gate_received = steps.send_half(d_gate, by_near[2])
    small_received = steps.send(smalls, small_stages[0])
    d_down = steps.add(d_down, down_received)
    steps.mark()
    d_own = keep + steps.take(d_own_received).astype(FULL)
    d_before = lax.ppermute(d_own[rows:].astype(LOW), "shard", up)
    smalls = smalls + steps.take(small_received)
    small_received = steps.send(smalls, small_stages[1])
    steps.mark(d_own)
    attn, attn_received = steps.send_half(steps.add(attn, attn_received), by_near[2])
    d_gate = steps.add(d_gate, gate_received)
    for stage in by_near[3:]:
        attn = steps.add(attn, attn_received)
        attn, attn_received = steps.send_half(attn, stage)
        d_gate, gate_received = steps.send_half(d_gate, stage)
        d_gate = steps.add(d_gate, gate_received)
        d_down, down_received = steps.send_half(d_down, stage)
        d_down = steps.add(d_down, down_received)
    wide = tiles * shard_rows
    d_feed, d_out = joined(d_down[0], d_gate[0, : 2 * wide]), d_gate[0, 2 * wide :]
    for bit in range(2, bits_of(lax.axis_size("rep"))):
        d_feed = steps.add(d_feed, exchange(d_feed, ("rep", bit)))
        d_out = steps.add(d_out, exchange(d_out, ("rep", bit)))
    feed_received = steps.send(joined(d_feed, d_out), by_x[0])
    smalls = smalls + steps.take(small_received)
    small_received = steps.send(smalls, small_stages[2])
    steps.mark()
    attn = steps.add(attn, attn_received)[0]
    for bit in range(2, bits_of(lax.axis_size("rep"))):
        attn = steps.add(attn, exchange(attn, ("rep", bit)))
    attn_received = steps.send(attn, by_x[0])
    smalls = smalls + steps.take(small_received)
    small_received = steps.send(smalls, small_stages[3])
    feed_received = steps.take(feed_received)
    feed = d_feed.shape[0]
    d_feed = joined(d_feed, feed_received[:feed], add_low(d_out, feed_received[feed:]))
    feed_other = steps.send(d_feed, by_core)
    d_tokens, output = steps.call(
        tokens_kernel,
        (),
        (tokens, gains, d_resid, d_own[:rows], steps.take(d_before), out_keep, out_other),
        (shaped((rows, width), FULL), shaped((rows, width), LOW)),
        micros=400,
    )
    attn = steps.add(attn, attn_received)
    attn_other = steps.send(attn, by_core)
    feed_other = steps.take(feed_other)
    for stage in small_stages[4:]:
        smalls = smalls + steps.take(small_received)
        small_received = steps.send(smalls, stage)
    d_w_gate, d_w_up, d_w_ff_out, d_w_attn_out = steps.call(
        functools.partial(unpack_feed_kernel, tile_step),
        (where,),
        (d_feed, feed_other),
        (
            shaped(w_gate.shape, FULL),
            shaped(w_up.shape, FULL),
            shaped(w_ff_out.shape, FULL),
            shaped(w_attn_out.shape, FULL),
        ),
        micros=400,
    )
    attn_other = steps.take(attn_other)
    smalls = (smalls + steps.take(small_received)).reshape(-1)
    d_w_query, d_w_key, d_w_value = steps.call(
        functools.partial(unpack_attend_kernel, tuple(sizes)),
        (where,),
        (attn, attn_other),
        (shaped(w_query.shape, FULL),) * 3,
        micros=400,
    )

    def own_part(begin, length):
        return lax.dynamic_slice_in_dim(smalls, begin + shard * length, length)

    return (
        output,
        d_tokens,
        d_w_query,
        d_w_key,
        d_w_value,
        d_w_attn_out,
        from_core(d_w_gate),
        from_core(d_w_up),
        d_w_ff_out,
        own_part(0, shard_rows),
        own_part(width, shard_rows),
        own_part(2 * width, table_rows * heads_count).reshape(table_rows, heads_count),
    )


def solution(mesh):
    tokens_spec, rows_spec, line_spec = P(("rep", "shard"), None), P("shard", None), P("shard")
    return jax.shard_map(
        per_device,
        mesh=mesh,
        in_specs=(tokens_spec, tokens_spec, P()) + (rows_spec,) * 7 + (line_spec,) * 2 + (rows_spec,),
        out_specs=(tokens_spec,) * 2 + (rows_spec,) * 7 + (line_spec,) * 2 + (rows_spec,),
        check_vma=False,
    )
```

```python
import functools

import jax
import jax.numpy as jnp
import numpy as np
from jax import lax
from jax.experimental import pallas as pl
from jax.experimental.pallas import tpu as pltpu
from jax.sharding import PartitionSpec as P

NEG_FILL = -1e30
EPSILON = 1e-06
BORDERS = (1, 2, 3, 4, 5, 6, 7, 8, 12, 16, 23, 32, 46, 64, 91)
LANES = 128
SMALL = 8
SCALE = 2 * 10**8
GROUPS = (4, 2)
LOW = jnp.bfloat16
FULL = jnp.float32
GELU_A = float(np.sqrt(2.0 / np.pi))
GELU_B = 0.044715


def bits_of(count):
    return count.bit_length() - 1


def swap(block, axis, bit):
    count = lax.axis_size(axis)
    return lax.ppermute(block, axis, [(i, i ^ (1 << bit)) for i in range(count)])


def add_low(left, right):
    return (left.astype(FULL) + right.astype(FULL)).astype(LOW)


def gather_shards(block):
    for bit in far_first(lax.axis_size("shard")):
        block = jnp.concatenate([block, swap(block, "shard", bit)], axis=0)
    return block


def reverse_bits(value, count):
    result = 0
    for bit in range(bits_of(count)):
        result = result | (((value >> bit) & 1) << (bits_of(count) - 1 - bit))
    return result


def far_first(shards):
    return tuple(reversed(range(bits_of(shards))))


def near_first(shards):
    return tuple(range(bits_of(shards)))


def shards_at(shard, shards, order):
    places = []
    for place in range(shards):
        moved = sum(((place >> step) & 1) << bit for step, bit in enumerate(order))
        places.append(shard ^ moved)
    return places


def exchange(block, stage):
    return swap(block, *stage)


def places_of(stages, shards):
    places = []
    for place in range(2 ** len(stages)):
        side, shard = 0, 0
        for step, (axis, bit) in enumerate(stages):
            here = (place >> (len(stages) - 1 - step)) & 1
            if axis == "rep":
                side |= here
            else:
                shard |= here << bit
        places.append((side, shard))
    return places


def mark_kernel():
    pass


class Sequence:
    def __init__(self, token):
        self.token, self.sent = token, []

    def send(self, block, stage):
        self.sent.append(block)
        return exchange(block, stage)

    def send_half(self, blocks, stage):
        kept, sent = halves_of(blocks)
        return kept, self.send(sent, stage)

    def take(self, received):
        received, self.token = lax.optimization_barrier((received, self.token))
        return received

    def add(self, kept, received):
        return add_low(kept, self.take(received))

    def mark(self, *ready, micros=500):
        self.call(None, (), (), (), waits=ready, micros=micros)

    def call(self, kernel, scalars, arrays, outs, scratch=(), micros=3, waits=(), room=4):
        held = [(a.size, a.dtype) for a in (*arrays, *outs)]
        held += [(int(np.prod(a.shape)), a.dtype) for a in scratch]
        needed = sum(size * jnp.dtype(dtype).itemsize for size, dtype in held)
        waits, self.sent = (*waits, *self.sent), []
        skip, given = 1 + len(waits), 1 + len(waits) + len(scalars) + len(arrays) + len(outs)

        def body(*refs):
            if kernel is not None:
                kernel(*refs[skip:given], *refs[given + 1 :])

        def placed(arrays, space):
            return [pl.BlockSpec(memory_space=space) for _ in arrays]

        *results, self.token = pl.pallas_call(
            body,
            out_shape=(*outs, shaped(self.token.shape, self.token.dtype)),
            in_specs=placed((self.token, *waits), pl.ANY)
            + placed(scalars, pltpu.SMEM)
            + placed(arrays, pltpu.VMEM),
            out_specs=(*placed(outs, pltpu.VMEM), pl.BlockSpec(memory_space=pl.ANY)),
            scratch_shapes=scratch,
            input_output_aliases={0: len(outs)},
            compiler_params=pltpu.CompilerParams(vmem_limit_bytes=min(needed + room * 2**20, 58 * 2**20)),
            cost_estimate=pl.CostEstimate(
                flops=int(micros * SCALE), bytes_accessed=10**6, transcendentals=0
            ),
            name=getattr(kernel, "func", kernel or mark_kernel).__name__,
        )(self.token, *waits, *scalars, *arrays)
        return results


def halves_of(blocks):
    half = blocks.shape[0] // 2
    return blocks[:half], blocks[half:]


def sum_replicas(block, first_bit):
    for bit in range(first_bit, bits_of(lax.axis_size("rep"))):
        block = add_low(block, swap(block, "rep", bit))
    return block


def bucket_onehot(period, buckets):
    index = np.arange(period)
    relative = np.where(index < period // 2, index, index - period)
    distance = np.abs(relative)
    bucket = buckets // 2 * (relative > 0).astype(np.int64)
    for border in BORDERS:
        bucket = bucket + (distance >= border).astype(np.int64)
    return (bucket[:, None] == np.arange(buckets)[None, :]).astype(np.float32)


def mm(left, right):
    return lax.dot_general(left, right, (((1,), (0,)), ((), ())), preferred_element_type=FULL)


def mm_nt(left, right):
    return lax.dot_general(left, right, (((1,), (1,)), ((), ())), preferred_element_type=FULL)


def mm_tn(left, right):
    return lax.dot_general(left, right, (((0,), (0,)), ((), ())), preferred_element_type=FULL)


def inverse_rms(values):
    return lax.rsqrt(jnp.mean(values * values, axis=-1, keepdims=True) + EPSILON)


def norm_back(values, scale, gain, grad):
    inner = jnp.mean(gain * grad * values, axis=-1, keepdims=True)
    return scale * gain * grad - values * (scale * scale * scale * inner)


def pick(mask, left, right):
    return jnp.where(mask, left.astype(FULL), right.astype(FULL)).astype(left.dtype)


def aligned(index, size):
    return pl.ds(pl.multiple_of(index, 8), size)


def lanes_at(index, size):
    return pl.ds(pl.multiple_of(index, LANES), size)


def bias_tiles(bias_row, rows):
    rolled = pltpu.roll(
        jnp.broadcast_to(bias_row, (rows, 2 * rows)), 0, 1, stride=1, stride_axis=0
    )
    return rolled[:, :rows], rolled[:, rows:]


def core_of(where):
    return where[0] & 1


def side_of(where):
    return (where[0] >> 1) & 1


def tail_of(row_starts, stream):
    rows = row_starts.shape[1]
    return row_starts[3 * stream + 1 : 3 * stream + 2, rows - 1 : rows]


def pack_kernel(
    tile_step,
    where,
    w_query,
    w_key,
    w_value,
    w_out,
    w_gate,
    w_up,
    w_down,
    gain_one,
    gain_two,
    table,
    qkv,
    feed,
    rest,
):
    core, side = core_of(where), side_of(where)
    rows, half = w_query.shape[0], w_query.shape[1] // 2
    tiles = w_gate.shape[1] // (4 * LANES)
    width = qkv.shape[1]
    qkv[rows:, :] = jnp.zeros((SMALL, width), LOW)
    for which in range(2):

        @pl.when(side == which)
        def _():
            for t in range(width // LANES):
                part, tile = divmod(which * (3 * half - width) // LANES + t, half // LANES)
                qkv[:rows, t * LANES : (t + 1) * LANES] = (w_query, w_key, w_value)[part][
                    :, lanes_at(core * half + tile * LANES, LANES)
                ]

    qkv[rows : rows + 1, :rows] = gain_one[...]
    qkv[rows + 1 : rows + 2, :rows] = gain_two[...]
    qkv[rows + 2 : rows + 2 + table.shape[0], : table.shape[1]] = table[...]
    for which, ref in enumerate((w_gate, w_up)):
        for t in range(tiles):
            lane = tile_step(core, side * tiles + t)
            first = (which * tiles + t) * rows
            feed[first : first + rows, :] = ref[:, lanes_at(lane, LANES)]
    down_rows = w_down.shape[0] // 2
    own = aligned(core * down_rows, down_rows)
    rest[:down_rows, :] = w_down[own, :half]
    rest[down_rows : 2 * down_rows, :] = w_down[own, half:]
    rest[2 * down_rows :, :] = w_out[:, lanes_at(core * half, half)]


def attend_kernel(
    shards,
    size,
    where,
    own_a,
    halo_a,
    pair_b,
    halo_b,
    part_0,
    part_1,
    part_2,
    part_3,
    row_starts,
    col_starts,
    onehot,
    heads,
    normed,
    qkv,
    weights,
    gains,
    bias,
    kv_before,
    smalls,
):
    rows, width = own_a.shape
    shard_rows, half = width // shards, weights.shape[1] // 3
    block = shard_rows + SMALL
    for index, shard in enumerate(shards_at(where[1], shards, far_first(shards))):
        upper, first = index // (shards // 2), index % (shards // 2) * block
        for other, sources in enumerate(((part_0, part_1), (part_2, part_3))):
            source = sources[upper]
            lane = (side_of(where) ^ other) * (weights.shape[1] - source.shape[1])
            weights[
                aligned(shard * shard_rows, shard_rows), lanes_at(lane, source.shape[1])
            ] = source[first : first + shard_rows, :]
        source = (part_0, part_1)[upper]
        smalls[aligned(shard * SMALL, SMALL), :] = source[
            first + shard_rows : first + block, :LANES
        ].astype(FULL)
    total = jnp.zeros((SMALL, width), FULL)
    for shard in range(shards):
        line = jnp.concatenate(
            [
                smalls[shard * SMALL : (shard + 1) * SMALL, :],
                jnp.zeros((SMALL, width - LANES), FULL),
            ],
            axis=1,
        )
        total = total + (pltpu.roll(line, shard * shard_rows, 1) if shard else line)
    gains[...] = total
    gain = total[0:1, :]
    heads_here = half // size
    shift = jnp.where(core_of(where) == 0, 0, LANES - heads_here)
    table = pltpu.roll(smalls[...], shift, 1).astype(LOW)
    bias[...] = mm_tn(table, onehot[...])[: bias.shape[0], :]
    for stream, (own_ref, halo) in enumerate(((own_a, halo_a), (pair_b, halo_b))):
        base = 2 * stream * rows
        lines = []
        for tokens in (halo[:rows, :], own_ref[:rows, :], halo[rows:, :]):
            values = tokens.astype(FULL)
            lines.append((values * inverse_rms(values) * gain).astype(LOW))
        normed[base : base + rows, :] = lines[1]
        normed[base + rows : base + 2 * rows, :] = lines[2]
        for part in range(3):
            columns = slice(part * half, (part + 1) * half)
            qkv[base : base + 2 * rows, columns] = mm(
                normed[base : base + 2 * rows, :], weights[:, columns]
            ).astype(LOW)
            if part:
                kv_before[:, (part - 1) * half : part * half] = mm(
                    lines[0], weights[:, columns]
                ).astype(LOW)
        own_col = col_starts[:, 2 * stream : 2 * stream + 1]
        in_before = own_col == row_starts[3 * stream : 3 * stream + 1, :]
        in_own = own_col == row_starts[3 * stream + 1 : 3 * stream + 2, :]
        in_after = own_col == row_starts[3 * stream + 2 : 3 * stream + 3, :]
        allowed = in_own | in_before | in_after
        own, ahead = slice(base, base + rows), slice(base + rows, base + 2 * rows)
        for pair in range(half // size // 2):
            mixed = []
            for head in (2 * pair, 2 * pair + 1):
                at = head * size
                query = qkv[own, at : at + size]
                keys = slice(half + at, half + at + size)
                values = slice(2 * half + at, 2 * half + at + size)
                near, far = bias_tiles(bias[head : head + 1, :], rows)
                scores = jnp.where(
                    in_own,
                    mm_nt(query, qkv[own, keys]) + near,
                    jnp.where(
                        in_before,
                        mm_nt(query, kv_before[:, at : at + size]),
                        mm_nt(query, qkv[ahead, keys]),
                    )
                    + far,
                )
                scores = jnp.where(allowed, scores, NEG_FILL)
                expd = jnp.exp(scores - jnp.max(scores, axis=-1, keepdims=True))
                probs = expd * (1.0 / jnp.sum(expd, axis=-1, keepdims=True))
                total = mm(jnp.where(in_own, probs, 0.0).astype(LOW), qkv[own, values])
                total = total + mm(
                    jnp.where(in_before, probs, 0.0).astype(LOW),
                    kv_before[:, half + at : half + at + size],
                )
                total = total + mm(
                    jnp.where(in_after, probs, 0.0).astype(LOW), qkv[ahead, values]
                )
                mixed.append(total)
            heads[stream * rows : (stream + 1) * rows, 2 * pair * size : (2 * pair + 2) * size] = (
                jnp.concatenate(mixed, axis=1).astype(LOW)
            )


def feed_kernel(
    shards,
    where,
    heads_mine,
    heads_other,
    tokens_a,
    cotangent_a,
    pair_b,
    gains,
    rest_0,
    rest_1,
    rest_2,
    rest_3,
    part_0,
    part_1,
    part_2,
    part_3,
    out_keep,
    out_send,
    d_keep,
    d_send,
    resid,
    normed_ff,
    hidden,
    d_gate,
    d_linear,
    w_out,
    w_gate,
    w_up,
    w_down,
):
    rows, width = tokens_a.shape
    inner = w_gate.shape[1]
    shard_rows, down_rows = width // shards, inner // shards
    slab, half = inner // 2, width // 2
    tiles = slab // LANES
    block = 2 * tiles * shard_rows
    core, side = core_of(where), side_of(where)
    for index, shard in enumerate(shards_at(where[1], shards, far_first(shards))):
        upper, first = divmod(index, shards // 2)
        target = aligned(shard * shard_rows, shard_rows)
        for other, sources in enumerate(((part_0, part_1), (part_2, part_3))):
            part, start = sources[upper], first * block
            for t in range(tiles):
                lane = lanes_at((side ^ other) * slab + t * LANES, LANES)
                at = start + t * shard_rows
                w_gate[target, lane] = part[at : at + shard_rows, :]
                at = start + (tiles + t) * shard_rows
                w_up[target, lane] = part[at : at + shard_rows, :]
        rest, start = (rest_0, rest_1)[upper], first * (2 * down_rows + shard_rows)
        down = aligned(shard * down_rows, down_rows)
        w_down[down, :half] = rest[start : start + down_rows, :]
        w_down[down, half:] = rest[start + down_rows : start + 2 * down_rows, :]
        for other, sources in enumerate(((rest_0, rest_1), (rest_2, rest_3))):
            at = start + 2 * down_rows
            w_out[target, lanes_at((core ^ other) * half, half)] = sources[upper][
                at : at + shard_rows, :
            ]
    gain = gains[1:2, :]
    mine = mm(heads_mine[...], w_out[aligned(core * half, half), :])
    other = mm(heads_other[...], w_out[aligned((1 - core) * half, half), :])
    cotangents = (cotangent_a[...], pair_b[rows:, :])
    for stream, tokens in enumerate((tokens_a[...], pair_b[:rows, :])):
        span, back = slice(stream * rows, (stream + 1) * rows), slice((1 - stream) * rows, (2 - stream) * rows)
        value = tokens.astype(FULL) + (mine[span] + other[back])
        resid[span, :] = value
        normed_ff[span, :] = (value * inverse_rms(value) * gain).astype(LOW)
    for q in range(2):
        columns = slice(q * slab, (q + 1) * slab)
        for stream, cotangent in enumerate(cotangents):
            span = slice(stream * rows, (stream + 1) * rows)
            gate = mm(normed_ff[span, :], w_gate[:, columns])
            linear = mm(normed_ff[span, :], w_up[:, columns])
            d_hidden = mm_nt(cotangent, w_down[columns, :])
            square = gate * gate
            tanh = jnp.tanh(GELU_A * (gate + GELU_B * square * gate))
            rise = 0.5 * (1.0 + tanh)
            gelu = gate * rise
            slope = rise + 0.5 * gate * (1.0 - tanh * tanh) * (
                GELU_A * (1.0 + 3.0 * GELU_B * square)
            )
            hidden[span, columns] = (gelu * linear).astype(LOW)
            d_gate[span, columns] = (d_hidden * linear * slope).astype(LOW)
            d_linear[span, columns] = (d_hidden * gelu).astype(LOW)
    d_normed = mm_nt(d_gate[...], w_gate[...]) + mm_nt(d_linear[...], w_up[...])
    d_keep[...] = d_normed
    d_send[...] = d_normed.astype(LOW)
    out_keep[...] = resid[:rows, :] + mm(hidden[:rows, :], w_down[...])
    out_send[...] = mm(hidden[rows:, :], w_down[...]).astype(LOW)


def resid_grads_kernel(
    where,
    d_keep,
    d_other,
    resid,
    cotangent_a,
    pair_b,
    gains,
    w_out,
    d_resid,
    d_attn,
    d_heads,
    d_gain,
):
    rows, width = cotangent_a.shape
    half = width // 2
    for stream, cotangent in enumerate((cotangent_a[...], pair_b[rows:, :])):
        span, back = slice(stream * rows, (stream + 1) * rows), slice((1 - stream) * rows, (2 - stream) * rows)
        d_normed = d_keep[span, :] + d_other[back, :].astype(FULL)
        values = resid[span, :]
        scale = inverse_rms(values)
        grad = cotangent.astype(FULL) + norm_back(values, scale, gains[1:2, :], d_normed)
        d_attn[span, :] = grad.astype(LOW)
        if stream == 0:
            d_resid[...] = grad
            d_gain[...] = jnp.sum(d_normed * values * scale, axis=0, keepdims=True)
    d_heads[...] = mm_nt(d_attn[...], w_out[aligned(core_of(where) * half, half), :]).astype(LOW)


def wide_grads_kernel(shards, stages, where, normed_ff, grad, keep, send, whole):
    width, slab = normed_ff.shape[1], grad.shape[1] // 2
    shard_rows = width // shards
    for other in range(2):
        part = side_of(where) ^ other
        whole[other, :, :] = mm_tn(normed_ff[...], grad[:, lanes_at(part * slab, slab)]).astype(LOW)
    for place, (other, relative) in enumerate(places_of(stages, shards)):
        target = (keep, send)[place // shards]
        source = aligned((where[1] ^ relative) * shard_rows, shard_rows)
        for t in range(slab // LANES):
            target[place % shards, t * shard_rows : (t + 1) * shard_rows, :] = whole[
                other, source, t * LANES : (t + 1) * LANES
            ]


def down_grads_kernel(
    shards, stages, where, hidden, cotangent_a, pair_b, keep, send, whole
):
    inner, (rows, width) = hidden.shape[1], cotangent_a.shape
    slab, down_rows = inner // 2, inner // shards // 2
    for q in range(2):
        columns = slice(q * slab, (q + 1) * slab)
        whole[columns, :] = (
            mm_tn(hidden[:rows, columns], cotangent_a[...])
            + mm_tn(hidden[rows:, columns], pair_b[rows:, :])
        ).astype(LOW)
    for place, (other, relative) in enumerate(places_of(stages, shards)):
        target = (keep, send)[place // shards]
        part = side_of(where) ^ other
        source = aligned((where[1] ^ relative) * 2 * down_rows + part * down_rows, down_rows)
        for t in range(width // LANES):
            target[place % shards, t * down_rows : (t + 1) * down_rows, :] = whole[
                source, t * LANES : (t + 1) * LANES
            ]


def split_shards(shards, stages, where, whole, keep, send, by_tiles=False):
    shard_rows = whole.shape[0] // shards
    for place, (_, relative) in enumerate(places_of(stages, shards)):
        target = (keep, send)[place // (shards // 2)]
        source = aligned((where[1] ^ relative) * shard_rows, shard_rows)
        if by_tiles:
            for t in range(whole.shape[1] // LANES):
                target[place % (shards // 2), t * shard_rows : (t + 1) * shard_rows, :] = whole[
                    source, t * LANES : (t + 1) * LANES
                ]
        else:
            target[place % (shards // 2), :, :] = whole[source, :]


def score_grads(query, key, value, grad, offset, mask):
    scores = jnp.where(mask, mm_nt(query, key) + offset, NEG_FILL)
    expd = jnp.exp(scores - jnp.max(scores, axis=-1, keepdims=True))
    probs = expd * (1.0 / jnp.sum(expd, axis=-1, keepdims=True))
    d_probs = mm_nt(grad, value)
    weighted = jnp.sum(d_probs * probs, axis=-1, keepdims=True)
    d_scores = (probs * (d_probs - weighted)).astype(LOW)
    return (
        mm(d_scores, key),
        mm_tn(d_scores, query),
        mm_tn(probs.astype(LOW), grad),
        d_scores.astype(FULL),
    )


def fold_diagonals(flat):
    rows = flat.shape[0]
    folded = flat[:8, :]
    for base in range(8, rows, 8):
        folded = folded + pltpu.roll(flat[base : base + 8, :], 2 * rows - base, 1)
    return folded


def inside_grads_kernel(
    size,
    shards,
    stages,
    where,
    qkv,
    d_heads,
    heads_mine,
    heads_other,
    d_attn,
    row_starts,
    col_starts,
    bias,
    d_cols,
    d_bias,
    keep,
    send,
    d_out,
):
    rows, half = row_starts.shape[1], d_heads.shape[1]
    core = core_of(where)
    lane = lanes_at(core * half, half)
    value = mm_tn(heads_mine[...], d_attn[:, lane])
    d_out[aligned(core * half, half), :] = value.astype(LOW)
    value = mm_tn(heads_other[:rows, :], d_attn[rows:, lane])
    value = value + mm_tn(heads_other[rows:, :], d_attn[:rows, lane])
    d_out[aligned((1 - core) * half, half), :] = value.astype(LOW)
    split_shards(shards, stages, where, d_out, keep, send, by_tiles=True)
    masks, grads = [], []
    for stream in range(2):
        own_col = col_starts[:, 2 * stream : 2 * stream + 1]
        own_row = row_starts[3 * stream + 1 : 3 * stream + 2, :]
        settled = own_col != tail_of(row_starts, stream)
        masks.append((own_col == own_row) & settled)
        began = settled & (own_col >= ((where[0] ^ stream) * shards + where[1]) * rows)
        grad = d_heads[stream * rows : (stream + 1) * rows, :].astype(FULL)
        grads.append(jnp.where(began, grad, 0.0).astype(LOW))
    for pair in range(half // size // 2):
        outs = []
        for head in (2 * pair, 2 * pair + 1):
            near, _ = bias_tiles(bias[head : head + 1, :], rows)
            at = head * size
            flat = jnp.zeros((rows, rows), FULL)
            for stream in range(2):
                own = slice(2 * stream * rows, (2 * stream + 1) * rows)
                one = score_grads(
                    qkv[own, at : at + size],
                    qkv[own, half + at : half + at + size],
                    qkv[own, 2 * half + at : 2 * half + at + size],
                    grads[stream][:, at : at + size],
                    near,
                    masks[stream],
                )
                flat = flat + one[3]
                outs.append(one)
            flat = jnp.concatenate([flat, jnp.zeros((rows, rows), FULL)], axis=1)
            d_bias[8 * head : 8 * head + 8, :] = fold_diagonals(flat)
        for part in range(3):
            columns = slice(part * half + 2 * pair * size, part * half + (2 * pair + 2) * size)
            for stream in range(2):
                d_cols[stream * rows : (stream + 1) * rows, columns] = jnp.concatenate(
                    [outs[stream][part], outs[2 + stream][part]], axis=1
                ).astype(LOW)


def crossing_grads_kernel(
    shards,
    first_head,
    last_head,
    size,
    stages,
    where,
    qkv,
    normed,
    d_heads,
    d_after,
    d_inside,
    row_starts,
    col_starts,
    bias,
    d_cols,
    keep,
    send,
    d_bias,
    d_weights,
):
    rows, half = row_starts.shape[1], d_heads.shape[1]
    width = normed.shape[1]
    group = (last_head - first_head) * size
    span = slice(first_head * size, last_head * size)
    last_cols, masks, turns, mixes, grads = [], [], [], [], []
    for stream in range(2):
        tail = tail_of(row_starts, stream)
        own_col = col_starts[:, 2 * stream : 2 * stream + 1]
        after_col = col_starts[:, 2 * stream + 1 : 2 * stream + 2]
        own_row = row_starts[3 * stream + 1 : 3 * stream + 2, :]
        after_row = row_starts[3 * stream + 2 : 3 * stream + 3, :]
        is_last_col, is_last_row = own_col == tail, own_row == tail
        mix_col = jnp.where(is_last_col, own_col, after_col)
        mix_row = jnp.where(is_last_row, own_row, after_row)
        last_cols.append(is_last_col)
        masks.append((mix_col == tail) & (mix_row == tail))
        turns.append(is_last_col != is_last_row)
        base = 2 * stream * rows
        mix = []
        for part in range(3):
            columns = slice(part * half + first_head * size, part * half + last_head * size)
            mix.append(
                pick(
                    is_last_col,
                    qkv[base : base + rows, columns],
                    qkv[base + rows : base + 2 * rows, columns],
                )
            )
        mixes.append(mix)
        here = slice(stream * rows, (stream + 1) * rows)
        mixed = jnp.where(
            is_last_col, d_heads[here, span].astype(FULL), d_after[here, span].astype(FULL)
        )
        grads.append(jnp.where(mix_col == tail, mixed, 0.0).astype(LOW))
    for pair in range((last_head - first_head) // 2):
        outs = []
        for index in (2 * pair, 2 * pair + 1):
            head = first_head + index
            near, far = bias_tiles(bias[head : head + 1, :], rows)
            at = index * size
            kept, turned = jnp.zeros((rows, rows), FULL), jnp.zeros((rows, rows), FULL)
            for stream in range(2):
                mix = mixes[stream]
                two = score_grads(
                    mix[0][:, at : at + size],
                    mix[1][:, at : at + size],
                    mix[2][:, at : at + size],
                    grads[stream][:, at : at + size],
                    jnp.where(turns[stream], far, near),
                    masks[stream],
                )
                kept = kept + jnp.where(turns[stream], 0.0, two[3])
                turned = turned + jnp.where(turns[stream], two[3], 0.0)
                outs.append(two)
            d_bias[8 * index : 8 * index + 8, :] = fold_diagonals(
                jnp.concatenate([kept, turned], axis=1)
            )
        for part in range(3):
            columns = slice(part * group + 2 * pair * size, part * group + (2 * pair + 2) * size)
            for stream in range(2):
                d_cols[stream * rows : (stream + 1) * rows, columns] = jnp.concatenate(
                    [outs[stream][part], outs[2 + stream][part]], axis=1
                ).astype(LOW)
    total = [jnp.zeros((width, group), FULL) for _ in range(3)]
    for stream in range(2):
        base = 2 * stream * rows
        own, ahead = normed[base : base + rows, :], normed[base + rows : base + 2 * rows, :]
        normed_mix = pick(last_cols[stream], own, ahead)
        here = slice(stream * rows, (stream + 1) * rows)
        for part in range(3):
            inner = slice(part * half + first_head * size, part * half + last_head * size)
            total[part] = total[part] + mm_tn(own, d_inside[here, inner])
            total[part] = total[part] + mm_tn(
                normed_mix, d_cols[here, part * group : (part + 1) * group]
            )
    for part in range(3):
        d_weights[:, part * group : (part + 1) * group] = total[part].astype(LOW)
    split_shards(shards, stages, where, d_weights, keep, send)


def normed_grads_kernel(
    sizes, weights, d_inside, own_a, halo_a, pair_b, halo_b, row_starts, col_starts, *refs
):
    *crossing, keep, send, d_gain = refs
    rows, half = col_starts.shape[0], weights.shape[1] // 3
    inside = mm_nt(d_inside[...], weights[...])
    across = jnp.zeros(inside.shape, FULL)
    begin = 0
    for ref, group in zip(crossing, sizes, strict=True):
        for part in range(3):
            across = across + mm_nt(
                ref[:, part * group : (part + 1) * group],
                weights[:, part * half + begin : part * half + begin + group],
            )
        begin += group
    total = jnp.zeros((1, weights.shape[0]), FULL)
    streams = ((own_a, halo_a, keep), (pair_b, halo_b, send))
    for stream, (own, halo, target) in enumerate(streams):
        is_last = col_starts[:, 2 * stream : 2 * stream + 1] == tail_of(row_starts, stream)
        here = slice(stream * rows, (stream + 1) * rows)
        mine = jnp.where(is_last, across[here], inside[here])
        sent = jnp.where(is_last, 0.0, across[here])
        target[:rows, :] = mine.astype(target.dtype)
        target[rows:, :] = sent.astype(target.dtype)
        values, ahead = own[:rows, :].astype(FULL), halo[rows:, :].astype(FULL)
        share = mine * (values * inverse_rms(values)) + sent * (ahead * inverse_rms(ahead))
        total = total + jnp.sum(share, axis=0, keepdims=True)
    d_gain[...] = total


def tokens_kernel(own, gains, d_resid, d_own, d_before, out_keep, out_other, d_tokens, output):
    values = own[...].astype(FULL)
    grad = d_own[...] + d_before[...].astype(FULL)
    d_tokens[...] = d_resid[...] + norm_back(values, inverse_rms(values), gains[0:1, :], grad)
    output[...] = (out_keep[...] + out_other[...].astype(FULL)).astype(LOW)


def unpack_feed_kernel(tile_step, where, mine, other, d_gate, d_up, d_down, d_out):
    rows, half = d_out.shape[0], d_out.shape[1] // 2
    tiles, down_tiles = d_gate.shape[1] // (4 * LANES), d_down.shape[1] // LANES
    down_rows = d_down.shape[0] // 4
    begin = 0
    for relative in range(2):
        side = side_of(where) ^ relative
        for which, part in enumerate((mine, other)):
            core = core_of(where) ^ which
            at = begin
            target = aligned((2 * core + side) * down_rows, down_rows)
            for t in range(down_tiles):
                d_down[target, t * LANES : (t + 1) * LANES] = part[
                    at + t * down_rows : at + (t + 1) * down_rows, :
                ].astype(FULL)
            at += down_tiles * down_rows
            for matrix in (d_up, d_gate):
                for t in range(tiles):
                    lane = lanes_at(tile_step(core, side * tiles + t), LANES)
                    matrix[:, lane] = part[at + t * rows : at + (t + 1) * rows, :].astype(FULL)
                at += tiles * rows
        begin = at
    for which, part in enumerate((mine, other)):
        core = core_of(where) ^ which
        for t in range(half // LANES):
            first = begin + t * rows
            d_out[:, lanes_at(core * half + t * LANES, LANES)] = part[
                first : first + rows, :
            ].astype(FULL)


def unpack_attend_kernel(sizes, where, mine, other, d_query, d_key, d_value):
    half = d_query.shape[1] // 2
    for which, ref in enumerate((mine, other)):
        core = core_of(where) ^ which
        begin, column = 0, 0
        for group in sizes:
            for target in (d_query, d_key, d_value):
                target[:, lanes_at(core * half + begin, group)] = ref[
                    :, column : column + group
                ].astype(FULL)
                column += group
            begin += group


def shaped(shape, dtype):
    return jax.ShapeDtypeStruct(shape, dtype)


def per_device(
    tokens,
    cotangent,
    offsets,
    w_query,
    w_key,
    w_value,
    w_attn_out,
    w_gate,
    w_up,
    w_ff_out,
    gain_attn,
    gain_ff,
    rel_table,
):
    rows, width = tokens.shape
    shards = lax.axis_size("shard")
    shard, rep = lax.axis_index("shard"), lax.axis_index("rep")
    heads_count, table_rows = rel_table.shape[1], rel_table.shape[0]
    buckets = table_rows * shards
    shard_rows, inner = w_gate.shape
    half, size = width // 2, width // heads_count
    own_heads = heads_count // 2
    piece = w_ff_out.shape[0] // 2
    core = rep % 2
    where = jnp.stack([rep, shard]).astype(jnp.int32)

    starts_all = jnp.arange(offsets.shape[0], dtype=jnp.int32) - offsets
    start_pad = jnp.pad(starts_all, (rows, rows), constant_values=-1)
    first_a, first_b = (rep * shards + shard) * rows, ((rep ^ 1) * shards + shard) * rows
    window_a = lax.dynamic_slice_in_dim(start_pad, first_a, 3 * rows).reshape(3, rows)
    window_b = lax.dynamic_slice_in_dim(start_pad, first_b, 3 * rows).reshape(3, rows)
    row_starts = jnp.concatenate([window_a, window_b], axis=0)
    col_starts = jnp.stack([window_a[1], window_a[2], window_b[1], window_b[2]], axis=1)
    by_tiles = piece % LANES == 0

    def tile_step(which_core, tile):
        if by_tiles:
            per_shard = piece // LANES
            return ((tile // per_shard * 2 + which_core) * per_shard + tile % per_shard) * LANES
        return which_core * (inner // 2) + tile * LANES

    def by_core(matrix):
        if by_tiles:
            return matrix
        split = matrix.reshape(shard_rows, shards, 2, piece).transpose(0, 2, 1, 3)
        return split.reshape(shard_rows, inner)

    def from_core(matrix):
        if by_tiles:
            return matrix
        split = matrix.reshape(shard_rows, 2, shards, piece).transpose(0, 2, 1, 3)
        return split.reshape(shard_rows, inner)

    tiles = inner // (4 * LANES)
    down_block = width // LANES * (piece // 2)
    qkv_side = -(-3 * half // (2 * LANES)) * LANES
    steps = Sequence(jnp.zeros((8, LANES), FULL))
    qkv_own, ff_own, rest_own = steps.call(
        functools.partial(pack_kernel, tile_step),
        (where,),
        (
            w_query,
            w_key,
            w_value,
            w_attn_out,
            by_core(w_gate),
            by_core(w_up),
            w_ff_out,
            gain_attn.reshape(1, shard_rows),
            gain_ff.reshape(1, shard_rows),
            rel_table,
        ),
        (
            shaped((shard_rows + SMALL, qkv_side), LOW),
            shaped((2 * tiles * shard_rows, LANES), LOW),
            shaped((2 * piece + shard_rows, half), LOW),
        ),
        room=58,
    )
    onehot = np.zeros((shards, SMALL, 2 * rows), np.float32)
    onehot[:, 2 : 2 + table_rows] = bucket_onehot(2 * rows, buckets).T.reshape(
        shards, table_rows, 2 * rows
    )
    onehot = jnp.asarray(onehot.reshape(shards * SMALL, 2 * rows), LOW)


    up = [(i, i + 1) for i in range(shards - 1)]
    down = [(i + 1, i) for i in range(shards - 1)]
    by_x, by_core = (("rep", 1),), ("rep", 0)
    far, near = far_first(shards), near_first(shards)

    def joined(*parts, axis=0):
        return jnp.concatenate(parts, axis=axis)

    pair = joined(tokens, cotangent)
    received, pair_b = steps.send(qkv_own, ("shard", far[0])), steps.send(pair, by_core)
    steps.mark()
    qkv_near, pair_b = joined(qkv_own, steps.take(received)), steps.take(pair_b)
    shifted = steps.take(tokens)
    ff_received = steps.send(steps.take(ff_own), ("shard", far[0]))
    rest_received = steps.send(steps.take(rest_own), ("shard", far[0]))
    before, ahead = lax.ppermute(shifted, "shard", up), lax.ppermute(shifted, "shard", down)
    for bit in far[1:-1]:
        received = steps.send(qkv_near, ("shard", bit))
        steps.mark()
        qkv_near = joined(qkv_near, steps.take(received))
    qkv_far, qkv_side = steps.send(qkv_near, ("shard", far[-1])), steps.send(qkv_near, by_x[0])
    ff_near = joined(ff_own, steps.take(ff_received))
    ff_received = steps.send(ff_near, ("shard", far[1]))
    steps.mark()
    halo = joined(steps.take(before), steps.take(ahead))
    halo_b = steps.send(halo, by_core)
    rest_near = joined(rest_own, steps.take(rest_received))
    rest_received = steps.send(rest_near, ("shard", far[1]))
    steps.mark()
    qkv_far, qkv_side = steps.take(qkv_far), steps.take(qkv_side)
    qkv_other = steps.send(qkv_far, by_x[0])
    ff_near = joined(ff_near, steps.take(ff_received))
    halo_b = steps.take(halo_b)
    for bit in far[2:-1]:
        ff_received = steps.send(ff_near, ("shard", bit))
        rest_near = joined(rest_near, steps.take(rest_received))
        rest_received = steps.send(rest_near, ("shard", bit))
        steps.mark()
        ff_near = joined(ff_near, steps.take(ff_received))
    ff_far, ff_side = steps.send(ff_near, ("shard", far[-1])), steps.send(ff_near, by_x[0])
    steps.mark()
    rest_near = joined(rest_near, steps.take(rest_received))
    rest_far = steps.send(rest_near, ("shard", far[-1]))
    qkv_other = steps.take(qkv_other)
    heads, normed, qkv, w_qkv, gains, bias = steps.call(
        functools.partial(attend_kernel, shards, size),
        (where,),
        (
            tokens,
            halo,
            pair_b,
            halo_b,
            qkv_near,
            qkv_far,
            qkv_side,
            qkv_other,
            row_starts,
            col_starts,
            onehot,
        ),
        (
            shaped((2 * rows, half), LOW),
            shaped((4 * rows, width), LOW),
            shaped((4 * rows, 3 * half), LOW),
            shaped((width, 3 * half), LOW),
            shaped((SMALL, width), FULL),
            shaped((8, 2 * rows), FULL),
        ),
        [pltpu.VMEM((rows, 2 * half), LOW), pltpu.VMEM((shards * SMALL, LANES), FULL)],
        micros=12,
    )
    heads_other, rest_near_b = steps.send(heads, by_core), steps.send(rest_near, by_core)
    ff_far, ff_side = steps.take(ff_far), steps.take(ff_side)
    ff_other = steps.send(steps.take(ff_far), by_x[0])
    steps.mark()
    heads_other, rest_near_b = steps.take(heads_other), steps.take(rest_near_b)
    rest_far = steps.take(rest_far)
    rest_far_b = steps.send(rest_far, by_core)
    steps.mark()
    ff_other, rest_far_b = steps.take(ff_other), steps.take(rest_far_b)
    wide = shaped((2 * rows, inner // 2), LOW)
    (
        out_keep,
        out_send,
        d_normed_keep,
        d_normed_send,
        resid,
        normed_ff,
        hidden,
        d_gate,
        d_linear,
        w_out,
    ) = steps.call(
        functools.partial(feed_kernel, shards),
        (where,),
        (
            heads,
            heads_other,
            tokens,
            cotangent,
            pair_b,
            gains,
            rest_near,
            rest_far,
            rest_near_b,
            rest_far_b,
            ff_near,
            ff_far,
            ff_side,
            ff_other,
        ),
        (
            shaped((rows, width), FULL),
            shaped((rows, width), LOW),
            shaped((2 * rows, width), FULL),
            shaped((2 * rows, width), LOW),
            shaped((2 * rows, width), FULL),
            shaped((2 * rows, width), LOW),
            wide,
            wide,
            wide,
            shaped((width, width), LOW),
        ),
        [
            pltpu.VMEM((width, inner // 2), LOW),
            pltpu.VMEM((width, inner // 2), LOW),
            pltpu.VMEM((inner // 2, width), LOW),
        ],
        micros=400,
    )
    d_normed_other, out_other = swap(d_normed_send, *by_core), swap(out_send, *by_core)
    slices = shaped((shards, tiles * shard_rows, LANES), LOW)
    down_slices = shaped((shards, down_block, LANES), LOW)
    by_near = tuple(("shard", bit) for bit in near)
    down_stages = by_x + by_near
    gate_stages = by_near[:1] + by_x + by_near[1:]
    up_stages = by_x + by_near[1:2] + by_near[:1] + by_near[2:]
    down_keep, down_send = steps.call(
        functools.partial(down_grads_kernel, shards, down_stages),
        (where,),
        (hidden, cotangent, pair_b),
        (down_slices, down_slices),
        [pltpu.VMEM((inner // 2, width), LOW)],
        micros=4,
    )
    down_received = exchange(down_send, down_stages[0])
    d_normed_other, out_other = steps.take(d_normed_other), steps.take(out_other)
    d_resid, d_attn, d_heads, d_gain_two = steps.call(
        resid_grads_kernel,
        (where,),
        (d_normed_keep, d_normed_other, resid, cotangent, pair_b, gains, w_out),
        (
            shaped((rows, width), FULL),
            shaped((2 * rows, width), LOW),
            shaped((2 * rows, half), LOW),
            shaped((1, width), FULL),
        ),
        micros=5,
    )
    d_heads_after = lax.ppermute(d_heads, "shard", down)
    gate_keep, gate_send = steps.call(
        functools.partial(wide_grads_kernel, shards, gate_stages),
        (where,),
        (normed_ff, d_gate),
        (slices, slices),
        [pltpu.VMEM((2, width, inner // 4), LOW)],
        micros=4,
    )
    gate_received = exchange(gate_send, gate_stages[0])
    up_keep, up_send = steps.call(
        functools.partial(wide_grads_kernel, shards, up_stages),
        (where,),
        (normed_ff, d_linear),
        (slices, slices),
        [pltpu.VMEM((2, width, inner // 4), LOW)],
        micros=4,
    )
    up_received = exchange(up_send, up_stages[0])
    out_slices = shaped((shards // 2, shard_rows * half // LANES, LANES), LOW)
    d_inside, d_bias, o_keep, o_send = steps.call(
        functools.partial(inside_grads_kernel, size, shards, by_near),
        (where,),
        (qkv, d_heads, heads, heads_other, d_attn, row_starts, col_starts, bias),
        (
            shaped((2 * rows, 3 * half), LOW),
            shaped((8 * own_heads, 2 * rows), FULL),
            out_slices,
            out_slices,
        ),
        [pltpu.VMEM((width, half), LOW)],
        micros=11,
    )

    d_down, down_received = steps.send_half(steps.add(down_keep, down_received), down_stages[1])
    o_received = steps.send(o_send, by_near[0])
    d_heads_after = steps.take(d_heads_after)
    sizes = [count * size for count in GROUPS]

    def crossing_grads(first, count):
        attn_slices = shaped((shards // 2, shard_rows, 3 * count * size), LOW)
        return steps.call(
            functools.partial(
                crossing_grads_kernel, shards, first, first + count, size, by_near
            ),
            (where,),
            (qkv, normed, d_heads, d_heads_after, d_inside, row_starts, col_starts, bias),
            (
                shaped((2 * rows, 3 * count * size), LOW),
                attn_slices,
                attn_slices,
                shaped((8 * count, 2 * rows), FULL),
            ),
            [pltpu.VMEM((width, 3 * count * size), LOW)],
            micros=12 if not first else 400,
            room=58,
        )

    cols_one, one_keep, one_send, d_bias_one = crossing_grads(0, GROUPS[0])
    one_received = steps.send(one_send, by_near[0])
    d_gate, gate_received = steps.send_half(steps.add(gate_keep, gate_received), gate_stages[1])
    d_up, up_received = steps.send_half(steps.add(up_keep, up_received), up_stages[1])
    d_down, down_received = steps.send_half(steps.add(d_down, down_received), down_stages[2])
    cols_two, two_keep, two_send, d_bias_two = crossing_grads(GROUPS[0], GROUPS[1])
    d_out = steps.add(o_keep, o_received)
    two_received = steps.send(two_send, by_near[0])
    d_gate = joined(steps.add(d_gate, gate_received), d_out, axis=1)
    d_gate, gate_received = steps.send_half(d_gate, by_near[1])
    d_down, down_received = steps.send_half(steps.add(d_down, down_received), down_stages[3])
    d_up, up_received = steps.send_half(steps.add(d_up, up_received), up_stages[2])
    keep, send, d_gain_one = steps.call(
        functools.partial(normed_grads_kernel, tuple(sizes)),
        (),
        (
            w_qkv,
            d_inside,
            tokens,
            halo,
            pair_b,
            halo_b,
            row_starts,
            col_starts,
            cols_one,
            cols_two,
        ),
        (
            shaped((2 * rows, width), FULL),
            shaped((2 * rows, width), LOW),
            shaped((1, width), FULL),
        ),
        micros=400,
        room=58,
    )
    folds = np.stack([np.roll(bucket_onehot(2 * rows, buckets), row, axis=0) for row in range(8)])
    d_bias = d_bias + jnp.concatenate([d_bias_one, d_bias_two], axis=0)
    d_bias = d_bias.reshape(own_heads, 16 * rows)
    d_table = lax.dot_general(
        d_bias,
        jnp.asarray(folds.reshape(16 * rows, buckets)),
        (((1,), (0,)), ((), ())),
        precision=lax.Precision.HIGHEST,
    )
    d_table = lax.dynamic_update_slice(
        jnp.zeros((heads_count, buckets), FULL), d_table, (core * own_heads, 0)
    ).T
    smalls = jnp.concatenate([d_gain_one.reshape(-1), d_gain_two.reshape(-1), d_table.reshape(-1)])
    rest = -smalls.shape[0] % (8 * LANES)
    smalls = jnp.pad(smalls, (0, rest)).reshape(-1, LANES)
    small_stages = list(by_near)
    small_stages += [("rep", bit) for bit in reversed(range(bits_of(lax.axis_size("rep"))))]
    attn = joined(
        steps.add(one_keep, one_received), steps.add(two_keep, two_received), axis=2
    )
    attn, attn_received = steps.send_half(attn, by_near[1])
    d_own_received = exchange(send, by_core)
    d_gate = joined(steps.add(d_up, up_received), steps.add(d_gate, gate_received), axis=1)
    d_gate, gate_received = steps.send_half(d_gate, by_near[2])
    small_received = steps.send(smalls, small_stages[0])
    d_down = steps.add(d_down, down_received)
    steps.mark()
    d_own = keep + steps.take(d_own_received).astype(FULL)
    d_before = lax.ppermute(d_own[rows:].astype(LOW), "shard", up)
    smalls = smalls + steps.take(small_received)
    small_received = steps.send(smalls, small_stages[1])
    steps.mark(d_own)
    attn, attn_received = steps.send_half(steps.add(attn, attn_received), by_near[2])
    d_gate = steps.add(d_gate, gate_received)
    for stage in by_near[3:]:
        attn = steps.add(attn, attn_received)
        attn, attn_received = steps.send_half(attn, stage)
        d_gate, gate_received = steps.send_half(d_gate, stage)
        d_gate = steps.add(d_gate, gate_received)
        d_down, down_received = steps.send_half(d_down, stage)
        d_down = steps.add(d_down, down_received)
    wide = tiles * shard_rows
    d_feed, d_out = joined(d_down[0], d_gate[0, : 2 * wide]), d_gate[0, 2 * wide :]
    for bit in range(2, bits_of(lax.axis_size("rep"))):
        d_feed = steps.add(d_feed, exchange(d_feed, ("rep", bit)))
        d_out = steps.add(d_out, exchange(d_out, ("rep", bit)))
    feed_received = steps.send(joined(d_feed, d_out), by_x[0])
    smalls = smalls + steps.take(small_received)
    small_received = steps.send(smalls, small_stages[2])
    steps.mark()
    attn = steps.add(attn, attn_received)[0]
    for bit in range(2, bits_of(lax.axis_size("rep"))):
        attn = steps.add(attn, exchange(attn, ("rep", bit)))
    attn_received = steps.send(attn, by_x[0])
    smalls = smalls + steps.take(small_received)
    small_received = steps.send(smalls, small_stages[3])
    feed_received = steps.take(feed_received)
    feed = d_feed.shape[0]
    d_feed = joined(d_feed, feed_received[:feed], add_low(d_out, feed_received[feed:]))
    feed_other = steps.send(d_feed, by_core)
    d_tokens, output = steps.call(
        tokens_kernel,
        (),
        (tokens, gains, d_resid, d_own[:rows], steps.take(d_before), out_keep, out_other),
        (shaped((rows, width), FULL), shaped((rows, width), LOW)),
        micros=400,
    )
    attn = steps.add(attn, attn_received)
    attn_other = steps.send(attn, by_core)
    feed_other = steps.take(feed_other)
    for stage in small_stages[4:]:
        smalls = smalls + steps.take(small_received)
        small_received = steps.send(smalls, stage)
    d_w_gate, d_w_up, d_w_ff_out, d_w_attn_out = steps.call(
        functools.partial(unpack_feed_kernel, tile_step),
        (where,),
        (d_feed, feed_other),
        (
            shaped(w_gate.shape, FULL),
            shaped(w_up.shape, FULL),
            shaped(w_ff_out.shape, FULL),
            shaped(w_attn_out.shape, FULL),
        ),
        micros=400,
    )
    attn_other = steps.take(attn_other)
    smalls = (smalls + steps.take(small_received)).reshape(-1)
    d_w_query, d_w_key, d_w_value = steps.call(
        functools.partial(unpack_attend_kernel, tuple(sizes)),
        (where,),
        (attn, attn_other),
        (shaped(w_query.shape, FULL),) * 3,
        micros=400,
    )

    def own_part(begin, length):
        return lax.dynamic_slice_in_dim(smalls, begin + shard * length, length)

    return (
        output,
        d_tokens,
        d_w_query,
        d_w_key,
        d_w_value,
        d_w_attn_out,
        from_core(d_w_gate),
        from_core(d_w_up),
        d_w_ff_out,
        own_part(0, shard_rows),
        own_part(width, shard_rows),
        own_part(2 * width, table_rows * heads_count).reshape(table_rows, heads_count),
    )


def solution(mesh):
    tokens_spec, rows_spec, line_spec = P(("rep", "shard"), None), P("shard", None), P("shard")
    return jax.shard_map(
        per_device,
        mesh=mesh,
        in_specs=(tokens_spec, tokens_spec, P()) + (rows_spec,) * 7 + (line_spec,) * 2 + (rows_spec,),
        out_specs=(tokens_spec,) * 2 + (rows_spec,) * 7 + (line_spec,) * 2 + (rows_spec,),
        check_vma=False,
    )
```
